512 devices in a mesh: boxes: 128 (over y, z, core), probe: 4 (over x).
Axes of the slice: x: 4, y: 8, z: 8, core: 2. Of those that a mesh axis runs over, the one named last changes fastest.
Arguments:
- probes: float32 [32, 1048576], P('probe', 'boxes'), may hold values from -0.3 to 0.3
- points: float32 [3, 1048576], P(None, 'boxes'), may hold values from -1 to 1, as said below
- near_list: int32 [4096, 6], P('boxes'), may hold values from -1 to 4095, as said below
- leaf_proxy: float32 [3, 262144], P(None, 'boxes'), may hold values from -1 to 1, as said below
- inner_proxy: float32 [3, 245760], P(None, 'boxes'), may hold values from -1 to 1, as said below
- top_proxy: float32 [3, 16128], replicated, may hold values from -1 to 1, as said below
- far_list: int32 [4096, 3], P('boxes'), may hold values from -1 to 4095, as said below
Outputs:
- kernel_product: float32 [32, 1048576], P('probe', 'boxes')
The draws below stay inside these ranges and needn't reach their ends.
Inputs may be any that keep to these rules, and one draw needn't show every extreme that they name: `points`: points on the unit sphere, box by box along a curve over it. `leaf_proxy`: proxy points on the unit sphere. `inner_proxy`: proxy points on the unit sphere. `top_proxy`: proxy points on the unit sphere. `near_list`: row b holds b - 1, b, b + 1 (modulo 4096) and those of the three candidates of row b of far_list that are -1 there, in some order, live entries first, then -1; some row is full. `far_list`: in row b, slot 0 holds b - 2, slot 1 holds b + 2, slot 2 holds b + 3 for even b and b - 3 for odd b (all modulo 4096), or -1.
All inputs are finite; a program needn't handle non-finite values.
Results may differ from the reference program's by a relative error of at most 0.00013.
Values sent between devices are 32-bit elements; how exact they have to be, the bound alone decides.
A program may use at most 64 MiB of HBM per device.

```python
import math
import jax
import jax.numpy as jnp
from jax import lax

BOXES_DEV = 32
P_SIZE = 256
R = 64
Q = 32
NEAR = 6
BOX_GROUPS = 128
BOXES = 4096
POINTS = 1048576
INNER_DEV = 30
TOP_NODES = 252


def sphere_spots(key, position):
    fraction = position / BOXES
    height = 1.0 - 2.0 * fraction
    radius = jnp.sqrt(1.0 - height * height)
    longitude = 2.0 * math.pi * 0.8 * math.sqrt(BOXES) * fraction
    spread = 2.0 / math.sqrt(BOXES)
    centre = jnp.stack([radius * jnp.cos(longitude), radius * jnp.sin(longitude), height], axis=0)
    jitter = jax.random.normal(key, centre.shape, jnp.float32)
    shifted = centre + spread * jitter
    return shifted / jnp.sqrt(jnp.sum(shifted * shifted, axis=0, keepdims=True))


def draw_points(key, part):
    first_key, second_key = jax.random.split(key)
    column = jnp.arange(POINTS)
    position = (column // P_SIZE).astype(jnp.float32) + jax.random.uniform(first_key, (POINTS,), jnp.float32)
    return sphere_spots(second_key, position)


def draw_leaf_proxy(key, part):
    first_key, second_key = jax.random.split(key)
    column = jnp.arange(BOXES * R)
    position = (column // R).astype(jnp.float32) + jax.random.uniform(first_key, (BOXES * R,), jnp.float32)
    return sphere_spots(second_key, position)


def draw_inner_proxy(key, part):
    first_key, second_key = jax.random.split(key)
    columns_all = BOX_GROUPS * INNER_DEV * R
    column = jnp.arange(columns_all)
    owner_group = column // (INNER_DEV * R)
    node_index = column // R % INNER_DEV
    node_span = jnp.ones_like(node_index)
    node_start = jnp.zeros_like(node_index)
    local_depth = BOXES_DEV.bit_length() - 1
    for height in range(1, local_depth):
        offset = BOXES_DEV - (BOXES_DEV >> height - 1)
        number = BOXES_DEV >> height
        inside = (node_index >= offset) & (node_index < offset + number)
        node_span = jnp.where(inside, 2 ** height, node_span)
        node_start = jnp.where(inside, owner_group * BOXES_DEV + (node_index - offset) * 2 ** height, node_start)
    position = node_start.astype(jnp.float32) + node_span.astype(jnp.float32) * jax.random.uniform(first_key, (columns_all,), jnp.float32)
    return sphere_spots(second_key, position)


def draw_top_proxy(key, part):
    first_key, second_key = jax.random.split(key)
    columns_all = TOP_NODES * R
    column = jnp.arange(columns_all)
    node_index = column // R
    node_span = jnp.ones_like(node_index)
    node_start = jnp.zeros_like(node_index)
    tree_depth = BOX_GROUPS.bit_length() - 1
    for height in range(tree_depth - 1):
        number = BOX_GROUPS >> height
        offset = 2 * BOX_GROUPS - 2 * number
        inside = (node_index >= offset) & (node_index < offset + number)
        node_span = jnp.where(inside, BOXES_DEV * 2 ** height, node_span)
        node_start = jnp.where(inside, (node_index - offset) * BOXES_DEV * 2 ** height, node_start)
    position = node_start.astype(jnp.float32) + node_span.astype(jnp.float32) * jax.random.uniform(first_key, (columns_all,), jnp.float32)
    return sphere_spots(second_key, position)


def box_lists(key):
    first_key, second_key, third_key = jax.random.split(jax.random.fold_in(key, 7), 3)
    box = jnp.arange(BOXES, dtype=jnp.int32)
    third = jnp.where(box % 2 == 0, box + 3, box - 3)
    candidates = (jnp.stack([box - 2, box + 2, third], axis=1) + BOXES) % BOXES
    heaviness = jax.random.randint(first_key, (BOX_GROUPS,), 0, 4)
    direct = jax.random.randint(second_key, (BOXES, 3), 0, 4) < jnp.repeat(heaviness, BOXES_DEV)[:, None]
    direct = direct.at[0].set(True).at[1].set(False)
    beside = (jnp.stack([box - 1, box, box + 1], axis=1) + BOXES) % BOXES
    near_ids = jnp.concatenate([beside, candidates], axis=1)
    live = jnp.concatenate([jnp.ones((BOXES, 3), dtype=bool), direct], axis=1)
    ranks = jax.random.permutation(third_key, jnp.tile(jnp.arange(NEAR, dtype=jnp.int32), (BOXES, 1)), axis=1, independent=True)
    score = (1 - live.astype(jnp.int32)) * NEAR + ranks
    order = jnp.argsort(score, axis=1)
    near_rows = jnp.take_along_axis(jnp.where(live, near_ids, -1), order, axis=1)
    far_rows = jnp.where(direct, -1, candidates)
    return (near_rows.astype(jnp.int32), far_rows.astype(jnp.int32))


def draw_near_list(key, part):
    return box_lists(key)[0]


def draw_far_list(key, part):
    return box_lists(key)[1]


def steps_of(stream_key, dims, pieces, least, high):
    loudness, own = 1.0, jax.random.fold_in(stream_key, 6)
    for axis_at, parts in pieces:
        steps = jnp.exp(jax.random.uniform(jax.random.fold_in(own, axis_at), (parts,), jnp.float32, least / len(pieces), high / len(pieces)))
        loudness = loudness * jnp.repeat(steps, dims[axis_at] // parts).reshape([-1 if axis == axis_at else 1 for axis in range(len(dims))])
    return loudness


def bell_draw(key, dims, scale, most, cuts=(), held_as=jnp.bfloat16):
    values = jax.random.normal(key, dims, jnp.float32) * scale
    if len(cuts) > 0:
        values = steps_of(key, dims, cuts, -0.22, 0.18) * values
    return jnp.clip(values, min=-most, max=most).astype(held_as)


def setup_inputs(seed: int = 0) -> dict:
    streams_of = jax.random.split(jax.random.key(seed), 8)
    probes = bell_draw(streams_of[0], (Q, POINTS), 0.05, 0.3, ((0, 4), (1, 128)), jnp.float32)
    points = draw_points(jax.random.fold_in(streams_of[7], 71), 0)
    near_list = draw_near_list(jax.random.fold_in(streams_of[7], 71), 0)
    leaf_proxy = draw_leaf_proxy(jax.random.fold_in(streams_of[7], 71), 0)
    inner_proxy = draw_inner_proxy(jax.random.fold_in(streams_of[7], 71), 0)
    top_proxy = draw_top_proxy(jax.random.fold_in(streams_of[7], 71), 0)
    far_list = draw_far_list(jax.random.fold_in(streams_of[7], 71), 0)
    return {"probes": probes, "points": points, "near_list": near_list, "leaf_proxy": leaf_proxy, "inner_proxy": inner_proxy, "top_proxy": top_proxy, "far_list": far_list}


SHARPNESS = 0.05
NUGGET = 1.0
PRECISE = lax.Precision.HIGHEST


def kernel_matrix(left_points, right_points, kernel_scale):
    distance_sq = (left_points[0][..., :, None] - right_points[0][..., None, :]) ** 2
    distance_sq = distance_sq + (left_points[1][..., :, None] - right_points[1][..., None, :]) ** 2
    distance_sq = distance_sq + (left_points[2][..., :, None] - right_points[2][..., None, :]) ** 2
    return 1.0 / (1.0 + kernel_scale * distance_sq)


def interpolation(left_points, right_points, kernel_scale):
    values = kernel_matrix(left_points, right_points, kernel_scale)
    return values / jnp.sum(values, axis=-1, keepdims=True)


def level_sources(number):
    node = jnp.arange(number, dtype=jnp.int32)
    third = jnp.where(node % 2 == 0, node + 3, node - 3)
    wide = 1.0 if number > 4 else 0.0
    return [(node - 2) % number, (node + 2) % number, third % number], [wide, 1.0, wide]


def reference(probes, points, near_list, leaf_proxy, inner_proxy, top_proxy, far_list):
    kernel_scale = SHARPNESS * BOXES
    groups = BOX_GROUPS
    probe_tiles = probes.reshape(Q, BOXES, P_SIZE)
    box_points = points.reshape(3, BOXES, P_SIZE)
    live_slot = near_list >= 0
    safe_index = jnp.where(live_slot, near_list, 0).astype(jnp.int32)
    slot_weight = live_slot.astype(jnp.float32)

    def near_group(near_inputs):
        slot_index, slot_mask, targets = near_inputs
        near_values = probe_tiles[:, slot_index, :] * slot_mask[None, :, :, None]
        source_points = box_points[:, slot_index, :]
        kernel_block = kernel_matrix(source_points, targets[:, :, None, :], kernel_scale)
        return jnp.einsum('qbns,bnst->qbt', near_values, kernel_block, precision=PRECISE)

    near_field = lax.map(near_group, (safe_index.reshape(groups, BOXES_DEV, NEAR),
                                      slot_weight.reshape(groups, BOXES_DEV, NEAR),
                                      jnp.moveaxis(box_points.reshape(3, groups, BOXES_DEV, P_SIZE), 1, 0)))
    near_field = jnp.moveaxis(near_field, 0, 1).reshape(Q, POINTS)

    local_depth = BOXES_DEV.bit_length() - 1
    tree_depth = groups.bit_length() - 1
    inner_points = inner_proxy.reshape(3, groups, INNER_DEV, R)
    top_points = top_proxy.reshape(3, TOP_NODES, R)
    proxies = [leaf_proxy.reshape(3, BOXES, R)]
    for height in range(1, local_depth):
        offset = BOXES_DEV - (BOXES_DEV >> (height - 1))
        number = BOXES_DEV >> height
        proxies.append(inner_points[:, :, offset:offset + number, :].reshape(3, groups * number, R))
    for height in range(tree_depth - 1):
        offset = 2 * groups - 2 * (groups >> height)
        proxies.append(top_points[:, offset:offset + (groups >> height), :])
    levels_all = len(proxies)
    leaf_basis = interpolation(box_points, proxies[0], kernel_scale)
    moments = [jnp.einsum('qbp,bpr->qbr', probe_tiles, leaf_basis, precision=PRECISE)]
    transfer_maps = []
    for height in range(levels_all - 1):
        parent_points = jnp.repeat(proxies[height + 1], 2, axis=1)
        interp_map = interpolation(proxies[height], parent_points, kernel_scale)
        transfer_maps.append(interp_map)
        lifted = jnp.einsum('qnr,nrs->qns', moments[-1], interp_map, precision=PRECISE)
        moments.append(lifted.reshape(Q, -1, 2, R).sum(axis=2))
    couplings = []
    for height in range(levels_all):
        number = proxies[height].shape[1]
        if height == 0:
            live_far = far_list >= 0
            source_ids = [jnp.where(live_far[:, slot], far_list[:, slot], 0).astype(jnp.int32) for slot in range(3)]
            source_masks = [live_far[:, slot].astype(jnp.float32)[None, :, None] for slot in range(3)]
        else:
            source_ids, source_masks = level_sources(number)
        coupling = jnp.zeros((Q, number, R), jnp.float32)
        for slot in range(3):
            kernel_block = kernel_matrix(proxies[height][:, source_ids[slot], :], proxies[height], kernel_scale)
            source_moment = moments[height][:, source_ids[slot], :] * source_masks[slot]
            coupling = coupling + jnp.einsum('qnr,nrs->qns', source_moment, kernel_block, precision=PRECISE)
        couplings.append(coupling)
    descent = couplings[-1]
    for height in range(levels_all - 2, -1, -1):
        descent = jnp.einsum('qns,nrs->qnr', jnp.repeat(descent, 2, axis=1), transfer_maps[height], precision=PRECISE)
        descent = descent + couplings[height]
    far_field = jnp.einsum('qbr,bpr->qbp', descent, leaf_basis, precision=PRECISE)
    return near_field + far_field.reshape(Q, POINTS) + NUGGET * probes
```

```python
import jax
import jax.numpy as jnp
from jax import lax
from jax.sharding import PartitionSpec as P

BOXES_DEV = 32
P_SIZE = 256
R = 64
W = 3
INNER_DEV = 30


SHARPNESS = 0.05
NUGGET = 1.0
PRECISE = lax.Precision.HIGHEST


def with_halo(array, sides, width):
    for axis, dim in sides:
        size, length = (lax.axis_size(axis), array.shape[dim])
        up = [(i, (i + 1) % size) for i in range(size)]
        down = [(j, i) for i, j in up]
        last = lax.slice_in_dim(array, length - width, length, axis=dim)
        initial = lax.slice_in_dim(array, 0, width, axis=dim)
        before = lax.ppermute(last, axis, up)
        after = lax.ppermute(initial, axis, down)
        array = jnp.concatenate([before, array, after], axis=dim)
    return array


def kernel_matrix(left_points, right_points, kernel_scale):
    distance_sq = (left_points[0][..., :, None] - right_points[0][..., None, :]) ** 2
    distance_sq = distance_sq + (left_points[1][..., :, None] - right_points[1][..., None, :]) ** 2
    distance_sq = distance_sq + (left_points[2][..., :, None] - right_points[2][..., None, :]) ** 2
    return 1.0 / (1.0 + kernel_scale * distance_sq)


def interpolation(left_points, right_points, kernel_scale):
    values = kernel_matrix(left_points, right_points, kernel_scale)
    return values / jnp.sum(values, axis=-1, keepdims=True)


def body(probes, points, near_list, leaf_proxy, inner_proxy, top_proxy, far_list):
    groups = lax.axis_size("boxes")
    device = lax.axis_index("boxes")
    boxes_all = BOXES_DEV * groups
    kernel_scale = SHARPNESS * boxes_all
    rows_here = probes.shape[0]
    local_depth = BOXES_DEV.bit_length() - 1
    tree_depth = groups.bit_length() - 1
    live_slot = near_list >= 0
    slot_weight = live_slot.astype(jnp.float32)
    where_in = jnp.where(live_slot, (near_list - device * BOXES_DEV + W + boxes_all) % boxes_all, 0)
    box_points = points.reshape(3, BOXES_DEV, P_SIZE)
    stacked = jnp.concatenate([probes, points], axis=0)
    extended = with_halo(stacked, (("boxes", 1),), W * P_SIZE)
    extended = extended.reshape(rows_here + 3, BOXES_DEV + 2 * W, P_SIZE)

    def near_box(near_inputs):
        slot_index, slot_mask, targets = near_inputs
        near_tiles = jnp.take(extended, slot_index, axis=1)
        near_values = near_tiles[:rows_here] * slot_mask[None, :, None]
        kernel_block = kernel_matrix(near_tiles[rows_here:], targets[:, None, :], kernel_scale)
        return jnp.einsum("qns,nst->qt", near_values, kernel_block, precision=PRECISE)

    near_field = lax.map(near_box, (where_in, slot_weight, jnp.moveaxis(box_points, 1, 0)))
    near_field = jnp.moveaxis(near_field, 0, 1).reshape(rows_here, BOXES_DEV * P_SIZE)
    probe_tiles = probes.reshape(rows_here, BOXES_DEV, P_SIZE)
    leaf_points = leaf_proxy.reshape(3, BOXES_DEV, R)
    leaf_basis = interpolation(box_points, leaf_points, kernel_scale)
    inner_points = inner_proxy.reshape(3, INNER_DEV, R)
    top_points = top_proxy.reshape(3, top_proxy.shape[1] // R, R)

    def node_proxy(height, node_index):
        offset = 2 * groups - 2 * (groups >> height)
        return lax.dynamic_slice_in_dim(top_points, offset + node_index, 1, 1)

    proxies = [leaf_points]
    for height in range(1, local_depth):
        offset = BOXES_DEV - (BOXES_DEV >> height - 1)
        number = BOXES_DEV >> height
        proxies.append(inner_points[:, offset : offset + number, :])
    proxies.append(node_proxy(0, device))
    level_moments = [jnp.einsum("qbp,bpr->qbr", probe_tiles, leaf_basis, precision=PRECISE)]
    transfer_maps = []
    for height in range(local_depth):
        interp_map = interpolation(
            proxies[height], jnp.repeat(proxies[height + 1], 2, axis=1), kernel_scale
        )
        transfer_maps.append(interp_map)
        lifted = jnp.einsum("qnr,nrs->qns", level_moments[-1], interp_map, precision=PRECISE)
        level_moments.append(lifted.reshape(rows_here, -1, 2, R).sum(axis=2))
    pyramid = jnp.concatenate(
        [
            jnp.concatenate(level_moments[:local_depth], axis=1),
            jnp.concatenate([leaf_points, inner_points], axis=1),
        ],
        axis=0,
    )
    pyramid_nodes = pyramid.shape[1]
    spread = with_halo(pyramid, (("boxes", 1),), pyramid_nodes)
    local_couplings = []
    for height in range(local_depth):
        count = BOXES_DEV >> height
        start = 0 if height == 0 else 2 * BOXES_DEV - (BOXES_DEV >> height - 1)
        view = jnp.concatenate(
            [
                spread[:, block * pyramid_nodes + start : block * pyramid_nodes + start + count, :]
                for block in range(3)
            ],
            axis=1,
        )
        if height == 0:
            live_far = far_list >= 0
            slot_ids = [
                jnp.where(
                    live_far[:, slot],
                    (far_list[:, slot] - device * BOXES_DEV + BOXES_DEV + boxes_all) % boxes_all,
                    0,
                )
                for slot in range(3)
            ]
            slot_masks = [live_far[:, slot].astype(jnp.float32)[None, :, None] for slot in range(3)]
        else:
            node = jnp.arange(count, dtype=jnp.int32)
            third = jnp.where(node % 2 == 0, node + 3, node - 3)
            slot_ids = [node - 2 + count, node + 2 + count, third + count]
            slot_masks = [None, None, None]
        coupling = jnp.zeros((rows_here, count, R), jnp.float32)
        for slot in range(3):
            picked = jnp.take(view, slot_ids[slot], axis=1)
            kernel_block = kernel_matrix(picked[rows_here:], proxies[height], kernel_scale)
            source_moment = picked[:rows_here]
            if slot_masks[slot] is not None:
                source_moment = source_moment * slot_masks[slot]
            coupling = coupling + jnp.einsum(
                "qnr,nrs->qns", source_moment, kernel_block, precision=PRECISE
            )
        local_couplings.append(coupling)

    top_levels = tree_depth - 1
    level_points = []
    for height in range(top_levels):
        offset = 2 * groups - 2 * (groups >> height)
        level_points.append(top_points[:, offset : offset + (groups >> height), :])
    level_moments_top = [
        lax.all_gather(level_moments[local_depth], "boxes", axis=1, tiled=True)
    ]
    edge_maps = []
    for height in range(top_levels - 1):
        interp_map = interpolation(
            level_points[height], jnp.repeat(level_points[height + 1], 2, axis=1), kernel_scale
        )
        edge_maps.append(interp_map)
        lifted = jnp.einsum("qnr,nrs->qns", level_moments_top[-1], interp_map, precision=PRECISE)
        level_moments_top.append(lifted.reshape(rows_here, -1, 2, R).sum(axis=2))
    top_couplings = []
    for height in range(top_levels):
        number = groups >> height
        node = device // 2**height
        third = jnp.where(node % 2 == 0, node + 3, node - 3) % number
        if number > 4:
            source_ids = [(node - 2) % number, (node + 2) % number, third]
        else:
            source_ids = [(node + 2) % number]
        target_points = lax.dynamic_slice_in_dim(level_points[height], node, 1, 1)
        coupling = jnp.zeros((rows_here, 1, R), jnp.float32)
        for source in source_ids:
            kernel_block = kernel_matrix(
                lax.dynamic_slice_in_dim(level_points[height], source, 1, 1), target_points, kernel_scale
            )
            source_moment = lax.dynamic_slice_in_dim(level_moments_top[height], source, 1, 1)
            coupling = coupling + jnp.einsum(
                "qnr,nrs->qns", source_moment, kernel_block, precision=PRECISE
            )
        top_couplings.append(coupling)
    descent = top_couplings[-1]
    for height in range(top_levels - 2, -1, -1):
        own_edge = lax.dynamic_slice_in_dim(edge_maps[height], device // 2**height, 1, 0)
        descent = (
            jnp.einsum("qns,nrs->qnr", descent, own_edge, precision=PRECISE)
            + top_couplings[height]
        )
    for height in range(local_depth - 1, -1, -1):
        descent = jnp.einsum(
            "qns,nrs->qnr", jnp.repeat(descent, 2, axis=1), transfer_maps[height], precision=PRECISE
        )
        descent = descent + local_couplings[height]
    far_field = jnp.einsum("qbr,bpr->qbp", descent, leaf_basis, precision=PRECISE).reshape(
        rows_here, BOXES_DEV * P_SIZE
    )
    return near_field + far_field + NUGGET * probes


def solution(mesh):
    in_specs = (
        P("probe", "boxes"),
        P(None, "boxes"),
        P("boxes", None),
        P(None, "boxes"),
        P(None, "boxes"),
        P(),
        P("boxes", None),
    )
    out_specs = P("probe", "boxes")
    return jax.shard_map(body, mesh=mesh, in_specs=in_specs, out_specs=out_specs, check_vma=False)
```

```python
import jax
import jax.numpy as jnp
from jax import lax
from jax.sharding import PartitionSpec as P

BOXES_DEV = 32
P_SIZE = 256
R = 64
W = 3
INNER_DEV = 30


SHARPNESS = 0.05
NUGGET = 1.0
PRECISE = lax.Precision.HIGHEST


def with_halo(array, sides, width):
    for axis, dim in sides:
        size, length = (lax.axis_size(axis), array.shape[dim])
        up = [(i, (i + 1) % size) for i in range(size)]
        down = [(j, i) for i, j in up]
        last = lax.slice_in_dim(array, length - width, length, axis=dim)
        initial = lax.slice_in_dim(array, 0, width, axis=dim)
        before = lax.ppermute(last, axis, up)
        after = lax.ppermute(initial, axis, down)
        array = jnp.concatenate([before, array, after], axis=dim)
    return array


def kernel_matrix(left_points, right_points, kernel_scale):
    distance_sq = (left_points[0][..., :, None] - right_points[0][..., None, :]) ** 2
    distance_sq = distance_sq + (left_points[1][..., :, None] - right_points[1][..., None, :]) ** 2
    distance_sq = distance_sq + (left_points[2][..., :, None] - right_points[2][..., None, :]) ** 2
    return 1.0 / (1.0 + kernel_scale * distance_sq)


def interpolation(left_points, right_points, kernel_scale):
    values = kernel_matrix(left_points, right_points, kernel_scale)
    return values / jnp.sum(values, axis=-1, keepdims=True)


def body(probes, points, near_list, leaf_proxy, inner_proxy, top_proxy, far_list):
    groups = lax.axis_size("boxes")
    device = lax.axis_index("boxes")
    boxes_all = BOXES_DEV * groups
    kernel_scale = SHARPNESS * boxes_all
    rows_here = probes.shape[0]
    local_depth = BOXES_DEV.bit_length() - 1
    tree_depth = groups.bit_length() - 1
    live_slot = near_list >= 0
    slot_weight = live_slot.astype(jnp.float32)
    where_in = jnp.where(live_slot, (near_list - device * BOXES_DEV + W + boxes_all) % boxes_all, 0)
    box_points = points.reshape(3, BOXES_DEV, P_SIZE)
    stacked = jnp.concatenate([probes, points], axis=0)
    extended = with_halo(stacked, (("boxes", 1),), W * P_SIZE)
    extended = extended.reshape(rows_here + 3, BOXES_DEV + 2 * W, P_SIZE)

    def near_box(near_inputs):
        slot_index, slot_mask, targets = near_inputs
        near_tiles = jnp.take(extended, slot_index, axis=1)
        near_values = near_tiles[:rows_here] * slot_mask[None, :, None]
        kernel_block = kernel_matrix(near_tiles[rows_here:], targets[:, None, :], kernel_scale)
        return jnp.einsum("qns,nst->qt", near_values, kernel_block, precision=PRECISE)

    near_field = lax.map(near_box, (where_in, slot_weight, jnp.moveaxis(box_points, 1, 0)))
    near_field = jnp.moveaxis(near_field, 0, 1).reshape(rows_here, BOXES_DEV * P_SIZE)
    probe_tiles = probes.reshape(rows_here, BOXES_DEV, P_SIZE)
    leaf_points = leaf_proxy.reshape(3, BOXES_DEV, R)
    leaf_basis = interpolation(box_points, leaf_points, kernel_scale)
    inner_points = inner_proxy.reshape(3, INNER_DEV, R)
    top_points = top_proxy.reshape(3, top_proxy.shape[1] // R, R)

    def node_proxy(height, node_index):
        offset = 2 * groups - 2 * (groups >> height)
        return lax.dynamic_slice_in_dim(top_points, offset + node_index, 1, 1)

    proxies = [leaf_points]
    for height in range(1, local_depth):
        offset = BOXES_DEV - (BOXES_DEV >> height - 1)
        number = BOXES_DEV >> height
        proxies.append(inner_points[:, offset : offset + number, :])
    proxies.append(node_proxy(0, device))
    level_moments = [jnp.einsum("qbp,bpr->qbr", probe_tiles, leaf_basis, precision=PRECISE)]
    transfer_maps = []
    for height in range(local_depth):
        interp_map = interpolation(
            proxies[height], jnp.repeat(proxies[height + 1], 2, axis=1), kernel_scale
        )
        transfer_maps.append(interp_map)
        lifted = jnp.einsum("qnr,nrs->qns", level_moments[-1], interp_map, precision=PRECISE)
        level_moments.append(lifted.reshape(rows_here, -1, 2, R).sum(axis=2))
    pyramid = jnp.concatenate(
        [
            jnp.concatenate(level_moments[:local_depth], axis=1),
            jnp.concatenate([leaf_points, inner_points], axis=1),
        ],
        axis=0,
    )
    pyramid_nodes = pyramid.shape[1]
    spread = with_halo(pyramid, (("boxes", 1),), pyramid_nodes)
    local_couplings = []
    for height in range(local_depth):
        count = BOXES_DEV >> height
        start = 0 if height == 0 else 2 * BOXES_DEV - (BOXES_DEV >> height - 1)
        view = jnp.concatenate(
            [
                spread[:, block * pyramid_nodes + start : block * pyramid_nodes + start + count, :]
                for block in range(3)
            ],
            axis=1,
        )
        if height == 0:
            live_far = far_list >= 0
            slot_ids = [
                jnp.where(
                    live_far[:, slot],
                    (far_list[:, slot] - device * BOXES_DEV + BOXES_DEV + boxes_all) % boxes_all,
                    0,
                )
                for slot in range(3)
            ]
            slot_masks = [live_far[:, slot].astype(jnp.float32)[None, :, None] for slot in range(3)]
        else:
            node = jnp.arange(count, dtype=jnp.int32)
            third = jnp.where(node % 2 == 0, node + 3, node - 3)
            slot_ids = [node - 2 + count, node + 2 + count, third + count]
            slot_masks = [None, None, None]
        coupling = jnp.zeros((rows_here, count, R), jnp.float32)
        for slot in range(3):
            picked = jnp.take(view, slot_ids[slot], axis=1)
            kernel_block = kernel_matrix(picked[rows_here:], proxies[height], kernel_scale)
            source_moment = picked[:rows_here]
            if slot_masks[slot] is not None:
                source_moment = source_moment * slot_masks[slot]
            coupling = coupling + jnp.einsum(
                "qnr,nrs->qns", source_moment, kernel_block, precision=PRECISE
            )
        local_couplings.append(coupling)

    top_levels = tree_depth - 1
    level_points = []
    level_offsets = []
    for height in range(top_levels):
        offset = 2 * groups - 2 * (groups >> height)
        level_offsets.append(offset)
        level_points.append(top_points[:, offset : offset + (groups >> height), :])
    own_edges = []
    for height in range(top_levels - 1):
        own_edges.append(
            interpolation(
                lax.dynamic_slice_in_dim(level_points[height], device // 2**height, 1, 1),
                lax.dynamic_slice_in_dim(level_points[height + 1], device // 2 ** (height + 1), 1, 1),
                kernel_scale,
            )
        )
    path_moment = level_moments[local_depth]
    board = jnp.zeros((rows_here, level_offsets[-1] + 4, R), jnp.float32)
    for height in range(top_levels):
        if height > 0:
            path_moment = jnp.einsum(
                "qnr,nrs->qns", path_moment, own_edges[height - 1], precision=PRECISE
            )
        board = lax.dynamic_update_slice_in_dim(
            board, path_moment, level_offsets[height] + device // 2**height, 1
        )
    board = lax.psum(board, "boxes")
    top_couplings = []
    for height in range(top_levels):
        number = groups >> height
        node = device // 2**height
        third = jnp.where(node % 2 == 0, node + 3, node - 3) % number
        if number > 4:
            source_ids = [(node - 2) % number, (node + 2) % number, third]
        else:
            source_ids = [(node + 2) % number]
        target_points = lax.dynamic_slice_in_dim(level_points[height], node, 1, 1)
        coupling = jnp.zeros((rows_here, 1, R), jnp.float32)
        for source in source_ids:
            kernel_block = kernel_matrix(
                lax.dynamic_slice_in_dim(level_points[height], source, 1, 1), target_points, kernel_scale
            )
            source_moment = lax.dynamic_slice_in_dim(board, level_offsets[height] + source, 1, 1)
            coupling = coupling + jnp.einsum(
                "qnr,nrs->qns", source_moment, kernel_block, precision=PRECISE
            )
        top_couplings.append(coupling)
    descent = top_couplings[-1]
    for height in range(top_levels - 2, -1, -1):
        descent = (
            jnp.einsum("qns,nrs->qnr", descent, own_edges[height], precision=PRECISE)
            + top_couplings[height]
        )
    for height in range(local_depth - 1, -1, -1):
        descent = jnp.einsum(
            "qns,nrs->qnr", jnp.repeat(descent, 2, axis=1), transfer_maps[height], precision=PRECISE
        )
        descent = descent + local_couplings[height]
    far_field = jnp.einsum("qbr,bpr->qbp", descent, leaf_basis, precision=PRECISE).reshape(
        rows_here, BOXES_DEV * P_SIZE
    )
    return near_field + far_field + NUGGET * probes


def solution(mesh):
    in_specs = (
        P("probe", "boxes"),
        P(None, "boxes"),
        P("boxes", None),
        P(None, "boxes"),
        P(None, "boxes"),
        P(),
        P("boxes", None),
    )
    out_specs = P("probe", "boxes")
    return jax.shard_map(body, mesh=mesh, in_specs=in_specs, out_specs=out_specs, check_vma=False)
```

```python
import functools

import jax
import jax.numpy as jnp
from jax import lax
from jax.experimental import pallas as pl
from jax.experimental.pallas import tpu as pltpu
from jax.sharding import PartitionSpec as P

BOXES_DEV = 32
P_SIZE = 256
R = 64
W = 3
INNER_DEV = 30


SHARPNESS = 0.05
NUGGET = 1.0
PRECISE = lax.Precision.HIGHEST


def with_halo(array, sides, width):
    for axis, dim in sides:
        size, length = (lax.axis_size(axis), array.shape[dim])
        up = [(i, (i + 1) % size) for i in range(size)]
        down = [(j, i) for i, j in up]
        last = lax.slice_in_dim(array, length - width, length, axis=dim)
        initial = lax.slice_in_dim(array, 0, width, axis=dim)
        before = lax.ppermute(last, axis, up)
        after = lax.ppermute(initial, axis, down)
        array = jnp.concatenate([before, array, after], axis=dim)
    return array


def kernel_matrix(left_points, right_points, kernel_scale):
    distance_sq = (left_points[0][..., :, None] - right_points[0][..., None, :]) ** 2
    distance_sq = distance_sq + (left_points[1][..., :, None] - right_points[1][..., None, :]) ** 2
    distance_sq = distance_sq + (left_points[2][..., :, None] - right_points[2][..., None, :]) ** 2
    return 1.0 / (1.0 + kernel_scale * distance_sq)


def interpolation(left_points, right_points, kernel_scale):
    values = kernel_matrix(left_points, right_points, kernel_scale)
    return values / jnp.sum(values, axis=-1, keepdims=True)


def near_kernel(kernel_scale, slots, source_ref, probes_ref, coords_ref, target_ref, out_ref):
    box = pl.program_id(0)
    target_x = target_ref[0:1, :]
    target_y = target_ref[1:2, :]
    target_z = target_ref[2:3, :]
    out_ref[...] = jnp.zeros_like(out_ref)
    for slot in range(slots):
        source = source_ref[box * slots + slot]

        @pl.when(source >= 0)
        def _():
            near = coords_ref[source]
            distance_sq = (near[:, 0:1] - target_x) ** 2
            distance_sq = distance_sq + (near[:, 1:2] - target_y) ** 2
            distance_sq = distance_sq + (near[:, 2:3] - target_z) ** 2
            kernel_block = 1.0 / (1.0 + kernel_scale * distance_sq)
            out_ref[...] += jnp.dot(
                probes_ref[source], kernel_block, precision=PRECISE,
                preferred_element_type=jnp.float32,
            )


def near_field_call(slot_source, probe_tiles, coord_tiles, points, kernel_scale):
    tiles, rows, size = probe_tiles.shape
    boxes = points.shape[1] // size
    slots = slot_source.shape[0] // boxes
    return pl.pallas_call(
        functools.partial(near_kernel, kernel_scale, slots),
        out_shape=jax.ShapeDtypeStruct((rows, boxes * size), jnp.float32),
        grid_spec=pltpu.PrefetchScalarGridSpec(
            num_scalar_prefetch=1,
            grid=(boxes,),
            in_specs=[
                pl.BlockSpec((tiles, rows, size), lambda b, s: (0, 0, 0)),
                pl.BlockSpec((tiles, size, 3), lambda b, s: (0, 0, 0)),
                pl.BlockSpec((3, size), lambda b, s: (0, b)),
            ],
            out_specs=pl.BlockSpec((rows, size), lambda b, s: (0, b)),
        ),
        compiler_params=pltpu.CompilerParams(dimension_semantics=("arbitrary",)),
        cost_estimate=pl.CostEstimate(
            flops=boxes * slots * size * size * (2 * rows + 12),
            transcendentals=0,
            bytes_accessed=4 * (probe_tiles.size + coord_tiles.size * 43 + 2 * rows * boxes * size),
        ),
    )(slot_source, probe_tiles, coord_tiles, points)


def body(probes, points, near_list, leaf_proxy, inner_proxy, top_proxy, far_list):
    groups = lax.axis_size("boxes")
    device = lax.axis_index("boxes")
    boxes_all = BOXES_DEV * groups
    kernel_scale = SHARPNESS * boxes_all
    rows_here = probes.shape[0]
    local_depth = BOXES_DEV.bit_length() - 1
    tree_depth = groups.bit_length() - 1
    live_slot = near_list >= 0
    slot_weight = live_slot.astype(jnp.float32)
    where_in = jnp.where(live_slot, (near_list - device * BOXES_DEV + W + boxes_all) % boxes_all, 0)
    box_points = points.reshape(3, BOXES_DEV, P_SIZE)
    stacked = jnp.concatenate([probes, points], axis=0)
    extended = with_halo(stacked, (("boxes", 1),), W * P_SIZE)
    extended = extended.reshape(rows_here + 3, BOXES_DEV + 2 * W, P_SIZE)

    slot_source = jnp.where(live_slot, jnp.clip(where_in, 0, BOXES_DEV + 2 * W - 1), -1)
    near_field = near_field_call(
        slot_source.reshape(-1).astype(jnp.int32),
        jnp.moveaxis(extended[:rows_here], 1, 0),
        jnp.moveaxis(extended[rows_here:], 0, 2),
        points,
        kernel_scale,
    )
    probe_tiles = probes.reshape(rows_here, BOXES_DEV, P_SIZE)
    leaf_points = leaf_proxy.reshape(3, BOXES_DEV, R)
    leaf_basis = interpolation(box_points, leaf_points, kernel_scale)
    inner_points = inner_proxy.reshape(3, INNER_DEV, R)
    top_points = top_proxy.reshape(3, top_proxy.shape[1] // R, R)

    def node_proxy(height, node_index):
        offset = 2 * groups - 2 * (groups >> height)
        return lax.dynamic_slice_in_dim(top_points, offset + node_index, 1, 1)

    proxies = [leaf_points]
    for height in range(1, local_depth):
        offset = BOXES_DEV - (BOXES_DEV >> height - 1)
        number = BOXES_DEV >> height
        proxies.append(inner_points[:, offset : offset + number, :])
    proxies.append(node_proxy(0, device))
    level_moments = [jnp.einsum("qbp,bpr->qbr", probe_tiles, leaf_basis, precision=PRECISE)]
    transfer_maps = []
    for height in range(local_depth):
        interp_map = interpolation(
            proxies[height], jnp.repeat(proxies[height + 1], 2, axis=1), kernel_scale
        )
        transfer_maps.append(interp_map)
        lifted = jnp.einsum("qnr,nrs->qns", level_moments[-1], interp_map, precision=PRECISE)
        level_moments.append(lifted.reshape(rows_here, -1, 2, R).sum(axis=2))
    pyramid = jnp.concatenate(
        [
            jnp.concatenate(level_moments[:local_depth], axis=1),
            jnp.concatenate([leaf_points, inner_points], axis=1),
        ],
        axis=0,
    )
    pyramid_nodes = pyramid.shape[1]
    spread = with_halo(pyramid, (("boxes", 1),), pyramid_nodes)
    local_couplings = []
    for height in range(local_depth):
        count = BOXES_DEV >> height
        start = 0 if height == 0 else 2 * BOXES_DEV - (BOXES_DEV >> height - 1)
        view = jnp.concatenate(
            [
                spread[:, block * pyramid_nodes + start : block * pyramid_nodes + start + count, :]
                for block in range(3)
            ],
            axis=1,
        )
        if height == 0:
            live_far = far_list >= 0
            slot_ids = [
                jnp.where(
                    live_far[:, slot],
                    (far_list[:, slot] - device * BOXES_DEV + BOXES_DEV + boxes_all) % boxes_all,
                    0,
                )
                for slot in range(3)
            ]
            slot_masks = [live_far[:, slot].astype(jnp.float32)[None, :, None] for slot in range(3)]
        else:
            node = jnp.arange(count, dtype=jnp.int32)
            third = jnp.where(node % 2 == 0, node + 3, node - 3)
            slot_ids = [node - 2 + count, node + 2 + count, third + count]
            slot_masks = [None, None, None]
        coupling = jnp.zeros((rows_here, count, R), jnp.float32)
        for slot in range(3):
            picked = jnp.take(view, slot_ids[slot], axis=1)
            kernel_block = kernel_matrix(picked[rows_here:], proxies[height], kernel_scale)
            source_moment = picked[:rows_here]
            if slot_masks[slot] is not None:
                source_moment = source_moment * slot_masks[slot]
            coupling = coupling + jnp.einsum(
                "qnr,nrs->qns", source_moment, kernel_block, precision=PRECISE
            )
        local_couplings.append(coupling)

    top_levels = tree_depth - 1
    level_points = []
    for height in range(top_levels):
        offset = 2 * groups - 2 * (groups >> height)
        level_points.append(top_points[:, offset : offset + (groups >> height), :])
    level_moments_top = [
        lax.all_gather(level_moments[local_depth], "boxes", axis=1, tiled=True)
    ]
    edge_maps = []
    for height in range(top_levels - 1):
        interp_map = interpolation(
            level_points[height], jnp.repeat(level_points[height + 1], 2, axis=1), kernel_scale
        )
        edge_maps.append(interp_map)
        lifted = jnp.einsum("qnr,nrs->qns", level_moments_top[-1], interp_map, precision=PRECISE)
        level_moments_top.append(lifted.reshape(rows_here, -1, 2, R).sum(axis=2))
    top_couplings = []
    for height in range(top_levels):
        number = groups >> height
        node = device // 2**height
        third = jnp.where(node % 2 == 0, node + 3, node - 3) % number
        if number > 4:
            source_ids = [(node - 2) % number, (node + 2) % number, third]
        else:
            source_ids = [(node + 2) % number]
        target_points = lax.dynamic_slice_in_dim(level_points[height], node, 1, 1)
        coupling = jnp.zeros((rows_here, 1, R), jnp.float32)
        for source in source_ids:
            kernel_block = kernel_matrix(
                lax.dynamic_slice_in_dim(level_points[height], source, 1, 1), target_points, kernel_scale
            )
            source_moment = lax.dynamic_slice_in_dim(level_moments_top[height], source, 1, 1)
            coupling = coupling + jnp.einsum(
                "qnr,nrs->qns", source_moment, kernel_block, precision=PRECISE
            )
        top_couplings.append(coupling)
    descent = top_couplings[-1]
    for height in range(top_levels - 2, -1, -1):
        own_edge = lax.dynamic_slice_in_dim(edge_maps[height], device // 2**height, 1, 0)
        descent = (
            jnp.einsum("qns,nrs->qnr", descent, own_edge, precision=PRECISE)
            + top_couplings[height]
        )
    for height in range(local_depth - 1, -1, -1):
        descent = jnp.einsum(
            "qns,nrs->qnr", jnp.repeat(descent, 2, axis=1), transfer_maps[height], precision=PRECISE
        )
        descent = descent + local_couplings[height]
    far_field = jnp.einsum("qbr,bpr->qbp", descent, leaf_basis, precision=PRECISE).reshape(
        rows_here, BOXES_DEV * P_SIZE
    )
    return near_field + far_field + NUGGET * probes


def solution(mesh):
    in_specs = (
        P("probe", "boxes"),
        P(None, "boxes"),
        P("boxes", None),
        P(None, "boxes"),
        P(None, "boxes"),
        P(),
        P("boxes", None),
    )
    out_specs = P("probe", "boxes")
    return jax.shard_map(body, mesh=mesh, in_specs=in_specs, out_specs=out_specs, check_vma=False)
```

```python
import functools

import jax
import jax.numpy as jnp
from jax import lax
from jax.experimental import pallas as pl
from jax.experimental.pallas import tpu as pltpu
from jax.sharding import PartitionSpec as P

BOXES_DEV = 32
P_SIZE = 256
R = 64
W = 3
INNER_DEV = 30


SHARPNESS = 0.05
NUGGET = 1.0
PRECISE = lax.Precision.HIGHEST


def with_halo(array, sides, width):
    for axis, dim in sides:
        size, length = (lax.axis_size(axis), array.shape[dim])
        up = [(i, (i + 1) % size) for i in range(size)]
        down = [(j, i) for i, j in up]
        last = lax.slice_in_dim(array, length - width, length, axis=dim)
        initial = lax.slice_in_dim(array, 0, width, axis=dim)
        before = lax.ppermute(last, axis, up)
        after = lax.ppermute(initial, axis, down)
        array = jnp.concatenate([before, array, after], axis=dim)
    return array


def kernel_matrix(left_points, right_points, kernel_scale):
    distance_sq = (left_points[0][..., :, None] - right_points[0][..., None, :]) ** 2
    distance_sq = distance_sq + (left_points[1][..., :, None] - right_points[1][..., None, :]) ** 2
    distance_sq = distance_sq + (left_points[2][..., :, None] - right_points[2][..., None, :]) ** 2
    return 1.0 / (1.0 + kernel_scale * distance_sq)


def interpolation(left_points, right_points, kernel_scale):
    values = kernel_matrix(left_points, right_points, kernel_scale)
    return values / jnp.sum(values, axis=-1, keepdims=True)


def near_kernel(kernel_scale, slots, source_ref, probes_ref, coords_ref, target_ref, out_ref):
    box = pl.program_id(0)
    target_x = target_ref[0:1, :]
    target_y = target_ref[1:2, :]
    target_z = target_ref[2:3, :]
    out_ref[...] = jnp.zeros_like(out_ref)
    for slot in range(slots):
        source = source_ref[box * slots + slot]

        @pl.when(source >= 0)
        def _():
            near = coords_ref[source]
            distance_sq = (near[:, 0:1] - target_x) ** 2
            distance_sq = distance_sq + (near[:, 1:2] - target_y) ** 2
            distance_sq = distance_sq + (near[:, 2:3] - target_z) ** 2
            kernel_block = 1.0 / (1.0 + kernel_scale * distance_sq)
            out_ref[...] += jnp.dot(
                probes_ref[source], kernel_block, precision=PRECISE,
                preferred_element_type=jnp.float32,
            )


def near_field_call(slot_source, probe_tiles, coord_tiles, points, kernel_scale):
    tiles, rows, size = probe_tiles.shape
    boxes = points.shape[1] // size
    slots = slot_source.shape[0] // boxes
    return pl.pallas_call(
        functools.partial(near_kernel, kernel_scale, slots),
        out_shape=jax.ShapeDtypeStruct((rows, boxes * size), jnp.float32),
        grid_spec=pltpu.PrefetchScalarGridSpec(
            num_scalar_prefetch=1,
            grid=(boxes,),
            in_specs=[
                pl.BlockSpec((tiles, rows, size), lambda b, s: (0, 0, 0)),
                pl.BlockSpec((tiles, size, 3), lambda b, s: (0, 0, 0)),
                pl.BlockSpec((3, size), lambda b, s: (0, b)),
            ],
            out_specs=pl.BlockSpec((rows, size), lambda b, s: (0, b)),
        ),
        compiler_params=pltpu.CompilerParams(dimension_semantics=("arbitrary",)),
        cost_estimate=pl.CostEstimate(
            flops=boxes * slots * size * size * (2 * rows + 12),
            transcendentals=0,
            bytes_accessed=4 * (probe_tiles.size + coord_tiles.size * 43 + 2 * rows * boxes * size),
        ),
    )(slot_source, probe_tiles, coord_tiles, points)


def body(probes, points, near_list, leaf_proxy, inner_proxy, top_proxy, far_list):
    groups = lax.axis_size("boxes")
    device = lax.axis_index("boxes")
    boxes_all = BOXES_DEV * groups
    kernel_scale = SHARPNESS * boxes_all
    rows_here = probes.shape[0]
    local_depth = BOXES_DEV.bit_length() - 1
    tree_depth = groups.bit_length() - 1
    live_slot = near_list >= 0
    slot_weight = live_slot.astype(jnp.float32)
    where_in = jnp.where(live_slot, (near_list - device * BOXES_DEV + W + boxes_all) % boxes_all, 0)
    box_points = points.reshape(3, BOXES_DEV, P_SIZE)
    stacked = jnp.concatenate([probes, points], axis=0)
    extended = with_halo(stacked, (("boxes", 1),), W * P_SIZE)
    extended = extended.reshape(rows_here + 3, BOXES_DEV + 2 * W, P_SIZE)

    slot_source = jnp.where(live_slot, jnp.clip(where_in, 0, BOXES_DEV + 2 * W - 1), -1)
    near_field = near_field_call(
        slot_source.reshape(-1).astype(jnp.int32),
        jnp.moveaxis(extended[:rows_here], 1, 0),
        jnp.moveaxis(extended[rows_here:], 0, 2),
        points,
        kernel_scale,
    )
    probe_tiles = probes.reshape(rows_here, BOXES_DEV, P_SIZE)
    leaf_points = leaf_proxy.reshape(3, BOXES_DEV, R)
    leaf_basis = interpolation(box_points, leaf_points, kernel_scale)
    inner_points = inner_proxy.reshape(3, INNER_DEV, R)
    top_points = top_proxy.reshape(3, top_proxy.shape[1] // R, R)

    def node_proxy(height, node_index):
        offset = 2 * groups - 2 * (groups >> height)
        return lax.dynamic_slice_in_dim(top_points, offset + node_index, 1, 1)

    proxies = [leaf_points]
    for height in range(1, local_depth):
        offset = BOXES_DEV - (BOXES_DEV >> height - 1)
        number = BOXES_DEV >> height
        proxies.append(inner_points[:, offset : offset + number, :])
    proxies.append(node_proxy(0, device))
    level_moments = [jnp.einsum("qbp,bpr->qbr", probe_tiles, leaf_basis, precision=PRECISE)]
    transfer_maps = []
    for height in range(local_depth):
        interp_map = interpolation(
            proxies[height], jnp.repeat(proxies[height + 1], 2, axis=1), kernel_scale
        )
        transfer_maps.append(interp_map)
        lifted = jnp.einsum("qnr,nrs->qns", level_moments[-1], interp_map, precision=PRECISE)
        level_moments.append(lifted.reshape(rows_here, -1, 2, R).sum(axis=2))
    pyramid = jnp.concatenate(
        [
            jnp.concatenate(level_moments[:local_depth], axis=1),
            jnp.concatenate([leaf_points, inner_points], axis=1),
        ],
        axis=0,
    )
    pyramid_nodes = pyramid.shape[1]
    spread = with_halo(pyramid, (("boxes", 1),), pyramid_nodes)
    local_couplings = []
    for height in range(local_depth):
        count = BOXES_DEV >> height
        start = 0 if height == 0 else 2 * BOXES_DEV - (BOXES_DEV >> height - 1)
        view = jnp.concatenate(
            [
                spread[:, block * pyramid_nodes + start : block * pyramid_nodes + start + count, :]
                for block in range(3)
            ],
            axis=1,
        )
        if height == 0:
            live_far = far_list >= 0
            slot_ids = [
                jnp.where(
                    live_far[:, slot],
                    (far_list[:, slot] - device * BOXES_DEV + BOXES_DEV + boxes_all) % boxes_all,
                    0,
                )
                for slot in range(3)
            ]
            slot_masks = [live_far[:, slot].astype(jnp.float32)[None, :, None] for slot in range(3)]
        else:
            node = jnp.arange(count, dtype=jnp.int32)
            third = jnp.where(node % 2 == 0, node + 3, node - 3)
            slot_ids = [node - 2 + count, node + 2 + count, third + count]
            slot_masks = [None, None, None]
        coupling = jnp.zeros((rows_here, count, R), jnp.float32)
        for slot in range(3):
            picked = jnp.take(view, slot_ids[slot], axis=1)
            kernel_block = kernel_matrix(picked[rows_here:], proxies[height], kernel_scale)
            source_moment = picked[:rows_here]
            if slot_masks[slot] is not None:
                source_moment = source_moment * slot_masks[slot]
            coupling = coupling + jnp.einsum(
                "qnr,nrs->qns", source_moment, kernel_block, precision=PRECISE
            )
        local_couplings.append(coupling)

    top_levels = tree_depth - 1
    level_points = []
    for height in range(top_levels):
        offset = 2 * groups - 2 * (groups >> height)
        level_points.append(top_points[:, offset : offset + (groups >> height), :])
    own_edges = []
    for height in range(top_levels - 1):
        own_edges.append(
            interpolation(
                lax.dynamic_slice_in_dim(level_points[height], device // 2**height, 1, 1),
                lax.dynamic_slice_in_dim(level_points[height + 1], device // 2 ** (height + 1), 1, 1),
                kernel_scale,
            )
        )
    path_moments = [level_moments[local_depth]]
    for height in range(top_levels - 1):
        path_moments.append(
            jnp.einsum("qnr,nrs->qns", path_moments[-1], own_edges[height], precision=PRECISE)
        )
    gathered = lax.all_gather(jnp.concatenate(path_moments, axis=1), "boxes", axis=0)
    top_couplings = []
    for height in range(top_levels):
        number = groups >> height
        node = device // 2**height
        level_sums = gathered[:, :, height, :].reshape(number, 2**height, rows_here, R).sum(axis=1)
        third = jnp.where(node % 2 == 0, node + 3, node - 3) % number
        if number > 4:
            source_ids = [(node - 2) % number, (node + 2) % number, third]
        else:
            source_ids = [(node + 2) % number]
        target_points = lax.dynamic_slice_in_dim(level_points[height], node, 1, 1)
        coupling = jnp.zeros((rows_here, 1, R), jnp.float32)
        for source in source_ids:
            kernel_block = kernel_matrix(
                lax.dynamic_slice_in_dim(level_points[height], source, 1, 1), target_points, kernel_scale
            )
            source_moment = lax.dynamic_index_in_dim(level_sums, source, 0, keepdims=False)
            coupling = coupling + jnp.einsum(
                "qnr,nrs->qns", source_moment[:, None, :], kernel_block, precision=PRECISE
            )
        top_couplings.append(coupling)
    descent = top_couplings[-1]
    for height in range(top_levels - 2, -1, -1):
        descent = (
            jnp.einsum("qns,nrs->qnr", descent, own_edges[height], precision=PRECISE)
            + top_couplings[height]
        )
    for height in range(local_depth - 1, -1, -1):
        descent = jnp.einsum(
            "qns,nrs->qnr", jnp.repeat(descent, 2, axis=1), transfer_maps[height], precision=PRECISE
        )
        descent = descent + local_couplings[height]
    far_field = jnp.einsum("qbr,bpr->qbp", descent, leaf_basis, precision=PRECISE).reshape(
        rows_here, BOXES_DEV * P_SIZE
    )
    return near_field + far_field + NUGGET * probes


def solution(mesh):
    in_specs = (
        P("probe", "boxes"),
        P(None, "boxes"),
        P("boxes", None),
        P(None, "boxes"),
        P(None, "boxes"),
        P(),
        P("boxes", None),
    )
    out_specs = P("probe", "boxes")
    return jax.shard_map(body, mesh=mesh, in_specs=in_specs, out_specs=out_specs, check_vma=False)
```

```python
import functools

import jax
import jax.numpy as jnp
from jax import lax
from jax.experimental import pallas as pl
from jax.experimental.pallas import tpu as pltpu
from jax.sharding import PartitionSpec as P

BOXES_DEV = 32
P_SIZE = 256
R = 64
W = 3
INNER_DEV = 30


SHARPNESS = 0.05
NUGGET = 1.0
PRECISE = lax.Precision.HIGHEST


def with_halo(array, sides, width):
    for axis, dim in sides:
        size, length = (lax.axis_size(axis), array.shape[dim])
        up = [(i, (i + 1) % size) for i in range(size)]
        down = [(j, i) for i, j in up]
        last = lax.slice_in_dim(array, length - width, length, axis=dim)
        initial = lax.slice_in_dim(array, 0, width, axis=dim)
        before = lax.ppermute(last, axis, up)
        after = lax.ppermute(initial, axis, down)
        array = jnp.concatenate([before, array, after], axis=dim)
    return array


def kernel_matrix(left_points, right_points, kernel_scale):
    distance_sq = (left_points[0][..., :, None] - right_points[0][..., None, :]) ** 2
    distance_sq = distance_sq + (left_points[1][..., :, None] - right_points[1][..., None, :]) ** 2
    distance_sq = distance_sq + (left_points[2][..., :, None] - right_points[2][..., None, :]) ** 2
    return 1.0 / (1.0 + kernel_scale * distance_sq)


def interpolation(left_points, right_points, kernel_scale):
    values = kernel_matrix(left_points, right_points, kernel_scale)
    return values / jnp.sum(values, axis=-1, keepdims=True)


def near_kernel(kernel_scale, slots, source_ref, probes_ref, coords_ref, target_ref, out_ref):
    box = pl.program_id(0)
    target_x = target_ref[0:1, :]
    target_y = target_ref[1:2, :]
    target_z = target_ref[2:3, :]
    out_ref[...] = jnp.zeros_like(out_ref)
    for slot in range(slots):
        source = source_ref[box * slots + slot]

        @pl.when(source >= 0)
        def _():
            near = coords_ref[source]
            distance_sq = (near[:, 0:1] - target_x) ** 2
            distance_sq = distance_sq + (near[:, 1:2] - target_y) ** 2
            distance_sq = distance_sq + (near[:, 2:3] - target_z) ** 2
            kernel_block = 1.0 / (1.0 + kernel_scale * distance_sq)
            out_ref[...] += jnp.dot(
                probes_ref[source], kernel_block, precision=PRECISE,
                preferred_element_type=jnp.float32,
            )


def near_field_call(slot_source, probe_tiles, coord_tiles, points, kernel_scale):
    tiles, rows, size = probe_tiles.shape
    boxes = points.shape[1] // size
    slots = slot_source.shape[0] // boxes
    return pl.pallas_call(
        functools.partial(near_kernel, kernel_scale, slots),
        out_shape=jax.ShapeDtypeStruct((rows, boxes * size), jnp.float32),
        grid_spec=pltpu.PrefetchScalarGridSpec(
            num_scalar_prefetch=1,
            grid=(boxes,),
            in_specs=[
                pl.BlockSpec((tiles, rows, size), lambda b, s: (0, 0, 0)),
                pl.BlockSpec((tiles, size, 3), lambda b, s: (0, 0, 0)),
                pl.BlockSpec((3, size), lambda b, s: (0, b)),
            ],
            out_specs=pl.BlockSpec((rows, size), lambda b, s: (0, b)),
        ),
        compiler_params=pltpu.CompilerParams(dimension_semantics=("arbitrary",)),
        cost_estimate=pl.CostEstimate(
            flops=boxes * slots * size * size * (2 * rows + 12),
            transcendentals=0,
            bytes_accessed=4 * (probe_tiles.size + coord_tiles.size * 43 + 2 * rows * boxes * size),
        ),
    )(slot_source, probe_tiles, coord_tiles, points)


def body(probes, points, near_list, leaf_proxy, inner_proxy, top_proxy, far_list):
    groups = lax.axis_size("boxes")
    device = lax.axis_index("boxes")
    boxes_all = BOXES_DEV * groups
    kernel_scale = SHARPNESS * boxes_all
    rows_here = probes.shape[0]
    local_depth = BOXES_DEV.bit_length() - 1
    tree_depth = groups.bit_length() - 1
    live_slot = near_list >= 0
    slot_weight = live_slot.astype(jnp.float32)
    where_in = jnp.where(live_slot, (near_list - device * BOXES_DEV + W + boxes_all) % boxes_all, 0)
    box_points = points.reshape(3, BOXES_DEV, P_SIZE)
    stacked = jnp.concatenate([probes, points], axis=0)
    extended = with_halo(stacked, (("boxes", 1),), W * P_SIZE)
    extended = extended.reshape(rows_here + 3, BOXES_DEV + 2 * W, P_SIZE)

    slot_source = jnp.where(live_slot, jnp.clip(where_in, 0, BOXES_DEV + 2 * W - 1), -1)
    near_field = near_field_call(
        slot_source.reshape(-1).astype(jnp.int32),
        jnp.moveaxis(extended[:rows_here], 1, 0),
        jnp.moveaxis(extended[rows_here:], 0, 2),
        points,
        kernel_scale,
    )
    probe_tiles = probes.reshape(rows_here, BOXES_DEV, P_SIZE)
    leaf_points = leaf_proxy.reshape(3, BOXES_DEV, R)
    leaf_basis = interpolation(box_points, leaf_points, kernel_scale)
    inner_points = inner_proxy.reshape(3, INNER_DEV, R)
    top_points = top_proxy.reshape(3, top_proxy.shape[1] // R, R)

    def node_proxy(height, node_index):
        offset = 2 * groups - 2 * (groups >> height)
        return lax.dynamic_slice_in_dim(top_points, offset + node_index, 1, 1)

    proxies = [leaf_points]
    for height in range(1, local_depth):
        offset = BOXES_DEV - (BOXES_DEV >> height - 1)
        number = BOXES_DEV >> height
        proxies.append(inner_points[:, offset : offset + number, :])
    proxies.append(node_proxy(0, device))
    level_moments = [jnp.einsum("qbp,bpr->qbr", probe_tiles, leaf_basis, precision=PRECISE)]
    transfer_maps = []
    for height in range(local_depth):
        interp_map = interpolation(
            proxies[height], jnp.repeat(proxies[height + 1], 2, axis=1), kernel_scale
        )
        transfer_maps.append(interp_map)
        lifted = jnp.einsum("qnr,nrs->qns", level_moments[-1], interp_map, precision=PRECISE)
        level_moments.append(lifted.reshape(rows_here, -1, 2, R).sum(axis=2))
    pyramid = jnp.concatenate(
        [
            jnp.concatenate(level_moments[:local_depth], axis=1),
            jnp.concatenate([leaf_points, inner_points], axis=1),
        ],
        axis=0,
    )
    pyramid_nodes = pyramid.shape[1]
    spread = with_halo(pyramid, (("boxes", 1),), pyramid_nodes)
    index_parts, target_parts, mask_parts = [], [], []
    for height in range(local_depth):
        count = BOXES_DEV >> height
        start = 0 if height == 0 else 2 * BOXES_DEV - (BOXES_DEV >> height - 1)
        if height == 0:
            live_far = far_list >= 0
            view_ids = [
                jnp.where(
                    live_far[:, slot],
                    (far_list[:, slot] - device * BOXES_DEV + BOXES_DEV + boxes_all) % boxes_all,
                    0,
                )
                for slot in range(3)
            ]
            mask_parts += [live_far[:, slot].astype(jnp.float32) for slot in range(3)]
        else:
            node = jnp.arange(count, dtype=jnp.int32)
            third = jnp.where(node % 2 == 0, node + 3, node - 3)
            view_ids = [node - 2 + count, node + 2 + count, third + count]
            mask_parts += [jnp.ones((count,), jnp.float32)] * 3
        for view_id in view_ids:
            index_parts.append(view_id // count * pyramid_nodes + start + view_id % count)
            target_parts.append(proxies[height])
    picked = jnp.take(spread, jnp.concatenate(index_parts), axis=1)
    kernel_block = kernel_matrix(picked[rows_here:], jnp.concatenate(target_parts, axis=1), kernel_scale)
    source_moment = picked[:rows_here] * jnp.concatenate(mask_parts)[None, :, None]
    contributions = jnp.einsum("qnr,nrs->qns", source_moment, kernel_block, precision=PRECISE)
    local_couplings = []
    first = 0
    for height in range(local_depth):
        count = BOXES_DEV >> height
        part = contributions[:, first : first + 3 * count, :]
        local_couplings.append(part.reshape(rows_here, 3, count, R).sum(axis=1))
        first += 3 * count

    top_levels = tree_depth - 1
    level_points = []
    for height in range(top_levels):
        offset = 2 * groups - 2 * (groups >> height)
        level_points.append(top_points[:, offset : offset + (groups >> height), :])
    own_edges = []
    for height in range(top_levels - 1):
        own_edges.append(
            interpolation(
                lax.dynamic_slice_in_dim(level_points[height], device // 2**height, 1, 1),
                lax.dynamic_slice_in_dim(level_points[height + 1], device // 2 ** (height + 1), 1, 1),
                kernel_scale,
            )
        )
    path_moments = [level_moments[local_depth]]
    for height in range(top_levels - 1):
        path_moments.append(
            jnp.einsum("qnr,nrs->qns", path_moments[-1], own_edges[height], precision=PRECISE)
        )
    gathered = lax.all_gather(jnp.concatenate(path_moments, axis=1), "boxes", axis=0)
    top_moments, top_sources, top_targets, top_slots = [], [], [], []
    for height in range(top_levels):
        number = groups >> height
        node = device // 2**height
        level_sums = gathered[:, :, height, :].reshape(number, 2**height, rows_here, R).sum(axis=1)
        third = jnp.where(node % 2 == 0, node + 3, node - 3) % number
        if number > 4:
            source_ids = [(node - 2) % number, (node + 2) % number, third]
        else:
            source_ids = [(node + 2) % number]
        top_slots.append(len(source_ids))
        for source in source_ids:
            top_moments.append(lax.dynamic_index_in_dim(level_sums, source, 0, keepdims=True))
            top_sources.append(lax.dynamic_slice_in_dim(level_points[height], source, 1, 1))
            top_targets.append(lax.dynamic_slice_in_dim(level_points[height], node, 1, 1))
    kernel_block = kernel_matrix(
        jnp.concatenate(top_sources, axis=1), jnp.concatenate(top_targets, axis=1), kernel_scale
    )
    contributions = jnp.einsum(
        "nqr,nrs->qns", jnp.concatenate(top_moments, axis=0), kernel_block, precision=PRECISE
    )
    top_couplings = []
    first = 0
    for slots in top_slots:
        top_couplings.append(contributions[:, first : first + slots, :].sum(axis=1, keepdims=True))
        first += slots
    descent = top_couplings[-1]
    for height in range(top_levels - 2, -1, -1):
        descent = (
            jnp.einsum("qns,nrs->qnr", descent, own_edges[height], precision=PRECISE)
            + top_couplings[height]
        )
    for height in range(local_depth - 1, -1, -1):
        descent = jnp.einsum(
            "qns,nrs->qnr", jnp.repeat(descent, 2, axis=1), transfer_maps[height], precision=PRECISE
        )
        descent = descent + local_couplings[height]
    far_field = jnp.einsum("qbr,bpr->qbp", descent, leaf_basis, precision=PRECISE).reshape(
        rows_here, BOXES_DEV * P_SIZE
    )
    return near_field + far_field + NUGGET * probes


def solution(mesh):
    in_specs = (
        P("probe", "boxes"),
        P(None, "boxes"),
        P("boxes", None),
        P(None, "boxes"),
        P(None, "boxes"),
        P(),
        P("boxes", None),
    )
    out_specs = P("probe", "boxes")
    return jax.shard_map(body, mesh=mesh, in_specs=in_specs, out_specs=out_specs, check_vma=False)
```

```python
import functools

import jax
import jax.numpy as jnp
from jax import lax
from jax.experimental import pallas as pl
from jax.experimental.pallas import tpu as pltpu
from jax.sharding import PartitionSpec as P

BOXES_DEV = 32
P_SIZE = 256
R = 64
W = 3
INNER_DEV = 30


SHARPNESS = 0.05
NUGGET = 1.0
PRECISE = lax.Precision.HIGHEST
MESH = pl.DeviceIdType.MESH


def halo_kernel(to_right, to_left, from_left, from_right, left_slot, right_slot, send_sems, recv_sems):
    me = lax.axis_index("boxes")
    size = lax.axis_size("boxes")
    probe = lax.axis_index("probe")
    right = lax.rem(me + 1, size)
    left = lax.rem(me + size - 1, size)
    barrier = pltpu.get_barrier_semaphore()
    for neighbour in (left, right):
        pl.semaphore_signal(barrier, inc=1, device_id=(neighbour, probe), device_id_type=MESH)
    pl.semaphore_wait(barrier, 2)
    rightward = pltpu.make_async_remote_copy(
        src_ref=to_right,
        dst_ref=left_slot,
        send_sem=send_sems.at[0],
        recv_sem=recv_sems.at[0],
        device_id=(right, probe),
        device_id_type=MESH,
    )
    leftward = pltpu.make_async_remote_copy(
        src_ref=to_left,
        dst_ref=right_slot,
        send_sem=send_sems.at[1],
        recv_sem=recv_sems.at[1],
        device_id=(left, probe),
        device_id_type=MESH,
    )
    rightward.start()
    leftward.start()
    rightward.wait()
    leftward.wait()
    from_left[...] = left_slot[...]
    from_right[...] = right_slot[...]


def exchange_halo(to_right, to_left):
    shape = jax.ShapeDtypeStruct(to_right.shape, to_right.dtype)
    vmem = pl.BlockSpec(memory_space=pltpu.VMEM)
    return pl.pallas_call(
        halo_kernel,
        out_shape=(shape, shape),
        in_specs=[vmem, vmem],
        out_specs=(vmem, vmem),
        scratch_shapes=[
            pltpu.VMEM(to_right.shape, to_right.dtype),
            pltpu.VMEM(to_right.shape, to_right.dtype),
            pltpu.SemaphoreType.DMA((2,)),
            pltpu.SemaphoreType.DMA((2,)),
        ],
        compiler_params=pltpu.CompilerParams(collective_id=0, has_side_effects=True),
    )(to_right, to_left)

def kernel_matrix(left_points, right_points, kernel_scale):
    distance_sq = (left_points[0][..., :, None] - right_points[0][..., None, :]) ** 2
    distance_sq = distance_sq + (left_points[1][..., :, None] - right_points[1][..., None, :]) ** 2
    distance_sq = distance_sq + (left_points[2][..., :, None] - right_points[2][..., None, :]) ** 2
    return 1.0 / (1.0 + kernel_scale * distance_sq)


def interpolation(left_points, right_points, kernel_scale):
    values = kernel_matrix(left_points, right_points, kernel_scale)
    return values / jnp.sum(values, axis=-1, keepdims=True)


def near_kernel(kernel_scale, slots, source_ref, probes_ref, coords_ref, target_ref, out_ref):
    box = pl.program_id(0)
    target_x = target_ref[0:1, :]
    target_y = target_ref[1:2, :]
    target_z = target_ref[2:3, :]
    out_ref[...] = jnp.zeros_like(out_ref)
    for slot in range(slots):
        source = source_ref[box * slots + slot]

        @pl.when(source >= 0)
        def _():
            near = coords_ref[source]
            distance_sq = (near[:, 0:1] - target_x) ** 2
            distance_sq = distance_sq + (near[:, 1:2] - target_y) ** 2
            distance_sq = distance_sq + (near[:, 2:3] - target_z) ** 2
            kernel_block = 1.0 / (1.0 + kernel_scale * distance_sq)
            out_ref[...] += jnp.dot(
                probes_ref[source], kernel_block, precision=PRECISE,
                preferred_element_type=jnp.float32,
            )


def near_field_call(slot_source, probe_tiles, coord_tiles, points, kernel_scale):
    tiles, rows, size = probe_tiles.shape
    boxes = points.shape[1] // size
    slots = slot_source.shape[0] // boxes
    return pl.pallas_call(
        functools.partial(near_kernel, kernel_scale, slots),
        out_shape=jax.ShapeDtypeStruct((rows, boxes * size), jnp.float32),
        grid_spec=pltpu.PrefetchScalarGridSpec(
            num_scalar_prefetch=1,
            grid=(boxes,),
            in_specs=[
                pl.BlockSpec((tiles, rows, size), lambda b, s: (0, 0, 0)),
                pl.BlockSpec((tiles, size, 3), lambda b, s: (0, 0, 0)),
                pl.BlockSpec((3, size), lambda b, s: (0, b)),
            ],
            out_specs=pl.BlockSpec((rows, size), lambda b, s: (0, b)),
        ),
        compiler_params=pltpu.CompilerParams(dimension_semantics=("arbitrary",)),
        cost_estimate=pl.CostEstimate(
            flops=boxes * slots * size * size * (2 * rows + 12),
            transcendentals=0,
            bytes_accessed=4 * (probe_tiles.size + coord_tiles.size * 43 + 2 * rows * boxes * size),
        ),
    )(slot_source, probe_tiles, coord_tiles, points)


def body(probes, points, near_list, leaf_proxy, inner_proxy, top_proxy, far_list):
    groups = lax.axis_size("boxes")
    device = lax.axis_index("boxes")
    boxes_all = BOXES_DEV * groups
    kernel_scale = SHARPNESS * boxes_all
    rows_here = probes.shape[0]
    local_depth = BOXES_DEV.bit_length() - 1
    tree_depth = groups.bit_length() - 1
    live_slot = near_list >= 0
    slot_weight = live_slot.astype(jnp.float32)
    where_in = jnp.where(live_slot, (near_list - device * BOXES_DEV + W + boxes_all) % boxes_all, 0)
    box_points = points.reshape(3, BOXES_DEV, P_SIZE)
    probe_tiles = probes.reshape(rows_here, BOXES_DEV, P_SIZE)
    leaf_points = leaf_proxy.reshape(3, BOXES_DEV, R)
    leaf_basis = interpolation(box_points, leaf_points, kernel_scale)
    inner_points = inner_proxy.reshape(3, INNER_DEV, R)
    top_points = top_proxy.reshape(3, top_proxy.shape[1] // R, R)

    def node_proxy(height, node_index):
        offset = 2 * groups - 2 * (groups >> height)
        return lax.dynamic_slice_in_dim(top_points, offset + node_index, 1, 1)

    proxies = [leaf_points]
    for height in range(1, local_depth):
        offset = BOXES_DEV - (BOXES_DEV >> height - 1)
        number = BOXES_DEV >> height
        proxies.append(inner_points[:, offset : offset + number, :])
    proxies.append(node_proxy(0, device))
    level_moments = [jnp.einsum("qbp,bpr->qbr", probe_tiles, leaf_basis, precision=PRECISE)]
    transfer_maps = []
    for height in range(local_depth):
        interp_map = interpolation(
            proxies[height], jnp.repeat(proxies[height + 1], 2, axis=1), kernel_scale
        )
        transfer_maps.append(interp_map)
        lifted = jnp.einsum("qnr,nrs->qns", level_moments[-1], interp_map, precision=PRECISE)
        level_moments.append(lifted.reshape(rows_here, -1, 2, R).sum(axis=2))
    pyramid = jnp.concatenate(
        [
            jnp.concatenate(level_moments[:local_depth], axis=1),
            jnp.concatenate([leaf_points, inner_points], axis=1),
        ],
        axis=0,
    )
    pyramid_nodes = pyramid.shape[1]
    stacked = jnp.concatenate([probes, points], axis=0)
    width = W * P_SIZE
    flat_pyramid = pyramid.reshape(rows_here + 3, -1)
    from_left, from_right = exchange_halo(
        jnp.concatenate([stacked[:, -width:], flat_pyramid], axis=1),
        jnp.concatenate([stacked[:, :width], flat_pyramid], axis=1),
    )
    extended = jnp.concatenate([from_left[:, :width], stacked, from_right[:, :width]], axis=1)
    extended = extended.reshape(rows_here + 3, BOXES_DEV + 2 * W, P_SIZE)
    spread = jnp.concatenate(
        [
            from_left[:, width:].reshape(pyramid.shape),
            pyramid,
            from_right[:, width:].reshape(pyramid.shape),
        ],
        axis=1,
    )
    slot_source = jnp.where(live_slot, jnp.clip(where_in, 0, BOXES_DEV + 2 * W - 1), -1)
    near_field = near_field_call(
        slot_source.reshape(-1).astype(jnp.int32),
        jnp.moveaxis(extended[:rows_here], 1, 0),
        jnp.moveaxis(extended[rows_here:], 0, 2),
        points,
        kernel_scale,
    )
    index_parts, target_parts, mask_parts = [], [], []
    for height in range(local_depth):
        count = BOXES_DEV >> height
        start = 0 if height == 0 else 2 * BOXES_DEV - (BOXES_DEV >> height - 1)
        if height == 0:
            live_far = far_list >= 0
            view_ids = [
                jnp.where(
                    live_far[:, slot],
                    (far_list[:, slot] - device * BOXES_DEV + BOXES_DEV + boxes_all) % boxes_all,
                    0,
                )
                for slot in range(3)
            ]
            mask_parts += [live_far[:, slot].astype(jnp.float32) for slot in range(3)]
        else:
            node = jnp.arange(count, dtype=jnp.int32)
            third = jnp.where(node % 2 == 0, node + 3, node - 3)
            view_ids = [node - 2 + count, node + 2 + count, third + count]
            mask_parts += [jnp.ones((count,), jnp.float32)] * 3
        for view_id in view_ids:
            index_parts.append(view_id // count * pyramid_nodes + start + view_id % count)
            target_parts.append(proxies[height])
    picked = jnp.take(spread, jnp.concatenate(index_parts), axis=1)
    kernel_block = kernel_matrix(picked[rows_here:], jnp.concatenate(target_parts, axis=1), kernel_scale)
    source_moment = picked[:rows_here] * jnp.concatenate(mask_parts)[None, :, None]
    contributions = jnp.einsum("qnr,nrs->qns", source_moment, kernel_block, precision=PRECISE)
    local_couplings = []
    first = 0
    for height in range(local_depth):
        count = BOXES_DEV >> height
        part = contributions[:, first : first + 3 * count, :]
        local_couplings.append(part.reshape(rows_here, 3, count, R).sum(axis=1))
        first += 3 * count

    top_levels = tree_depth - 1
    level_points = []
    for height in range(top_levels):
        offset = 2 * groups - 2 * (groups >> height)
        level_points.append(top_points[:, offset : offset + (groups >> height), :])
    own_edges = []
    for height in range(top_levels - 1):
        own_edges.append(
            interpolation(
                lax.dynamic_slice_in_dim(level_points[height], device // 2**height, 1, 1),
                lax.dynamic_slice_in_dim(level_points[height + 1], device // 2 ** (height + 1), 1, 1),
                kernel_scale,
            )
        )
    path_moments = [level_moments[local_depth]]
    for height in range(top_levels - 1):
        path_moments.append(
            jnp.einsum("qnr,nrs->qns", path_moments[-1], own_edges[height], precision=PRECISE)
        )
    gathered = lax.all_gather(jnp.concatenate(path_moments, axis=1), "boxes", axis=0)
    top_moments, top_sources, top_targets, top_slots = [], [], [], []
    for height in range(top_levels):
        number = groups >> height
        node = device // 2**height
        level_sums = gathered[:, :, height, :].reshape(number, 2**height, rows_here, R).sum(axis=1)
        third = jnp.where(node % 2 == 0, node + 3, node - 3) % number
        if number > 4:
            source_ids = [(node - 2) % number, (node + 2) % number, third]
        else:
            source_ids = [(node + 2) % number]
        top_slots.append(len(source_ids))
        for source in source_ids:
            top_moments.append(lax.dynamic_index_in_dim(level_sums, source, 0, keepdims=True))
            top_sources.append(lax.dynamic_slice_in_dim(level_points[height], source, 1, 1))
            top_targets.append(lax.dynamic_slice_in_dim(level_points[height], node, 1, 1))
    kernel_block = kernel_matrix(
        jnp.concatenate(top_sources, axis=1), jnp.concatenate(top_targets, axis=1), kernel_scale
    )
    contributions = jnp.einsum(
        "nqr,nrs->qns", jnp.concatenate(top_moments, axis=0), kernel_block, precision=PRECISE
    )
    top_couplings = []
    first = 0
    for slots in top_slots:
        top_couplings.append(contributions[:, first : first + slots, :].sum(axis=1, keepdims=True))
        first += slots
    descent = top_couplings[-1]
    for height in range(top_levels - 2, -1, -1):
        descent = (
            jnp.einsum("qns,nrs->qnr", descent, own_edges[height], precision=PRECISE)
            + top_couplings[height]
        )
    for height in range(local_depth - 1, -1, -1):
        descent = jnp.einsum(
            "qns,nrs->qnr", jnp.repeat(descent, 2, axis=1), transfer_maps[height], precision=PRECISE
        )
        descent = descent + local_couplings[height]
    far_field = jnp.einsum("qbr,bpr->qbp", descent, leaf_basis, precision=PRECISE).reshape(
        rows_here, BOXES_DEV * P_SIZE
    )
    return near_field + far_field + NUGGET * probes


def solution(mesh):
    in_specs = (
        P("probe", "boxes"),
        P(None, "boxes"),
        P("boxes", None),
        P(None, "boxes"),
        P(None, "boxes"),
        P(),
        P("boxes", None),
    )
    out_specs = P("probe", "boxes")
    return jax.shard_map(body, mesh=mesh, in_specs=in_specs, out_specs=out_specs, check_vma=False)
```

```python
import functools

import jax
import jax.numpy as jnp
from jax import lax
from jax.experimental import pallas as pl
from jax.experimental.pallas import tpu as pltpu
from jax.sharding import PartitionSpec as P

BOXES_DEV = 32
P_SIZE = 256
R = 64
W = 3
INNER_DEV = 30


SHARPNESS = 0.05
NUGGET = 1.0
PRECISE = lax.Precision.HIGHEST
MESH = pl.DeviceIdType.MESH


def halo_kernel(to_right, to_left, from_left, from_right, left_slot, right_slot, send_sems, recv_sems):
    me = lax.axis_index("boxes")
    size = lax.axis_size("boxes")
    probe = lax.axis_index("probe")
    right = lax.rem(me + 1, size)
    left = lax.rem(me + size - 1, size)
    barrier = pltpu.get_barrier_semaphore()
    for neighbour in (left, right):
        pl.semaphore_signal(barrier, inc=1, device_id=(neighbour, probe), device_id_type=MESH)
    pl.semaphore_wait(barrier, 2)
    rightward = pltpu.make_async_remote_copy(
        src_ref=to_right,
        dst_ref=left_slot,
        send_sem=send_sems.at[0],
        recv_sem=recv_sems.at[0],
        device_id=(right, probe),
        device_id_type=MESH,
    )
    leftward = pltpu.make_async_remote_copy(
        src_ref=to_left,
        dst_ref=right_slot,
        send_sem=send_sems.at[1],
        recv_sem=recv_sems.at[1],
        device_id=(left, probe),
        device_id_type=MESH,
    )
    rightward.start()
    leftward.start()
    rightward.wait()
    leftward.wait()
    from_left[...] = left_slot[...]
    from_right[...] = right_slot[...]


def exchange_halo(to_right, to_left):
    shape = jax.ShapeDtypeStruct(to_right.shape, to_right.dtype)
    vmem = pl.BlockSpec(memory_space=pltpu.VMEM)
    return pl.pallas_call(
        halo_kernel,
        out_shape=(shape, shape),
        in_specs=[vmem, vmem],
        out_specs=(vmem, vmem),
        scratch_shapes=[
            pltpu.VMEM(to_right.shape, to_right.dtype),
            pltpu.VMEM(to_right.shape, to_right.dtype),
            pltpu.SemaphoreType.DMA((2,)),
            pltpu.SemaphoreType.DMA((2,)),
        ],
        compiler_params=pltpu.CompilerParams(collective_id=0, has_side_effects=True),
    )(to_right, to_left)

def kernel_matrix(left_points, right_points, kernel_scale):
    distance_sq = (left_points[0][..., :, None] - right_points[0][..., None, :]) ** 2
    distance_sq = distance_sq + (left_points[1][..., :, None] - right_points[1][..., None, :]) ** 2
    distance_sq = distance_sq + (left_points[2][..., :, None] - right_points[2][..., None, :]) ** 2
    return 1.0 / (1.0 + kernel_scale * distance_sq)


def interpolation(left_points, right_points, kernel_scale):
    values = kernel_matrix(left_points, right_points, kernel_scale)
    return values / jnp.sum(values, axis=-1, keepdims=True)


def near_kernel(kernel_scale, slots, source_ref, probes_ref, coords_ref, target_ref, out_ref):
    box = pl.program_id(0)
    target_x = target_ref[0:1, :]
    target_y = target_ref[1:2, :]
    target_z = target_ref[2:3, :]
    out_ref[...] = jnp.zeros_like(out_ref)
    for slot in range(slots):
        source = source_ref[box * slots + slot]

        @pl.when(source >= 0)
        def _():
            near = coords_ref[source]
            distance_sq = (near[:, 0:1] - target_x) ** 2
            distance_sq = distance_sq + (near[:, 1:2] - target_y) ** 2
            distance_sq = distance_sq + (near[:, 2:3] - target_z) ** 2
            kernel_block = 1.0 / (1.0 + kernel_scale * distance_sq)
            out_ref[...] += jnp.dot(
                probes_ref[source], kernel_block, precision=lax.Precision.HIGH,
                preferred_element_type=jnp.float32,
            )


def near_field_call(slot_source, probe_tiles, coord_tiles, points, kernel_scale):
    tiles, rows, size = probe_tiles.shape
    boxes = points.shape[1] // size
    slots = slot_source.shape[0] // boxes
    return pl.pallas_call(
        functools.partial(near_kernel, kernel_scale, slots),
        out_shape=jax.ShapeDtypeStruct((rows, boxes * size), jnp.float32),
        grid_spec=pltpu.PrefetchScalarGridSpec(
            num_scalar_prefetch=1,
            grid=(boxes,),
            in_specs=[
                pl.BlockSpec((tiles, rows, size), lambda b, s: (0, 0, 0)),
                pl.BlockSpec((tiles, size, 3), lambda b, s: (0, 0, 0)),
                pl.BlockSpec((3, size), lambda b, s: (0, b)),
            ],
            out_specs=pl.BlockSpec((rows, size), lambda b, s: (0, b)),
        ),
        compiler_params=pltpu.CompilerParams(dimension_semantics=("arbitrary",)),
        cost_estimate=pl.CostEstimate(
            flops=boxes * slots * size * size * (2 * rows + 12),
            transcendentals=0,
            bytes_accessed=4 * (probe_tiles.size + coord_tiles.size * 43 + 2 * rows * boxes * size),
        ),
    )(slot_source, probe_tiles, coord_tiles, points)


def body(probes, points, near_list, leaf_proxy, inner_proxy, top_proxy, far_list):
    groups = lax.axis_size("boxes")
    device = lax.axis_index("boxes")
    boxes_all = BOXES_DEV * groups
    kernel_scale = SHARPNESS * boxes_all
    rows_here = probes.shape[0]
    local_depth = BOXES_DEV.bit_length() - 1
    tree_depth = groups.bit_length() - 1
    live_slot = near_list >= 0
    slot_weight = live_slot.astype(jnp.float32)
    where_in = jnp.where(live_slot, (near_list - device * BOXES_DEV + W + boxes_all) % boxes_all, 0)
    box_points = points.reshape(3, BOXES_DEV, P_SIZE)
    probe_tiles = probes.reshape(rows_here, BOXES_DEV, P_SIZE)
    leaf_points = leaf_proxy.reshape(3, BOXES_DEV, R)
    leaf_basis = interpolation(box_points, leaf_points, kernel_scale)
    inner_points = inner_proxy.reshape(3, INNER_DEV, R)
    top_points = top_proxy.reshape(3, top_proxy.shape[1] // R, R)

    def node_proxy(height, node_index):
        offset = 2 * groups - 2 * (groups >> height)
        return lax.dynamic_slice_in_dim(top_points, offset + node_index, 1, 1)

    proxies = [leaf_points]
    for height in range(1, local_depth):
        offset = BOXES_DEV - (BOXES_DEV >> height - 1)
        number = BOXES_DEV >> height
        proxies.append(inner_points[:, offset : offset + number, :])
    proxies.append(node_proxy(0, device))
    level_moments = [jnp.einsum("qbp,bpr->qbr", probe_tiles, leaf_basis, precision=PRECISE)]
    transfer_maps = []
    for height in range(local_depth):
        interp_map = interpolation(
            proxies[height], jnp.repeat(proxies[height + 1], 2, axis=1), kernel_scale
        )
        transfer_maps.append(interp_map)
        lifted = jnp.einsum("qnr,nrs->qns", level_moments[-1], interp_map, precision=PRECISE)
        level_moments.append(lifted.reshape(rows_here, -1, 2, R).sum(axis=2))
    pyramid = jnp.concatenate(
        [
            jnp.concatenate(level_moments[:local_depth], axis=1),
            jnp.concatenate([leaf_points, inner_points], axis=1),
        ],
        axis=0,
    )
    pyramid_nodes = pyramid.shape[1]
    stacked = jnp.concatenate([probes, points], axis=0)
    width = W * P_SIZE
    flat_pyramid = pyramid.reshape(rows_here + 3, -1)
    from_left, from_right = exchange_halo(
        jnp.concatenate([stacked[:, -width:], flat_pyramid], axis=1),
        jnp.concatenate([stacked[:, :width], flat_pyramid], axis=1),
    )
    extended = jnp.concatenate([from_left[:, :width], stacked, from_right[:, :width]], axis=1)
    extended = extended.reshape(rows_here + 3, BOXES_DEV + 2 * W, P_SIZE)
    spread = jnp.concatenate(
        [
            from_left[:, width:].reshape(pyramid.shape),
            pyramid,
            from_right[:, width:].reshape(pyramid.shape),
        ],
        axis=1,
    )
    slot_source = jnp.where(live_slot, jnp.clip(where_in, 0, BOXES_DEV + 2 * W - 1), -1)
    near_field = near_field_call(
        slot_source.reshape(-1).astype(jnp.int32),
        jnp.moveaxis(extended[:rows_here], 1, 0),
        jnp.moveaxis(extended[rows_here:], 0, 2),
        points,
        kernel_scale,
    )
    index_parts, target_parts, mask_parts = [], [], []
    for height in range(local_depth):
        count = BOXES_DEV >> height
        start = 0 if height == 0 else 2 * BOXES_DEV - (BOXES_DEV >> height - 1)
        if height == 0:
            live_far = far_list >= 0
            view_ids = [
                jnp.where(
                    live_far[:, slot],
                    (far_list[:, slot] - device * BOXES_DEV + BOXES_DEV + boxes_all) % boxes_all,
                    0,
                )
                for slot in range(3)
            ]
            mask_parts += [live_far[:, slot].astype(jnp.float32) for slot in range(3)]
        else:
            node = jnp.arange(count, dtype=jnp.int32)
            third = jnp.where(node % 2 == 0, node + 3, node - 3)
            view_ids = [node - 2 + count, node + 2 + count, third + count]
            mask_parts += [jnp.ones((count,), jnp.float32)] * 3
        for view_id in view_ids:
            index_parts.append(view_id // count * pyramid_nodes + start + view_id % count)
            target_parts.append(proxies[height])
    picked = jnp.take(spread, jnp.concatenate(index_parts), axis=1)
    kernel_block = kernel_matrix(picked[rows_here:], jnp.concatenate(target_parts, axis=1), kernel_scale)
    source_moment = picked[:rows_here] * jnp.concatenate(mask_parts)[None, :, None]
    contributions = jnp.einsum("qnr,nrs->qns", source_moment, kernel_block, precision=PRECISE)
    local_couplings = []
    first = 0
    for height in range(local_depth):
        count = BOXES_DEV >> height
        part = contributions[:, first : first + 3 * count, :]
        local_couplings.append(part.reshape(rows_here, 3, count, R).sum(axis=1))
        first += 3 * count

    top_levels = tree_depth - 1
    level_points = []
    for height in range(top_levels):
        offset = 2 * groups - 2 * (groups >> height)
        level_points.append(top_points[:, offset : offset + (groups >> height), :])
    own_edges = []
    for height in range(top_levels - 1):
        own_edges.append(
            interpolation(
                lax.dynamic_slice_in_dim(level_points[height], device // 2**height, 1, 1),
                lax.dynamic_slice_in_dim(level_points[height + 1], device // 2 ** (height + 1), 1, 1),
                kernel_scale,
            )
        )
    path_moments = [level_moments[local_depth]]
    for height in range(top_levels - 1):
        path_moments.append(
            jnp.einsum("qnr,nrs->qns", path_moments[-1], own_edges[height], precision=PRECISE)
        )
    gathered = lax.all_gather(jnp.concatenate(path_moments, axis=1), "boxes", axis=0)
    top_moments, top_sources, top_targets, top_slots = [], [], [], []
    for height in range(top_levels):
        number = groups >> height
        node = device // 2**height
        level_sums = gathered[:, :, height, :].reshape(number, 2**height, rows_here, R).sum(axis=1)
        third = jnp.where(node % 2 == 0, node + 3, node - 3) % number
        if number > 4:
            source_ids = [(node - 2) % number, (node + 2) % number, third]
        else:
            source_ids = [(node + 2) % number]
        top_slots.append(len(source_ids))
        for source in source_ids:
            top_moments.append(lax.dynamic_index_in_dim(level_sums, source, 0, keepdims=True))
            top_sources.append(lax.dynamic_slice_in_dim(level_points[height], source, 1, 1))
            top_targets.append(lax.dynamic_slice_in_dim(level_points[height], node, 1, 1))
    kernel_block = kernel_matrix(
        jnp.concatenate(top_sources, axis=1), jnp.concatenate(top_targets, axis=1), kernel_scale
    )
    contributions = jnp.einsum(
        "nqr,nrs->qns", jnp.concatenate(top_moments, axis=0), kernel_block, precision=PRECISE
    )
    top_couplings = []
    first = 0
    for slots in top_slots:
        top_couplings.append(contributions[:, first : first + slots, :].sum(axis=1, keepdims=True))
        first += slots
    descent = top_couplings[-1]
    for height in range(top_levels - 2, -1, -1):
        descent = (
            jnp.einsum("qns,nrs->qnr", descent, own_edges[height], precision=PRECISE)
            + top_couplings[height]
        )
    for height in range(local_depth - 1, -1, -1):
        descent = jnp.einsum(
            "qns,nrs->qnr", jnp.repeat(descent, 2, axis=1), transfer_maps[height], precision=PRECISE
        )
        descent = descent + local_couplings[height]
    far_field = jnp.einsum("qbr,bpr->qbp", descent, leaf_basis, precision=PRECISE).reshape(
        rows_here, BOXES_DEV * P_SIZE
    )
    return near_field + far_field + NUGGET * probes


def solution(mesh):
    in_specs = (
        P("probe", "boxes"),
        P(None, "boxes"),
        P("boxes", None),
        P(None, "boxes"),
        P(None, "boxes"),
        P(),
        P("boxes", None),
    )
    out_specs = P("probe", "boxes")
    return jax.shard_map(body, mesh=mesh, in_specs=in_specs, out_specs=out_specs, check_vma=False)
```

```python
import functools

import jax
import jax.numpy as jnp
from jax import lax
from jax.experimental import pallas as pl
from jax.experimental.pallas import tpu as pltpu
from jax.sharding import PartitionSpec as P

BOXES_DEV = 32
P_SIZE = 256
R = 64
W = 3
INNER_DEV = 30


SHARPNESS = 0.05
NUGGET = 1.0
PRECISE = lax.Precision.HIGHEST
MESH = pl.DeviceIdType.MESH


def halo_kernel(to_right, to_left, from_left, from_right, left_slot, right_slot, send_sems, recv_sems):
    me = lax.axis_index("boxes")
    size = lax.axis_size("boxes")
    probe = lax.axis_index("probe")
    right = lax.rem(me + 1, size)
    left = lax.rem(me + size - 1, size)
    barrier = pltpu.get_barrier_semaphore()
    for neighbour in (left, right):
        pl.semaphore_signal(barrier, inc=1, device_id=(neighbour, probe), device_id_type=MESH)
    pl.semaphore_wait(barrier, 2)
    rightward = pltpu.make_async_remote_copy(
        src_ref=to_right,
        dst_ref=left_slot,
        send_sem=send_sems.at[0],
        recv_sem=recv_sems.at[0],
        device_id=(right, probe),
        device_id_type=MESH,
    )
    leftward = pltpu.make_async_remote_copy(
        src_ref=to_left,
        dst_ref=right_slot,
        send_sem=send_sems.at[1],
        recv_sem=recv_sems.at[1],
        device_id=(left, probe),
        device_id_type=MESH,
    )
    rightward.start()
    leftward.start()
    rightward.wait()
    leftward.wait()
    from_left[...] = left_slot[...]
    from_right[...] = right_slot[...]


def exchange_halo(to_right, to_left):
    shape = jax.ShapeDtypeStruct(to_right.shape, to_right.dtype)
    vmem = pl.BlockSpec(memory_space=pltpu.VMEM)
    return pl.pallas_call(
        halo_kernel,
        out_shape=(shape, shape),
        in_specs=[vmem, vmem],
        out_specs=(vmem, vmem),
        scratch_shapes=[
            pltpu.VMEM(to_right.shape, to_right.dtype),
            pltpu.VMEM(to_right.shape, to_right.dtype),
            pltpu.SemaphoreType.DMA((2,)),
            pltpu.SemaphoreType.DMA((2,)),
        ],
        compiler_params=pltpu.CompilerParams(collective_id=0, has_side_effects=True),
    )(to_right, to_left)

def kernel_matrix(left_points, right_points, kernel_scale):
    distance_sq = (left_points[0][..., :, None] - right_points[0][..., None, :]) ** 2
    distance_sq = distance_sq + (left_points[1][..., :, None] - right_points[1][..., None, :]) ** 2
    distance_sq = distance_sq + (left_points[2][..., :, None] - right_points[2][..., None, :]) ** 2
    return 1.0 / (1.0 + kernel_scale * distance_sq)


def interpolation(left_points, right_points, kernel_scale):
    values = kernel_matrix(left_points, right_points, kernel_scale)
    return values / jnp.sum(values, axis=-1, keepdims=True)


def near_kernel(kernel_scale, slots, source_ref, probes_ref, coords_ref, target_ref, shift_ref,
                shift_col_ref, out_ref):
    box = pl.program_id(0)
    target = target_ref[...] - shift_col_ref[0]
    target_term = kernel_scale * jnp.sum(target * target, axis=0, keepdims=True)
    target_cross = (-2.0 * kernel_scale) * target
    out_ref[...] = jnp.zeros_like(out_ref)
    for slot in range(slots):
        source = source_ref[box * slots + slot]

        @pl.when(source >= 0)
        def _():
            near = coords_ref[source] - shift_ref[0]
            near_term = 1.0 + kernel_scale * jnp.sum(near * near, axis=1, keepdims=True)
            cross = jnp.dot(
                near, target_cross, precision=PRECISE, preferred_element_type=jnp.float32
            )
            kernel_block = 1.0 / ((cross + near_term) + target_term)
            out_ref[...] += jnp.dot(
                probes_ref[source], kernel_block, precision=lax.Precision.HIGH,
                preferred_element_type=jnp.float32,
            )


def near_field_call(slot_source, probe_tiles, coord_tiles, points, kernel_scale):
    tiles, rows, size = probe_tiles.shape
    boxes = points.shape[1] // size
    slots = slot_source.shape[0] // boxes
    lanes = 8
    coords = jnp.pad(coord_tiles, ((0, 0), (0, 0), (0, lanes - 3)))
    targets = jnp.pad(points, ((0, lanes - 3), (0, 0)))
    shift = jnp.pad(points.reshape(3, boxes, size)[:, :, 0].T, ((0, 0), (0, lanes - 3)))
    return pl.pallas_call(
        functools.partial(near_kernel, kernel_scale, slots),
        out_shape=jax.ShapeDtypeStruct((rows, boxes * size), jnp.float32),
        grid_spec=pltpu.PrefetchScalarGridSpec(
            num_scalar_prefetch=1,
            grid=(boxes,),
            in_specs=[
                pl.BlockSpec((tiles, rows, size), lambda b, s: (0, 0, 0)),
                pl.BlockSpec((tiles, size, lanes), lambda b, s: (0, 0, 0)),
                pl.BlockSpec((lanes, size), lambda b, s: (0, b)),
                pl.BlockSpec((1, 1, lanes), lambda b, s: (b, 0, 0)),
                pl.BlockSpec((1, lanes, 1), lambda b, s: (b, 0, 0)),
            ],
            out_specs=pl.BlockSpec((rows, size), lambda b, s: (0, b)),
        ),
        compiler_params=pltpu.CompilerParams(dimension_semantics=("arbitrary",)),
        cost_estimate=pl.CostEstimate(
            flops=boxes * slots * size * size * (2 * rows + 2 * lanes + 4),
            transcendentals=0,
            bytes_accessed=4 * (probe_tiles.size + coords.size + 2 * rows * boxes * size),
        ),
    )(slot_source, probe_tiles, coords, targets, shift[:, None, :], shift[:, :, None])


def body(probes, points, near_list, leaf_proxy, inner_proxy, top_proxy, far_list):
    groups = lax.axis_size("boxes")
    device = lax.axis_index("boxes")
    boxes_all = BOXES_DEV * groups
    kernel_scale = SHARPNESS * boxes_all
    rows_here = probes.shape[0]
    local_depth = BOXES_DEV.bit_length() - 1
    tree_depth = groups.bit_length() - 1
    live_slot = near_list >= 0
    slot_weight = live_slot.astype(jnp.float32)
    where_in = jnp.where(live_slot, (near_list - device * BOXES_DEV + W + boxes_all) % boxes_all, 0)
    box_points = points.reshape(3, BOXES_DEV, P_SIZE)
    probe_tiles = probes.reshape(rows_here, BOXES_DEV, P_SIZE)
    leaf_points = leaf_proxy.reshape(3, BOXES_DEV, R)
    leaf_basis = interpolation(box_points, leaf_points, kernel_scale)
    inner_points = inner_proxy.reshape(3, INNER_DEV, R)
    top_points = top_proxy.reshape(3, top_proxy.shape[1] // R, R)

    def node_proxy(height, node_index):
        offset = 2 * groups - 2 * (groups >> height)
        return lax.dynamic_slice_in_dim(top_points, offset + node_index, 1, 1)

    proxies = [leaf_points]
    for height in range(1, local_depth):
        offset = BOXES_DEV - (BOXES_DEV >> height - 1)
        number = BOXES_DEV >> height
        proxies.append(inner_points[:, offset : offset + number, :])
    proxies.append(node_proxy(0, device))
    level_moments = [jnp.einsum("qbp,bpr->qbr", probe_tiles, leaf_basis, precision=PRECISE)]
    transfer_maps = []
    for height in range(local_depth):
        interp_map = interpolation(
            proxies[height], jnp.repeat(proxies[height + 1], 2, axis=1), kernel_scale
        )
        transfer_maps.append(interp_map)
        lifted = jnp.einsum("qnr,nrs->qns", level_moments[-1], interp_map, precision=PRECISE)
        level_moments.append(lifted.reshape(rows_here, -1, 2, R).sum(axis=2))
    pyramid = jnp.concatenate(
        [
            jnp.concatenate(level_moments[:local_depth], axis=1),
            jnp.concatenate([leaf_points, inner_points], axis=1),
        ],
        axis=0,
    )
    pyramid_nodes = pyramid.shape[1]
    stacked = jnp.concatenate([probes, points], axis=0)
    width = W * P_SIZE
    flat_pyramid = pyramid.reshape(rows_here + 3, -1)
    from_left, from_right = exchange_halo(
        jnp.concatenate([stacked[:, -width:], flat_pyramid], axis=1),
        jnp.concatenate([stacked[:, :width], flat_pyramid], axis=1),
    )
    extended = jnp.concatenate([from_left[:, :width], stacked, from_right[:, :width]], axis=1)
    extended = extended.reshape(rows_here + 3, BOXES_DEV + 2 * W, P_SIZE)
    spread = jnp.concatenate(
        [
            from_left[:, width:].reshape(pyramid.shape),
            pyramid,
            from_right[:, width:].reshape(pyramid.shape),
        ],
        axis=1,
    )
    slot_source = jnp.where(live_slot, jnp.clip(where_in, 0, BOXES_DEV + 2 * W - 1), -1)
    near_field = near_field_call(
        slot_source.reshape(-1).astype(jnp.int32),
        jnp.moveaxis(extended[:rows_here], 1, 0),
        jnp.moveaxis(extended[rows_here:], 0, 2),
        points,
        kernel_scale,
    )
    index_parts, target_parts, mask_parts = [], [], []
    for height in range(local_depth):
        count = BOXES_DEV >> height
        start = 0 if height == 0 else 2 * BOXES_DEV - (BOXES_DEV >> height - 1)
        if height == 0:
            live_far = far_list >= 0
            view_ids = [
                jnp.where(
                    live_far[:, slot],
                    (far_list[:, slot] - device * BOXES_DEV + BOXES_DEV + boxes_all) % boxes_all,
                    0,
                )
                for slot in range(3)
            ]
            mask_parts += [live_far[:, slot].astype(jnp.float32) for slot in range(3)]
        else:
            node = jnp.arange(count, dtype=jnp.int32)
            third = jnp.where(node % 2 == 0, node + 3, node - 3)
            view_ids = [node - 2 + count, node + 2 + count, third + count]
            mask_parts += [jnp.ones((count,), jnp.float32)] * 3
        for view_id in view_ids:
            index_parts.append(view_id // count * pyramid_nodes + start + view_id % count)
            target_parts.append(proxies[height])
    picked = jnp.take(spread, jnp.concatenate(index_parts), axis=1)
    kernel_block = kernel_matrix(picked[rows_here:], jnp.concatenate(target_parts, axis=1), kernel_scale)
    source_moment = picked[:rows_here] * jnp.concatenate(mask_parts)[None, :, None]
    contributions = jnp.einsum("qnr,nrs->qns", source_moment, kernel_block, precision=PRECISE)
    local_couplings = []
    first = 0
    for height in range(local_depth):
        count = BOXES_DEV >> height
        part = contributions[:, first : first + 3 * count, :]
        local_couplings.append(part.reshape(rows_here, 3, count, R).sum(axis=1))
        first += 3 * count

    top_levels = tree_depth - 1
    level_points = []
    for height in range(top_levels):
        offset = 2 * groups - 2 * (groups >> height)
        level_points.append(top_points[:, offset : offset + (groups >> height), :])
    own_edges = []
    for height in range(top_levels - 1):
        own_edges.append(
            interpolation(
                lax.dynamic_slice_in_dim(level_points[height], device // 2**height, 1, 1),
                lax.dynamic_slice_in_dim(level_points[height + 1], device // 2 ** (height + 1), 1, 1),
                kernel_scale,
            )
        )
    path_moments = [level_moments[local_depth]]
    for height in range(top_levels - 1):
        path_moments.append(
            jnp.einsum("qnr,nrs->qns", path_moments[-1], own_edges[height], precision=PRECISE)
        )
    gathered = lax.all_gather(jnp.concatenate(path_moments, axis=1), "boxes", axis=0)
    top_moments, top_sources, top_targets, top_slots = [], [], [], []
    for height in range(top_levels):
        number = groups >> height
        node = device // 2**height
        level_sums = gathered[:, :, height, :].reshape(number, 2**height, rows_here, R).sum(axis=1)
        third = jnp.where(node % 2 == 0, node + 3, node - 3) % number
        if number > 4:
            source_ids = [(node - 2) % number, (node + 2) % number, third]
        else:
            source_ids = [(node + 2) % number]
        top_slots.append(len(source_ids))
        for source in source_ids:
            top_moments.append(lax.dynamic_index_in_dim(level_sums, source, 0, keepdims=True))
            top_sources.append(lax.dynamic_slice_in_dim(level_points[height], source, 1, 1))
            top_targets.append(lax.dynamic_slice_in_dim(level_points[height], node, 1, 1))
    kernel_block = kernel_matrix(
        jnp.concatenate(top_sources, axis=1), jnp.concatenate(top_targets, axis=1), kernel_scale
    )
    contributions = jnp.einsum(
        "nqr,nrs->qns", jnp.concatenate(top_moments, axis=0), kernel_block, precision=PRECISE
    )
    top_couplings = []
    first = 0
    for slots in top_slots:
        top_couplings.append(contributions[:, first : first + slots, :].sum(axis=1, keepdims=True))
        first += slots
    descent = top_couplings[-1]
    for height in range(top_levels - 2, -1, -1):
        descent = (
            jnp.einsum("qns,nrs->qnr", descent, own_edges[height], precision=PRECISE)
            + top_couplings[height]
        )
    for height in range(local_depth - 1, -1, -1):
        descent = jnp.einsum(
            "qns,nrs->qnr", jnp.repeat(descent, 2, axis=1), transfer_maps[height], precision=PRECISE
        )
        descent = descent + local_couplings[height]
    far_field = jnp.einsum("qbr,bpr->qbp", descent, leaf_basis, precision=PRECISE).reshape(
        rows_here, BOXES_DEV * P_SIZE
    )
    return near_field + far_field + NUGGET * probes


def solution(mesh):
    in_specs = (
        P("probe", "boxes"),
        P(None, "boxes"),
        P("boxes", None),
        P(None, "boxes"),
        P(None, "boxes"),
        P(),
        P("boxes", None),
    )
    out_specs = P("probe", "boxes")
    return jax.shard_map(body, mesh=mesh, in_specs=in_specs, out_specs=out_specs, check_vma=False)
```

```python
import functools

import jax
import jax.numpy as jnp
from jax import lax
from jax.experimental import pallas as pl
from jax.experimental.pallas import tpu as pltpu
from jax.sharding import PartitionSpec as P

BOXES_DEV = 32
P_SIZE = 256
R = 64
W = 3
INNER_DEV = 30


SHARPNESS = 0.05
NUGGET = 1.0
PRECISE = lax.Precision.HIGHEST
MESH = pl.DeviceIdType.MESH


def halo_kernel(to_right, to_left, from_left, from_right, left_slot, right_slot, send_sems, recv_sems):
    me = lax.axis_index("boxes")
    size = lax.axis_size("boxes")
    probe = lax.axis_index("probe")
    right = lax.rem(me + 1, size)
    left = lax.rem(me + size - 1, size)
    barrier = pltpu.get_barrier_semaphore()
    for neighbour in (left, right):
        pl.semaphore_signal(barrier, inc=1, device_id=(neighbour, probe), device_id_type=MESH)
    pl.semaphore_wait(barrier, 2)
    rightward = pltpu.make_async_remote_copy(
        src_ref=to_right,
        dst_ref=left_slot,
        send_sem=send_sems.at[0],
        recv_sem=recv_sems.at[0],
        device_id=(right, probe),
        device_id_type=MESH,
    )
    leftward = pltpu.make_async_remote_copy(
        src_ref=to_left,
        dst_ref=right_slot,
        send_sem=send_sems.at[1],
        recv_sem=recv_sems.at[1],
        device_id=(left, probe),
        device_id_type=MESH,
    )
    rightward.start()
    leftward.start()
    rightward.wait()
    leftward.wait()
    from_left[...] = left_slot[...]
    from_right[...] = right_slot[...]


def exchange_halo(to_right, to_left):
    shape = jax.ShapeDtypeStruct(to_right.shape, to_right.dtype)
    vmem = pl.BlockSpec(memory_space=pltpu.VMEM)
    return pl.pallas_call(
        halo_kernel,
        out_shape=(shape, shape),
        in_specs=[vmem, vmem],
        out_specs=(vmem, vmem),
        scratch_shapes=[
            pltpu.VMEM(to_right.shape, to_right.dtype),
            pltpu.VMEM(to_right.shape, to_right.dtype),
            pltpu.SemaphoreType.DMA((2,)),
            pltpu.SemaphoreType.DMA((2,)),
        ],
        compiler_params=pltpu.CompilerParams(collective_id=0, has_side_effects=True),
    )(to_right, to_left)

def kernel_matrix(left_points, right_points, kernel_scale):
    distance_sq = (left_points[0][..., :, None] - right_points[0][..., None, :]) ** 2
    distance_sq = distance_sq + (left_points[1][..., :, None] - right_points[1][..., None, :]) ** 2
    distance_sq = distance_sq + (left_points[2][..., :, None] - right_points[2][..., None, :]) ** 2
    return 1.0 / (1.0 + kernel_scale * distance_sq)


def interpolation(left_points, right_points, kernel_scale):
    values = kernel_matrix(left_points, right_points, kernel_scale)
    return values / jnp.sum(values, axis=-1, keepdims=True)


def near_kernel(kernel_scale, slots, source_ref, probes_ref, coords_ref, target_ref, out_ref):
    box = pl.program_id(0)
    size = target_ref.shape[0]
    target_x = jnp.broadcast_to(target_ref[:, 0:1], (size, size))
    target_y = jnp.broadcast_to(target_ref[:, 1:2], (size, size))
    target_z = jnp.broadcast_to(target_ref[:, 2:3], (size, size))
    out_ref[...] = jnp.zeros_like(out_ref)
    for slot in range(slots):
        source = source_ref[box * slots + slot]

        @pl.when(source >= 0)
        def _():
            near = coords_ref[source]
            distance_sq = (near[0:1, :] - target_x) ** 2
            distance_sq = distance_sq + (near[1:2, :] - target_y) ** 2
            distance_sq = distance_sq + (near[2:3, :] - target_z) ** 2
            kernel_block = 1.0 / (1.0 + kernel_scale * distance_sq)
            out_ref[...] += lax.dot_general(
                probes_ref[source], kernel_block, (((1,), (1,)), ((), ())),
                precision=lax.Precision.HIGH, preferred_element_type=jnp.float32,
            )


def near_field_call(slot_source, probe_tiles, coord_tiles, points, kernel_scale):
    tiles, rows, size = probe_tiles.shape
    boxes = points.shape[1] // size
    slots = slot_source.shape[0] // boxes
    return pl.pallas_call(
        functools.partial(near_kernel, kernel_scale, slots),
        out_shape=jax.ShapeDtypeStruct((rows, boxes * size), jnp.float32),
        grid_spec=pltpu.PrefetchScalarGridSpec(
            num_scalar_prefetch=1,
            grid=(boxes,),
            in_specs=[
                pl.BlockSpec((tiles, rows, size), lambda b, s: (0, 0, 0)),
                pl.BlockSpec((tiles, 3, size), lambda b, s: (0, 0, 0)),
                pl.BlockSpec((size, 3), lambda b, s: (b, 0)),
            ],
            out_specs=pl.BlockSpec((rows, size), lambda b, s: (0, b)),
        ),
        compiler_params=pltpu.CompilerParams(dimension_semantics=("arbitrary",)),
        cost_estimate=pl.CostEstimate(
            flops=boxes * slots * size * size * (2 * rows + 12),
            transcendentals=0,
            bytes_accessed=4 * (probe_tiles.size + coord_tiles.size + 2 * rows * boxes * size),
        ),
    )(slot_source, probe_tiles, coord_tiles, points.T)


def body(probes, points, near_list, leaf_proxy, inner_proxy, top_proxy, far_list):
    groups = lax.axis_size("boxes")
    device = lax.axis_index("boxes")
    boxes_all = BOXES_DEV * groups
    kernel_scale = SHARPNESS * boxes_all
    rows_here = probes.shape[0]
    local_depth = BOXES_DEV.bit_length() - 1
    tree_depth = groups.bit_length() - 1
    live_slot = near_list >= 0
    slot_weight = live_slot.astype(jnp.float32)
    where_in = jnp.where(live_slot, (near_list - device * BOXES_DEV + W + boxes_all) % boxes_all, 0)
    box_points = points.reshape(3, BOXES_DEV, P_SIZE)
    probe_tiles = probes.reshape(rows_here, BOXES_DEV, P_SIZE)
    leaf_points = leaf_proxy.reshape(3, BOXES_DEV, R)
    leaf_basis = interpolation(box_points, leaf_points, kernel_scale)
    inner_points = inner_proxy.reshape(3, INNER_DEV, R)
    top_points = top_proxy.reshape(3, top_proxy.shape[1] // R, R)

    def node_proxy(height, node_index):
        offset = 2 * groups - 2 * (groups >> height)
        return lax.dynamic_slice_in_dim(top_points, offset + node_index, 1, 1)

    proxies = [leaf_points]
    for height in range(1, local_depth):
        offset = BOXES_DEV - (BOXES_DEV >> height - 1)
        number = BOXES_DEV >> height
        proxies.append(inner_points[:, offset : offset + number, :])
    proxies.append(node_proxy(0, device))
    level_moments = [jnp.einsum("qbp,bpr->qbr", probe_tiles, leaf_basis, precision=PRECISE)]
    transfer_maps = []
    for height in range(local_depth):
        interp_map = interpolation(
            proxies[height], jnp.repeat(proxies[height + 1], 2, axis=1), kernel_scale
        )
        transfer_maps.append(interp_map)
        lifted = jnp.einsum("qnr,nrs->qns", level_moments[-1], interp_map, precision=PRECISE)
        level_moments.append(lifted.reshape(rows_here, -1, 2, R).sum(axis=2))
    pyramid = jnp.concatenate(
        [
            jnp.concatenate(level_moments[:local_depth], axis=1),
            jnp.concatenate([leaf_points, inner_points], axis=1),
        ],
        axis=0,
    )
    pyramid_nodes = pyramid.shape[1]
    stacked = jnp.concatenate([probes, points], axis=0)
    width = W * P_SIZE
    flat_pyramid = pyramid.reshape(rows_here + 3, -1)
    from_left, from_right = exchange_halo(
        jnp.concatenate([stacked[:, -width:], flat_pyramid], axis=1),
        jnp.concatenate([stacked[:, :width], flat_pyramid], axis=1),
    )
    extended = jnp.concatenate([from_left[:, :width], stacked, from_right[:, :width]], axis=1)
    extended = extended.reshape(rows_here + 3, BOXES_DEV + 2 * W, P_SIZE)
    spread = jnp.concatenate(
        [
            from_left[:, width:].reshape(pyramid.shape),
            pyramid,
            from_right[:, width:].reshape(pyramid.shape),
        ],
        axis=1,
    )
    slot_source = jnp.where(live_slot, jnp.clip(where_in, 0, BOXES_DEV + 2 * W - 1), -1)
    near_field = near_field_call(
        slot_source.reshape(-1).astype(jnp.int32),
        jnp.moveaxis(extended[:rows_here], 1, 0),
        jnp.moveaxis(extended[rows_here:], 0, 1),
        points,
        kernel_scale,
    )
    index_parts, target_parts, mask_parts = [], [], []
    for height in range(local_depth):
        count = BOXES_DEV >> height
        start = 0 if height == 0 else 2 * BOXES_DEV - (BOXES_DEV >> height - 1)
        if height == 0:
            live_far = far_list >= 0
            view_ids = [
                jnp.where(
                    live_far[:, slot],
                    (far_list[:, slot] - device * BOXES_DEV + BOXES_DEV + boxes_all) % boxes_all,
                    0,
                )
                for slot in range(3)
            ]
            mask_parts += [live_far[:, slot].astype(jnp.float32) for slot in range(3)]
        else:
            node = jnp.arange(count, dtype=jnp.int32)
            third = jnp.where(node % 2 == 0, node + 3, node - 3)
            view_ids = [node - 2 + count, node + 2 + count, third + count]
            mask_parts += [jnp.ones((count,), jnp.float32)] * 3
        for view_id in view_ids:
            index_parts.append(view_id // count * pyramid_nodes + start + view_id % count)
            target_parts.append(proxies[height])
    picked = jnp.take(spread, jnp.concatenate(index_parts), axis=1)
    kernel_block = kernel_matrix(picked[rows_here:], jnp.concatenate(target_parts, axis=1), kernel_scale)
    source_moment = picked[:rows_here] * jnp.concatenate(mask_parts)[None, :, None]
    contributions = jnp.einsum("qnr,nrs->qns", source_moment, kernel_block, precision=PRECISE)
    local_couplings = []
    first = 0
    for height in range(local_depth):
        count = BOXES_DEV >> height
        part = contributions[:, first : first + 3 * count, :]
        local_couplings.append(part.reshape(rows_here, 3, count, R).sum(axis=1))
        first += 3 * count

    top_levels = tree_depth - 1
    level_points = []
    for height in range(top_levels):
        offset = 2 * groups - 2 * (groups >> height)
        level_points.append(top_points[:, offset : offset + (groups >> height), :])
    own_edges = []
    for height in range(top_levels - 1):
        own_edges.append(
            interpolation(
                lax.dynamic_slice_in_dim(level_points[height], device // 2**height, 1, 1),
                lax.dynamic_slice_in_dim(level_points[height + 1], device // 2 ** (height + 1), 1, 1),
                kernel_scale,
            )
        )
    path_moments = [level_moments[local_depth]]
    for height in range(top_levels - 1):
        path_moments.append(
            jnp.einsum("qnr,nrs->qns", path_moments[-1], own_edges[height], precision=PRECISE)
        )
    gathered = lax.all_gather(jnp.concatenate(path_moments, axis=1), "boxes", axis=0)
    top_moments, top_sources, top_targets, top_slots = [], [], [], []
    for height in range(top_levels):
        number = groups >> height
        node = device // 2**height
        level_sums = gathered[:, :, height, :].reshape(number, 2**height, rows_here, R).sum(axis=1)
        third = jnp.where(node % 2 == 0, node + 3, node - 3) % number
        if number > 4:
            source_ids = [(node - 2) % number, (node + 2) % number, third]
        else:
            source_ids = [(node + 2) % number]
        top_slots.append(len(source_ids))
        for source in source_ids:
            top_moments.append(lax.dynamic_index_in_dim(level_sums, source, 0, keepdims=True))
            top_sources.append(lax.dynamic_slice_in_dim(level_points[height], source, 1, 1))
            top_targets.append(lax.dynamic_slice_in_dim(level_points[height], node, 1, 1))
    kernel_block = kernel_matrix(
        jnp.concatenate(top_sources, axis=1), jnp.concatenate(top_targets, axis=1), kernel_scale
    )
    contributions = jnp.einsum(
        "nqr,nrs->qns", jnp.concatenate(top_moments, axis=0), kernel_block, precision=PRECISE
    )
    top_couplings = []
    first = 0
    for slots in top_slots:
        top_couplings.append(contributions[:, first : first + slots, :].sum(axis=1, keepdims=True))
        first += slots
    descent = top_couplings[-1]
    for height in range(top_levels - 2, -1, -1):
        descent = (
            jnp.einsum("qns,nrs->qnr", descent, own_edges[height], precision=PRECISE)
            + top_couplings[height]
        )
    for height in range(local_depth - 1, -1, -1):
        descent = jnp.einsum(
            "qns,nrs->qnr", jnp.repeat(descent, 2, axis=1), transfer_maps[height], precision=PRECISE
        )
        descent = descent + local_couplings[height]
    far_field = jnp.einsum("qbr,bpr->qbp", descent, leaf_basis, precision=PRECISE).reshape(
        rows_here, BOXES_DEV * P_SIZE
    )
    return near_field + far_field + NUGGET * probes


def solution(mesh):
    in_specs = (
        P("probe", "boxes"),
        P(None, "boxes"),
        P("boxes", None),
        P(None, "boxes"),
        P(None, "boxes"),
        P(),
        P("boxes", None),
    )
    out_specs = P("probe", "boxes")
    return jax.shard_map(body, mesh=mesh, in_specs=in_specs, out_specs=out_specs, check_vma=False)
```

```python
import functools

import jax
import jax.numpy as jnp
from jax import lax
from jax.experimental import pallas as pl
from jax.experimental.pallas import tpu as pltpu
from jax.sharding import PartitionSpec as P

BOXES_DEV = 32
P_SIZE = 256
R = 64
W = 3
INNER_DEV = 30


SHARPNESS = 0.05
NUGGET = 1.0
PRECISE = lax.Precision.HIGHEST
MESH = pl.DeviceIdType.MESH


def halo_kernel(to_right, to_left, from_left, from_right, left_slot, right_slot, send_sems, recv_sems):
    me = lax.axis_index("boxes")
    size = lax.axis_size("boxes")
    probe = lax.axis_index("probe")
    right = lax.rem(me + 1, size)
    left = lax.rem(me + size - 1, size)
    barrier = pltpu.get_barrier_semaphore()
    for neighbour in (left, right):
        pl.semaphore_signal(barrier, inc=1, device_id=(neighbour, probe), device_id_type=MESH)
    pl.semaphore_wait(barrier, 2)
    rightward = pltpu.make_async_remote_copy(
        src_ref=to_right,
        dst_ref=left_slot,
        send_sem=send_sems.at[0],
        recv_sem=recv_sems.at[0],
        device_id=(right, probe),
        device_id_type=MESH,
    )
    leftward = pltpu.make_async_remote_copy(
        src_ref=to_left,
        dst_ref=right_slot,
        send_sem=send_sems.at[1],
        recv_sem=recv_sems.at[1],
        device_id=(left, probe),
        device_id_type=MESH,
    )
    rightward.start()
    leftward.start()
    rightward.wait()
    leftward.wait()
    from_left[...] = left_slot[...]
    from_right[...] = right_slot[...]


def exchange_halo(to_right, to_left):
    shape = jax.ShapeDtypeStruct(to_right.shape, to_right.dtype)
    vmem = pl.BlockSpec(memory_space=pltpu.VMEM)
    return pl.pallas_call(
        halo_kernel,
        out_shape=(shape, shape),
        in_specs=[vmem, vmem],
        out_specs=(vmem, vmem),
        scratch_shapes=[
            pltpu.VMEM(to_right.shape, to_right.dtype),
            pltpu.VMEM(to_right.shape, to_right.dtype),
            pltpu.SemaphoreType.DMA((2,)),
            pltpu.SemaphoreType.DMA((2,)),
        ],
        compiler_params=pltpu.CompilerParams(collective_id=0, has_side_effects=True),
    )(to_right, to_left)

def kernel_matrix(left_points, right_points, kernel_scale):
    distance_sq = (left_points[0][..., :, None] - right_points[0][..., None, :]) ** 2
    distance_sq = distance_sq + (left_points[1][..., :, None] - right_points[1][..., None, :]) ** 2
    distance_sq = distance_sq + (left_points[2][..., :, None] - right_points[2][..., None, :]) ** 2
    return 1.0 / (1.0 + kernel_scale * distance_sq)


def interpolation(left_points, right_points, kernel_scale):
    values = kernel_matrix(left_points, right_points, kernel_scale)
    return values / jnp.sum(values, axis=-1, keepdims=True)


def near_kernel(kernel_scale, slots, source_ref, probes_ref, coords_ref, target_ref, out_ref):
    box = pl.program_id(0)
    size = target_ref.shape[0]
    target_x = jnp.broadcast_to(target_ref[:, 0:1], (size, size))
    target_y = jnp.broadcast_to(target_ref[:, 1:2], (size, size))
    target_z = jnp.broadcast_to(target_ref[:, 2:3], (size, size))
    out_ref[...] = jnp.zeros_like(out_ref)
    for slot in range(slots):
        source = source_ref[box * slots + slot]

        @pl.when(source >= 0)
        def _():
            near = coords_ref[source]
            distance_sq = (near[0:1, :] - target_x) ** 2
            distance_sq = distance_sq + (near[1:2, :] - target_y) ** 2
            distance_sq = distance_sq + (near[2:3, :] - target_z) ** 2
            kernel_block = 1.0 / (1.0 + distance_sq)
            out_ref[...] += lax.dot_general(
                probes_ref[source], kernel_block, (((1,), (1,)), ((), ())),
                precision=lax.Precision.HIGH, preferred_element_type=jnp.float32,
            )


def near_field_call(slot_source, probe_tiles, coord_tiles, points, kernel_scale):
    tiles, rows, size = probe_tiles.shape
    boxes = points.shape[1] // size
    slots = slot_source.shape[0] // boxes
    stretch = kernel_scale**0.5
    return pl.pallas_call(
        functools.partial(near_kernel, kernel_scale, slots),
        out_shape=jax.ShapeDtypeStruct((rows, boxes * size), jnp.float32),
        grid_spec=pltpu.PrefetchScalarGridSpec(
            num_scalar_prefetch=1,
            grid=(boxes,),
            in_specs=[
                pl.BlockSpec((tiles, rows, size), lambda b, s: (0, 0, 0)),
                pl.BlockSpec((tiles, 3, size), lambda b, s: (0, 0, 0)),
                pl.BlockSpec((size, 3), lambda b, s: (b, 0)),
            ],
            out_specs=pl.BlockSpec((rows, size), lambda b, s: (0, b)),
        ),
        compiler_params=pltpu.CompilerParams(dimension_semantics=("arbitrary",)),
        cost_estimate=pl.CostEstimate(
            flops=boxes * slots * size * size * (2 * rows + 12),
            transcendentals=0,
            bytes_accessed=4 * (probe_tiles.size + coord_tiles.size + 2 * rows * boxes * size),
        ),
    )(slot_source, probe_tiles, coord_tiles * stretch, points.T * stretch)


def body(probes, points, near_list, leaf_proxy, inner_proxy, top_proxy, far_list):
    groups = lax.axis_size("boxes")
    device = lax.axis_index("boxes")
    boxes_all = BOXES_DEV * groups
    kernel_scale = SHARPNESS * boxes_all
    rows_here = probes.shape[0]
    local_depth = BOXES_DEV.bit_length() - 1
    tree_depth = groups.bit_length() - 1
    live_slot = near_list >= 0
    slot_weight = live_slot.astype(jnp.float32)
    where_in = jnp.where(live_slot, (near_list - device * BOXES_DEV + W + boxes_all) % boxes_all, 0)
    box_points = points.reshape(3, BOXES_DEV, P_SIZE)
    probe_tiles = probes.reshape(rows_here, BOXES_DEV, P_SIZE)
    leaf_points = leaf_proxy.reshape(3, BOXES_DEV, R)
    leaf_basis = interpolation(box_points, leaf_points, kernel_scale)
    inner_points = inner_proxy.reshape(3, INNER_DEV, R)
    top_points = top_proxy.reshape(3, top_proxy.shape[1] // R, R)

    def node_proxy(height, node_index):
        offset = 2 * groups - 2 * (groups >> height)
        return lax.dynamic_slice_in_dim(top_points, offset + node_index, 1, 1)

    proxies = [leaf_points]
    for height in range(1, local_depth):
        offset = BOXES_DEV - (BOXES_DEV >> height - 1)
        number = BOXES_DEV >> height
        proxies.append(inner_points[:, offset : offset + number, :])
    proxies.append(node_proxy(0, device))
    level_moments = [jnp.einsum("qbp,bpr->qbr", probe_tiles, leaf_basis, precision=PRECISE)]
    transfer_maps = []
    for height in range(local_depth):
        interp_map = interpolation(
            proxies[height], jnp.repeat(proxies[height + 1], 2, axis=1), kernel_scale
        )
        transfer_maps.append(interp_map)
        lifted = jnp.einsum("qnr,nrs->qns", level_moments[-1], interp_map, precision=PRECISE)
        level_moments.append(lifted.reshape(rows_here, -1, 2, R).sum(axis=2))
    pyramid = jnp.concatenate(
        [
            jnp.concatenate(level_moments[:local_depth], axis=1),
            jnp.concatenate([leaf_points, inner_points], axis=1),
        ],
        axis=0,
    )
    pyramid_nodes = pyramid.shape[1]
    stacked = jnp.concatenate([probes, points], axis=0)
    width = W * P_SIZE
    flat_pyramid = pyramid.reshape(rows_here + 3, -1)
    from_left, from_right = exchange_halo(
        jnp.concatenate([stacked[:, -width:], flat_pyramid], axis=1),
        jnp.concatenate([stacked[:, :width], flat_pyramid], axis=1),
    )
    extended = jnp.concatenate([from_left[:, :width], stacked, from_right[:, :width]], axis=1)
    extended = extended.reshape(rows_here + 3, BOXES_DEV + 2 * W, P_SIZE)
    spread = jnp.concatenate(
        [
            from_left[:, width:].reshape(pyramid.shape),
            pyramid,
            from_right[:, width:].reshape(pyramid.shape),
        ],
        axis=1,
    )
    slot_source = jnp.where(live_slot, jnp.clip(where_in, 0, BOXES_DEV + 2 * W - 1), -1)
    near_field = near_field_call(
        slot_source.reshape(-1).astype(jnp.int32),
        jnp.moveaxis(extended[:rows_here], 1, 0),
        jnp.moveaxis(extended[rows_here:], 0, 1),
        points,
        kernel_scale,
    )
    index_parts, target_parts, mask_parts = [], [], []
    for height in range(local_depth):
        count = BOXES_DEV >> height
        start = 0 if height == 0 else 2 * BOXES_DEV - (BOXES_DEV >> height - 1)
        if height == 0:
            live_far = far_list >= 0
            view_ids = [
                jnp.where(
                    live_far[:, slot],
                    (far_list[:, slot] - device * BOXES_DEV + BOXES_DEV + boxes_all) % boxes_all,
                    0,
                )
                for slot in range(3)
            ]
            mask_parts += [live_far[:, slot].astype(jnp.float32) for slot in range(3)]
        else:
            node = jnp.arange(count, dtype=jnp.int32)
            third = jnp.where(node % 2 == 0, node + 3, node - 3)
            view_ids = [node - 2 + count, node + 2 + count, third + count]
            mask_parts += [jnp.ones((count,), jnp.float32)] * 3
        for view_id in view_ids:
            index_parts.append(view_id // count * pyramid_nodes + start + view_id % count)
            target_parts.append(proxies[height])
    picked = jnp.take(spread, jnp.concatenate(index_parts), axis=1)
    kernel_block = kernel_matrix(picked[rows_here:], jnp.concatenate(target_parts, axis=1), kernel_scale)
    source_moment = picked[:rows_here] * jnp.concatenate(mask_parts)[None, :, None]
    contributions = jnp.einsum("qnr,nrs->qns", source_moment, kernel_block, precision=PRECISE)
    local_couplings = []
    first = 0
    for height in range(local_depth):
        count = BOXES_DEV >> height
        part = contributions[:, first : first + 3 * count, :]
        local_couplings.append(part.reshape(rows_here, 3, count, R).sum(axis=1))
        first += 3 * count

    top_levels = tree_depth - 1
    level_points = []
    for height in range(top_levels):
        offset = 2 * groups - 2 * (groups >> height)
        level_points.append(top_points[:, offset : offset + (groups >> height), :])
    own_edges = []
    for height in range(top_levels - 1):
        own_edges.append(
            interpolation(
                lax.dynamic_slice_in_dim(level_points[height], device // 2**height, 1, 1),
                lax.dynamic_slice_in_dim(level_points[height + 1], device // 2 ** (height + 1), 1, 1),
                kernel_scale,
            )
        )
    path_moments = [level_moments[local_depth]]
    for height in range(top_levels - 1):
        path_moments.append(
            jnp.einsum("qnr,nrs->qns", path_moments[-1], own_edges[height], precision=PRECISE)
        )
    gathered = lax.all_gather(jnp.concatenate(path_moments, axis=1), "boxes", axis=0)
    top_moments, top_sources, top_targets, top_slots = [], [], [], []
    for height in range(top_levels):
        number = groups >> height
        node = device // 2**height
        level_sums = gathered[:, :, height, :].reshape(number, 2**height, rows_here, R).sum(axis=1)
        third = jnp.where(node % 2 == 0, node + 3, node - 3) % number
        if number > 4:
            source_ids = [(node - 2) % number, (node + 2) % number, third]
        else:
            source_ids = [(node + 2) % number]
        top_slots.append(len(source_ids))
        for source in source_ids:
            top_moments.append(lax.dynamic_index_in_dim(level_sums, source, 0, keepdims=True))
            top_sources.append(lax.dynamic_slice_in_dim(level_points[height], source, 1, 1))
            top_targets.append(lax.dynamic_slice_in_dim(level_points[height], node, 1, 1))
    kernel_block = kernel_matrix(
        jnp.concatenate(top_sources, axis=1), jnp.concatenate(top_targets, axis=1), kernel_scale
    )
    contributions = jnp.einsum(
        "nqr,nrs->qns", jnp.concatenate(top_moments, axis=0), kernel_block, precision=PRECISE
    )
    top_couplings = []
    first = 0
    for slots in top_slots:
        top_couplings.append(contributions[:, first : first + slots, :].sum(axis=1, keepdims=True))
        first += slots
    descent = top_couplings[-1]
    for height in range(top_levels - 2, -1, -1):
        descent = (
            jnp.einsum("qns,nrs->qnr", descent, own_edges[height], precision=PRECISE)
            + top_couplings[height]
        )
    for height in range(local_depth - 1, -1, -1):
        descent = jnp.einsum(
            "qns,nrs->qnr", jnp.repeat(descent, 2, axis=1), transfer_maps[height], precision=PRECISE
        )
        descent = descent + local_couplings[height]
    far_field = jnp.einsum("qbr,bpr->qbp", descent, leaf_basis, precision=PRECISE).reshape(
        rows_here, BOXES_DEV * P_SIZE
    )
    return near_field + far_field + NUGGET * probes


def solution(mesh):
    in_specs = (
        P("probe", "boxes"),
        P(None, "boxes"),
        P("boxes", None),
        P(None, "boxes"),
        P(None, "boxes"),
        P(),
        P("boxes", None),
    )
    out_specs = P("probe", "boxes")
    return jax.shard_map(body, mesh=mesh, in_specs=in_specs, out_specs=out_specs, check_vma=False)
```

```python
import functools

import jax
import jax.numpy as jnp
from jax import lax
from jax.experimental import pallas as pl
from jax.experimental.pallas import tpu as pltpu
from jax.sharding import PartitionSpec as P

BOXES_DEV = 32
P_SIZE = 256
R = 64
W = 3
INNER_DEV = 30


SHARPNESS = 0.05
NUGGET = 1.0
PRECISE = lax.Precision.HIGHEST
MESH = pl.DeviceIdType.MESH


def halo_kernel(to_right, to_left, from_left, from_right, left_slot, right_slot, send_sems, recv_sems):
    me = lax.axis_index("boxes")
    size = lax.axis_size("boxes")
    probe = lax.axis_index("probe")
    right = lax.rem(me + 1, size)
    left = lax.rem(me + size - 1, size)
    barrier = pltpu.get_barrier_semaphore()
    for neighbour in (left, right):
        pl.semaphore_signal(barrier, inc=1, device_id=(neighbour, probe), device_id_type=MESH)
    pl.semaphore_wait(barrier, 2)
    rightward = pltpu.make_async_remote_copy(
        src_ref=to_right,
        dst_ref=left_slot,
        send_sem=send_sems.at[0],
        recv_sem=recv_sems.at[0],
        device_id=(right, probe),
        device_id_type=MESH,
    )
    leftward = pltpu.make_async_remote_copy(
        src_ref=to_left,
        dst_ref=right_slot,
        send_sem=send_sems.at[1],
        recv_sem=recv_sems.at[1],
        device_id=(left, probe),
        device_id_type=MESH,
    )
    rightward.start()
    leftward.start()
    rightward.wait()
    leftward.wait()
    from_left[...] = left_slot[...]
    from_right[...] = right_slot[...]


def exchange_halo(to_right, to_left):
    shape = jax.ShapeDtypeStruct(to_right.shape, to_right.dtype)
    vmem = pl.BlockSpec(memory_space=pltpu.VMEM)
    return pl.pallas_call(
        halo_kernel,
        out_shape=(shape, shape),
        in_specs=[vmem, vmem],
        out_specs=(vmem, vmem),
        scratch_shapes=[
            pltpu.VMEM(to_right.shape, to_right.dtype),
            pltpu.VMEM(to_right.shape, to_right.dtype),
            pltpu.SemaphoreType.DMA((2,)),
            pltpu.SemaphoreType.DMA((2,)),
        ],
        compiler_params=pltpu.CompilerParams(collective_id=0, has_side_effects=True),
    )(to_right, to_left)

def kernel_matrix(left_points, right_points, kernel_scale):
    distance_sq = (left_points[0][..., :, None] - right_points[0][..., None, :]) ** 2
    distance_sq = distance_sq + (left_points[1][..., :, None] - right_points[1][..., None, :]) ** 2
    distance_sq = distance_sq + (left_points[2][..., :, None] - right_points[2][..., None, :]) ** 2
    return 1.0 / (1.0 + kernel_scale * distance_sq)


def interpolation(left_points, right_points, kernel_scale):
    values = kernel_matrix(left_points, right_points, kernel_scale)
    return values / jnp.sum(values, axis=-1, keepdims=True)


def near_kernel(slots, halo, source_ref, probes_ref, coords_ref, target_ref, out_ref):
    box = pl.program_id(0)
    boxes = pl.num_programs(0)
    size = target_ref.shape[0]
    target_x = jnp.broadcast_to(target_ref[:, 0:1], (size, size))
    target_y = jnp.broadcast_to(target_ref[:, 1:2], (size, size))
    target_z = jnp.broadcast_to(target_ref[:, 2:3], (size, size))
    here = box + halo
    columns = pl.ds(pl.multiple_of(box * size, size), size)

    def block(tile):
        near = coords_ref[tile]
        distance_sq = (near[0:1, :] - target_x) ** 2
        distance_sq = distance_sq + (near[1:2, :] - target_y) ** 2
        distance_sq = distance_sq + (near[2:3, :] - target_z) ** 2
        return 1.0 / (1.0 + distance_sq)

    def gather_into(tile, kernel_block):
        out_ref[:, columns] += lax.dot_general(
            probes_ref[tile], kernel_block, (((1,), (1,)), ((), ())),
            precision=lax.Precision.HIGH, preferred_element_type=jnp.float32,
        )

    @pl.when(box == 0)
    def _():
        out_ref[...] = jnp.zeros_like(out_ref)
        gather_into(here - 1, block(here - 1))

    gather_into(here, block(here))
    pair_block = block(here + 1)
    gather_into(here + 1, pair_block)

    @pl.when(box < boxes - 1)
    def _():
        following = pl.ds(pl.multiple_of((box + 1) * size, size), size)
        out_ref[:, following] += jnp.dot(
            probes_ref[here], pair_block, precision=lax.Precision.HIGH,
            preferred_element_type=jnp.float32,
        )

    for slot in range(slots):
        source = source_ref[box * slots + slot]

        @pl.when((source >= 0) & (source != here - 1) & (source != here) & (source != here + 1))
        def _():
            gather_into(source, block(source))


def near_field_call(slot_source, probe_tiles, coord_tiles, points, kernel_scale):
    tiles, rows, size = probe_tiles.shape
    boxes = points.shape[1] // size
    slots = slot_source.shape[0] // boxes
    stretch = kernel_scale**0.5
    return pl.pallas_call(
        functools.partial(near_kernel, slots, W),
        out_shape=jax.ShapeDtypeStruct((rows, boxes * size), jnp.float32),
        grid_spec=pltpu.PrefetchScalarGridSpec(
            num_scalar_prefetch=1,
            grid=(boxes,),
            in_specs=[
                pl.BlockSpec((tiles, rows, size), lambda b, s: (0, 0, 0)),
                pl.BlockSpec((tiles, 3, size), lambda b, s: (0, 0, 0)),
                pl.BlockSpec((size, 3), lambda b, s: (b, 0)),
            ],
            out_specs=pl.BlockSpec((rows, boxes * size), lambda b, s: (0, 0)),
        ),
        compiler_params=pltpu.CompilerParams(dimension_semantics=("arbitrary",)),
        cost_estimate=pl.CostEstimate(
            flops=boxes * slots * size * size * (2 * rows + 12),
            transcendentals=0,
            bytes_accessed=4 * (probe_tiles.size + coord_tiles.size + 2 * rows * boxes * size),
        ),
    )(slot_source, probe_tiles, coord_tiles * stretch, points.T * stretch)


def body(probes, points, near_list, leaf_proxy, inner_proxy, top_proxy, far_list):
    groups = lax.axis_size("boxes")
    device = lax.axis_index("boxes")
    boxes_all = BOXES_DEV * groups
    kernel_scale = SHARPNESS * boxes_all
    rows_here = probes.shape[0]
    local_depth = BOXES_DEV.bit_length() - 1
    tree_depth = groups.bit_length() - 1
    live_slot = near_list >= 0
    slot_weight = live_slot.astype(jnp.float32)
    where_in = jnp.where(live_slot, (near_list - device * BOXES_DEV + W + boxes_all) % boxes_all, 0)
    box_points = points.reshape(3, BOXES_DEV, P_SIZE)
    probe_tiles = probes.reshape(rows_here, BOXES_DEV, P_SIZE)
    leaf_points = leaf_proxy.reshape(3, BOXES_DEV, R)
    leaf_basis = interpolation(box_points, leaf_points, kernel_scale)
    inner_points = inner_proxy.reshape(3, INNER_DEV, R)
    top_points = top_proxy.reshape(3, top_proxy.shape[1] // R, R)

    def node_proxy(height, node_index):
        offset = 2 * groups - 2 * (groups >> height)
        return lax.dynamic_slice_in_dim(top_points, offset + node_index, 1, 1)

    proxies = [leaf_points]
    for height in range(1, local_depth):
        offset = BOXES_DEV - (BOXES_DEV >> height - 1)
        number = BOXES_DEV >> height
        proxies.append(inner_points[:, offset : offset + number, :])
    proxies.append(node_proxy(0, device))
    level_moments = [jnp.einsum("qbp,bpr->qbr", probe_tiles, leaf_basis, precision=PRECISE)]
    transfer_maps = []
    for height in range(local_depth):
        interp_map = interpolation(
            proxies[height], jnp.repeat(proxies[height + 1], 2, axis=1), kernel_scale
        )
        transfer_maps.append(interp_map)
        lifted = jnp.einsum("qnr,nrs->qns", level_moments[-1], interp_map, precision=PRECISE)
        level_moments.append(lifted.reshape(rows_here, -1, 2, R).sum(axis=2))
    pyramid = jnp.concatenate(
        [
            jnp.concatenate(level_moments[:local_depth], axis=1),
            jnp.concatenate([leaf_points, inner_points], axis=1),
        ],
        axis=0,
    )
    pyramid_nodes = pyramid.shape[1]
    stacked = jnp.concatenate([probes, points], axis=0)
    width = W * P_SIZE
    flat_pyramid = pyramid.reshape(rows_here + 3, -1)
    from_left, from_right = exchange_halo(
        jnp.concatenate([stacked[:, -width:], flat_pyramid], axis=1),
        jnp.concatenate([stacked[:, :width], flat_pyramid], axis=1),
    )
    extended = jnp.concatenate([from_left[:, :width], stacked, from_right[:, :width]], axis=1)
    extended = extended.reshape(rows_here + 3, BOXES_DEV + 2 * W, P_SIZE)
    spread = jnp.concatenate(
        [
            from_left[:, width:].reshape(pyramid.shape),
            pyramid,
            from_right[:, width:].reshape(pyramid.shape),
        ],
        axis=1,
    )
    slot_source = jnp.where(live_slot, jnp.clip(where_in, 0, BOXES_DEV + 2 * W - 1), -1)
    near_field = near_field_call(
        slot_source.reshape(-1).astype(jnp.int32),
        jnp.moveaxis(extended[:rows_here], 1, 0),
        jnp.moveaxis(extended[rows_here:], 0, 1),
        points,
        kernel_scale,
    )
    index_parts, target_parts, mask_parts = [], [], []
    for height in range(local_depth):
        count = BOXES_DEV >> height
        start = 0 if height == 0 else 2 * BOXES_DEV - (BOXES_DEV >> height - 1)
        if height == 0:
            live_far = far_list >= 0
            view_ids = [
                jnp.where(
                    live_far[:, slot],
                    (far_list[:, slot] - device * BOXES_DEV + BOXES_DEV + boxes_all) % boxes_all,
                    0,
                )
                for slot in range(3)
            ]
            mask_parts += [live_far[:, slot].astype(jnp.float32) for slot in range(3)]
        else:
            node = jnp.arange(count, dtype=jnp.int32)
            third = jnp.where(node % 2 == 0, node + 3, node - 3)
            view_ids = [node - 2 + count, node + 2 + count, third + count]
            mask_parts += [jnp.ones((count,), jnp.float32)] * 3
        for view_id in view_ids:
            index_parts.append(view_id // count * pyramid_nodes + start + view_id % count)
            target_parts.append(proxies[height])
    picked = jnp.take(spread, jnp.concatenate(index_parts), axis=1)
    kernel_block = kernel_matrix(picked[rows_here:], jnp.concatenate(target_parts, axis=1), kernel_scale)
    source_moment = picked[:rows_here] * jnp.concatenate(mask_parts)[None, :, None]
    contributions = jnp.einsum("qnr,nrs->qns", source_moment, kernel_block, precision=PRECISE)
    local_couplings = []
    first = 0
    for height in range(local_depth):
        count = BOXES_DEV >> height
        part = contributions[:, first : first + 3 * count, :]
        local_couplings.append(part.reshape(rows_here, 3, count, R).sum(axis=1))
        first += 3 * count

    top_levels = tree_depth - 1
    level_points = []
    for height in range(top_levels):
        offset = 2 * groups - 2 * (groups >> height)
        level_points.append(top_points[:, offset : offset + (groups >> height), :])
    own_edges = []
    for height in range(top_levels - 1):
        own_edges.append(
            interpolation(
                lax.dynamic_slice_in_dim(level_points[height], device // 2**height, 1, 1),
                lax.dynamic_slice_in_dim(level_points[height + 1], device // 2 ** (height + 1), 1, 1),
                kernel_scale,
            )
        )
    path_moments = [level_moments[local_depth]]
    for height in range(top_levels - 1):
        path_moments.append(
            jnp.einsum("qnr,nrs->qns", path_moments[-1], own_edges[height], precision=PRECISE)
        )
    gathered = lax.all_gather(jnp.concatenate(path_moments, axis=1), "boxes", axis=0)
    top_moments, top_sources, top_targets, top_slots = [], [], [], []
    for height in range(top_levels):
        number = groups >> height
        node = device // 2**height
        level_sums = gathered[:, :, height, :].reshape(number, 2**height, rows_here, R).sum(axis=1)
        third = jnp.where(node % 2 == 0, node + 3, node - 3) % number
        if number > 4:
            source_ids = [(node - 2) % number, (node + 2) % number, third]
        else:
            source_ids = [(node + 2) % number]
        top_slots.append(len(source_ids))
        for source in source_ids:
            top_moments.append(lax.dynamic_index_in_dim(level_sums, source, 0, keepdims=True))
            top_sources.append(lax.dynamic_slice_in_dim(level_points[height], source, 1, 1))
            top_targets.append(lax.dynamic_slice_in_dim(level_points[height], node, 1, 1))
    kernel_block = kernel_matrix(
        jnp.concatenate(top_sources, axis=1), jnp.concatenate(top_targets, axis=1), kernel_scale
    )
    contributions = jnp.einsum(
        "nqr,nrs->qns", jnp.concatenate(top_moments, axis=0), kernel_block, precision=PRECISE
    )
    top_couplings = []
    first = 0
    for slots in top_slots:
        top_couplings.append(contributions[:, first : first + slots, :].sum(axis=1, keepdims=True))
        first += slots
    descent = top_couplings[-1]
    for height in range(top_levels - 2, -1, -1):
        descent = (
            jnp.einsum("qns,nrs->qnr", descent, own_edges[height], precision=PRECISE)
            + top_couplings[height]
        )
    for height in range(local_depth - 1, -1, -1):
        descent = jnp.einsum(
            "qns,nrs->qnr", jnp.repeat(descent, 2, axis=1), transfer_maps[height], precision=PRECISE
        )
        descent = descent + local_couplings[height]
    far_field = jnp.einsum("qbr,bpr->qbp", descent, leaf_basis, precision=PRECISE).reshape(
        rows_here, BOXES_DEV * P_SIZE
    )
    return near_field + far_field + NUGGET * probes


def solution(mesh):
    in_specs = (
        P("probe", "boxes"),
        P(None, "boxes"),
        P("boxes", None),
        P(None, "boxes"),
        P(None, "boxes"),
        P(),
        P("boxes", None),
    )
    out_specs = P("probe", "boxes")
    return jax.shard_map(body, mesh=mesh, in_specs=in_specs, out_specs=out_specs, check_vma=False)
```

```python
import functools

import jax
import jax.numpy as jnp
from jax import lax
from jax.experimental import pallas as pl
from jax.experimental.pallas import tpu as pltpu
from jax.sharding import PartitionSpec as P

BOXES_DEV = 32
P_SIZE = 256
R = 64
W = 3
INNER_DEV = 30


SHARPNESS = 0.05
NUGGET = 1.0
PRECISE = lax.Precision.HIGHEST
MESH = pl.DeviceIdType.MESH


def halo_kernel(to_right, to_left, from_left, from_right, left_slot, right_slot, send_sems, recv_sems):
    me = lax.axis_index("boxes")
    size = lax.axis_size("boxes")
    probe = lax.axis_index("probe")
    right = lax.rem(me + 1, size)
    left = lax.rem(me + size - 1, size)
    barrier = pltpu.get_barrier_semaphore()
    for neighbour in (left, right):
        pl.semaphore_signal(barrier, inc=1, device_id=(neighbour, probe), device_id_type=MESH)
    pl.semaphore_wait(barrier, 2)
    rightward = pltpu.make_async_remote_copy(
        src_ref=to_right,
        dst_ref=left_slot,
        send_sem=send_sems.at[0],
        recv_sem=recv_sems.at[0],
        device_id=(right, probe),
        device_id_type=MESH,
    )
    leftward = pltpu.make_async_remote_copy(
        src_ref=to_left,
        dst_ref=right_slot,
        send_sem=send_sems.at[1],
        recv_sem=recv_sems.at[1],
        device_id=(left, probe),
        device_id_type=MESH,
    )
    rightward.start()
    leftward.start()
    rightward.wait()
    leftward.wait()
    from_left[...] = left_slot[...]
    from_right[...] = right_slot[...]


def exchange_halo(to_right, to_left):
    shape = jax.ShapeDtypeStruct(to_right.shape, to_right.dtype)
    vmem = pl.BlockSpec(memory_space=pltpu.VMEM)
    return pl.pallas_call(
        halo_kernel,
        out_shape=(shape, shape),
        in_specs=[vmem, vmem],
        out_specs=(vmem, vmem),
        scratch_shapes=[
            pltpu.VMEM(to_right.shape, to_right.dtype),
            pltpu.VMEM(to_right.shape, to_right.dtype),
            pltpu.SemaphoreType.DMA((2,)),
            pltpu.SemaphoreType.DMA((2,)),
        ],
        compiler_params=pltpu.CompilerParams(collective_id=0, has_side_effects=True),
    )(to_right, to_left)

def kernel_matrix(left_points, right_points, kernel_scale):
    distance_sq = (left_points[0][..., :, None] - right_points[0][..., None, :]) ** 2
    distance_sq = distance_sq + (left_points[1][..., :, None] - right_points[1][..., None, :]) ** 2
    distance_sq = distance_sq + (left_points[2][..., :, None] - right_points[2][..., None, :]) ** 2
    return 1.0 / (1.0 + kernel_scale * distance_sq)


def interpolation(left_points, right_points, kernel_scale):
    values = kernel_matrix(left_points, right_points, kernel_scale)
    return values / jnp.sum(values, axis=-1, keepdims=True)


def near_kernel(slots, halo, source_ref, probes_ref, coords_ref, target_ref, out_ref):
    box = pl.program_id(0)
    boxes = pl.num_programs(0)
    size = target_ref.shape[0]
    target_x = jnp.broadcast_to(target_ref[:, 0:1], (size, size))
    target_y = jnp.broadcast_to(target_ref[:, 1:2], (size, size))
    target_z = jnp.broadcast_to(target_ref[:, 2:3], (size, size))
    here = box + halo
    columns = pl.ds(pl.multiple_of(box * size, size), size)

    def block(tile):
        near = coords_ref[tile]
        distance_sq = (near[0:1, :] - target_x) ** 2
        distance_sq = distance_sq + (near[1:2, :] - target_y) ** 2
        distance_sq = distance_sq + (near[2:3, :] - target_z) ** 2
        return 1.0 / (1.0 + distance_sq)

    def gather_into(tile, kernel_block):
        out_ref[:, columns] += lax.dot_general(
            probes_ref[tile], kernel_block, (((1,), (1,)), ((), ())),
            precision=lax.Precision.HIGH, preferred_element_type=jnp.float32,
        )

    @pl.when(box == 0)
    def _():
        out_ref[...] = jnp.zeros_like(out_ref)
        gather_into(here - 1, block(here - 1))

    gather_into(here, block(here))
    pair_block = block(here + 1)
    gather_into(here + 1, pair_block)

    @pl.when(box < boxes - 1)
    def _():
        following = pl.ds(pl.multiple_of((box + 1) * size, size), size)
        out_ref[:, following] += jnp.dot(
            probes_ref[here], pair_block, precision=lax.Precision.HIGH,
            preferred_element_type=jnp.float32,
        )

    def lists(row, tile):
        found = source_ref[row * slots] == tile
        for k in range(1, slots):
            found = found | (source_ref[row * slots + k] == tile)
        return found

    even = lax.rem(box, 2) == 0
    shared = []
    for step, allowed in ((2, True), (3, even)):
        partner = jnp.minimum(box + step, boxes - 1)
        shared.append(
            allowed & (box + step < boxes) & lists(box, here + step) & lists(partner, here)
        )
    skipped = []
    for step, allowed in ((2, True), (3, jnp.logical_not(even))):
        partner = jnp.maximum(box - step, 0)
        skipped.append(
            allowed & (box - step >= 0) & lists(box, here - step) & lists(partner, here)
        )
    for step, flag in zip((2, 3), shared):

        @pl.when(flag)
        def _():
            kernel_block = block(here + step)
            gather_into(here + step, kernel_block)
            later = pl.ds(pl.multiple_of((box + step) * size, size), size)
            out_ref[:, later] += jnp.dot(
                probes_ref[here], kernel_block, precision=lax.Precision.HIGH,
                preferred_element_type=jnp.float32,
            )

    for slot in range(slots):
        source = source_ref[box * slots + slot]
        done = (source == here - 1) | (source == here) | (source == here + 1)
        done = done | ((source == here + 2) & shared[0]) | ((source == here + 3) & shared[1])
        done = done | ((source == here - 2) & skipped[0]) | ((source == here - 3) & skipped[1])

        @pl.when((source >= 0) & jnp.logical_not(done))
        def _():
            gather_into(source, block(source))


def near_field_call(slot_source, probe_tiles, coord_tiles, points, kernel_scale):
    tiles, rows, size = probe_tiles.shape
    boxes = points.shape[1] // size
    slots = slot_source.shape[0] // boxes
    stretch = kernel_scale**0.5
    return pl.pallas_call(
        functools.partial(near_kernel, slots, W),
        out_shape=jax.ShapeDtypeStruct((rows, boxes * size), jnp.float32),
        grid_spec=pltpu.PrefetchScalarGridSpec(
            num_scalar_prefetch=1,
            grid=(boxes,),
            in_specs=[
                pl.BlockSpec((tiles, rows, size), lambda b, s: (0, 0, 0)),
                pl.BlockSpec((tiles, 3, size), lambda b, s: (0, 0, 0)),
                pl.BlockSpec((size, 3), lambda b, s: (b, 0)),
            ],
            out_specs=pl.BlockSpec((rows, boxes * size), lambda b, s: (0, 0)),
        ),
        compiler_params=pltpu.CompilerParams(dimension_semantics=("arbitrary",)),
        cost_estimate=pl.CostEstimate(
            flops=boxes * slots * size * size * (2 * rows + 12),
            transcendentals=0,
            bytes_accessed=4 * (probe_tiles.size + coord_tiles.size + 2 * rows * boxes * size),
        ),
    )(slot_source, probe_tiles, coord_tiles * stretch, points.T * stretch)


def body(probes, points, near_list, leaf_proxy, inner_proxy, top_proxy, far_list):
    groups = lax.axis_size("boxes")
    device = lax.axis_index("boxes")
    boxes_all = BOXES_DEV * groups
    kernel_scale = SHARPNESS * boxes_all
    rows_here = probes.shape[0]
    local_depth = BOXES_DEV.bit_length() - 1
    tree_depth = groups.bit_length() - 1
    live_slot = near_list >= 0
    slot_weight = live_slot.astype(jnp.float32)
    where_in = jnp.where(live_slot, (near_list - device * BOXES_DEV + W + boxes_all) % boxes_all, 0)
    box_points = points.reshape(3, BOXES_DEV, P_SIZE)
    probe_tiles = probes.reshape(rows_here, BOXES_DEV, P_SIZE)
    leaf_points = leaf_proxy.reshape(3, BOXES_DEV, R)
    leaf_basis = interpolation(box_points, leaf_points, kernel_scale)
    inner_points = inner_proxy.reshape(3, INNER_DEV, R)
    top_points = top_proxy.reshape(3, top_proxy.shape[1] // R, R)

    def node_proxy(height, node_index):
        offset = 2 * groups - 2 * (groups >> height)
        return lax.dynamic_slice_in_dim(top_points, offset + node_index, 1, 1)

    proxies = [leaf_points]
    for height in range(1, local_depth):
        offset = BOXES_DEV - (BOXES_DEV >> height - 1)
        number = BOXES_DEV >> height
        proxies.append(inner_points[:, offset : offset + number, :])
    proxies.append(node_proxy(0, device))
    level_moments = [jnp.einsum("qbp,bpr->qbr", probe_tiles, leaf_basis, precision=PRECISE)]
    transfer_maps = []
    for height in range(local_depth):
        interp_map = interpolation(
            proxies[height], jnp.repeat(proxies[height + 1], 2, axis=1), kernel_scale
        )
        transfer_maps.append(interp_map)
        lifted = jnp.einsum("qnr,nrs->qns", level_moments[-1], interp_map, precision=PRECISE)
        level_moments.append(lifted.reshape(rows_here, -1, 2, R).sum(axis=2))
    pyramid = jnp.concatenate(
        [
            jnp.concatenate(level_moments[:local_depth], axis=1),
            jnp.concatenate([leaf_points, inner_points], axis=1),
        ],
        axis=0,
    )
    pyramid_nodes = pyramid.shape[1]
    stacked = jnp.concatenate([probes, points], axis=0)
    width = W * P_SIZE
    flat_pyramid = pyramid.reshape(rows_here + 3, -1)
    from_left, from_right = exchange_halo(
        jnp.concatenate([stacked[:, -width:], flat_pyramid], axis=1),
        jnp.concatenate([stacked[:, :width], flat_pyramid], axis=1),
    )
    extended = jnp.concatenate([from_left[:, :width], stacked, from_right[:, :width]], axis=1)
    extended = extended.reshape(rows_here + 3, BOXES_DEV + 2 * W, P_SIZE)
    spread = jnp.concatenate(
        [
            from_left[:, width:].reshape(pyramid.shape),
            pyramid,
            from_right[:, width:].reshape(pyramid.shape),
        ],
        axis=1,
    )
    slot_source = jnp.where(live_slot, jnp.clip(where_in, 0, BOXES_DEV + 2 * W - 1), -1)
    near_field = near_field_call(
        slot_source.reshape(-1).astype(jnp.int32),
        jnp.moveaxis(extended[:rows_here], 1, 0),
        jnp.moveaxis(extended[rows_here:], 0, 1),
        points,
        kernel_scale,
    )
    index_parts, target_parts, mask_parts = [], [], []
    for height in range(local_depth):
        count = BOXES_DEV >> height
        start = 0 if height == 0 else 2 * BOXES_DEV - (BOXES_DEV >> height - 1)
        if height == 0:
            live_far = far_list >= 0
            view_ids = [
                jnp.where(
                    live_far[:, slot],
                    (far_list[:, slot] - device * BOXES_DEV + BOXES_DEV + boxes_all) % boxes_all,
                    0,
                )
                for slot in range(3)
            ]
            mask_parts += [live_far[:, slot].astype(jnp.float32) for slot in range(3)]
        else:
            node = jnp.arange(count, dtype=jnp.int32)
            third = jnp.where(node % 2 == 0, node + 3, node - 3)
            view_ids = [node - 2 + count, node + 2 + count, third + count]
            mask_parts += [jnp.ones((count,), jnp.float32)] * 3
        for view_id in view_ids:
            index_parts.append(view_id // count * pyramid_nodes + start + view_id % count)
            target_parts.append(proxies[height])
    picked = jnp.take(spread, jnp.concatenate(index_parts), axis=1)
    kernel_block = kernel_matrix(picked[rows_here:], jnp.concatenate(target_parts, axis=1), kernel_scale)
    source_moment = picked[:rows_here] * jnp.concatenate(mask_parts)[None, :, None]
    contributions = jnp.einsum("qnr,nrs->qns", source_moment, kernel_block, precision=PRECISE)
    local_couplings = []
    first = 0
    for height in range(local_depth):
        count = BOXES_DEV >> height
        part = contributions[:, first : first + 3 * count, :]
        local_couplings.append(part.reshape(rows_here, 3, count, R).sum(axis=1))
        first += 3 * count

    top_levels = tree_depth - 1
    level_points = []
    for height in range(top_levels):
        offset = 2 * groups - 2 * (groups >> height)
        level_points.append(top_points[:, offset : offset + (groups >> height), :])
    own_edges = []
    for height in range(top_levels - 1):
        own_edges.append(
            interpolation(
                lax.dynamic_slice_in_dim(level_points[height], device // 2**height, 1, 1),
                lax.dynamic_slice_in_dim(level_points[height + 1], device // 2 ** (height + 1), 1, 1),
                kernel_scale,
            )
        )
    path_moments = [level_moments[local_depth]]
    for height in range(top_levels - 1):
        path_moments.append(
            jnp.einsum("qnr,nrs->qns", path_moments[-1], own_edges[height], precision=PRECISE)
        )
    gathered = lax.all_gather(jnp.concatenate(path_moments, axis=1), "boxes", axis=0)
    top_moments, top_sources, top_targets, top_slots = [], [], [], []
    for height in range(top_levels):
        number = groups >> height
        node = device // 2**height
        level_sums = gathered[:, :, height, :].reshape(number, 2**height, rows_here, R).sum(axis=1)
        third = jnp.where(node % 2 == 0, node + 3, node - 3) % number
        if number > 4:
            source_ids = [(node - 2) % number, (node + 2) % number, third]
        else:
            source_ids = [(node + 2) % number]
        top_slots.append(len(source_ids))
        for source in source_ids:
            top_moments.append(lax.dynamic_index_in_dim(level_sums, source, 0, keepdims=True))
            top_sources.append(lax.dynamic_slice_in_dim(level_points[height], source, 1, 1))
            top_targets.append(lax.dynamic_slice_in_dim(level_points[height], node, 1, 1))
    kernel_block = kernel_matrix(
        jnp.concatenate(top_sources, axis=1), jnp.concatenate(top_targets, axis=1), kernel_scale
    )
    contributions = jnp.einsum(
        "nqr,nrs->qns", jnp.concatenate(top_moments, axis=0), kernel_block, precision=PRECISE
    )
    top_couplings = []
    first = 0
    for slots in top_slots:
        top_couplings.append(contributions[:, first : first + slots, :].sum(axis=1, keepdims=True))
        first += slots
    descent = top_couplings[-1]
    for height in range(top_levels - 2, -1, -1):
        descent = (
            jnp.einsum("qns,nrs->qnr", descent, own_edges[height], precision=PRECISE)
            + top_couplings[height]
        )
    for height in range(local_depth - 1, -1, -1):
        descent = jnp.einsum(
            "qns,nrs->qnr", jnp.repeat(descent, 2, axis=1), transfer_maps[height], precision=PRECISE
        )
        descent = descent + local_couplings[height]
    far_field = jnp.einsum("qbr,bpr->qbp", descent, leaf_basis, precision=PRECISE).reshape(
        rows_here, BOXES_DEV * P_SIZE
    )
    return near_field + far_field + NUGGET * probes


def solution(mesh):
    in_specs = (
        P("probe", "boxes"),
        P(None, "boxes"),
        P("boxes", None),
        P(None, "boxes"),
        P(None, "boxes"),
        P(),
        P("boxes", None),
    )
    out_specs = P("probe", "boxes")
    return jax.shard_map(body, mesh=mesh, in_specs=in_specs, out_specs=out_specs, check_vma=False)
```

```python
import functools

import jax
import jax.numpy as jnp
from jax import lax
from jax.experimental import pallas as pl
from jax.experimental.pallas import tpu as pltpu
from jax.sharding import PartitionSpec as P

BOXES_DEV = 32
P_SIZE = 256
R = 64
W = 3
INNER_DEV = 30


SHARPNESS = 0.05
NUGGET = 1.0
PRECISE = lax.Precision.HIGHEST
MESH = pl.DeviceIdType.MESH


def halo_kernel(to_right, to_left, from_left, from_right, left_slot, right_slot, send_sems, recv_sems):
    me = lax.axis_index("boxes")
    size = lax.axis_size("boxes")
    probe = lax.axis_index("probe")
    right = lax.rem(me + 1, size)
    left = lax.rem(me + size - 1, size)
    barrier = pltpu.get_barrier_semaphore()
    for neighbour in (left, right):
        pl.semaphore_signal(barrier, inc=1, device_id=(neighbour, probe), device_id_type=MESH)
    pl.semaphore_wait(barrier, 2)
    rightward = pltpu.make_async_remote_copy(
        src_ref=to_right,
        dst_ref=left_slot,
        send_sem=send_sems.at[0],
        recv_sem=recv_sems.at[0],
        device_id=(right, probe),
        device_id_type=MESH,
    )
    leftward = pltpu.make_async_remote_copy(
        src_ref=to_left,
        dst_ref=right_slot,
        send_sem=send_sems.at[1],
        recv_sem=recv_sems.at[1],
        device_id=(left, probe),
        device_id_type=MESH,
    )
    rightward.start()
    leftward.start()
    rightward.wait()
    leftward.wait()
    from_left[...] = left_slot[...]
    from_right[...] = right_slot[...]


def exchange_halo(to_right, to_left):
    shape = jax.ShapeDtypeStruct(to_right.shape, to_right.dtype)
    vmem = pl.BlockSpec(memory_space=pltpu.VMEM)
    return pl.pallas_call(
        halo_kernel,
        out_shape=(shape, shape),
        in_specs=[vmem, vmem],
        out_specs=(vmem, vmem),
        scratch_shapes=[
            pltpu.VMEM(to_right.shape, to_right.dtype),
            pltpu.VMEM(to_right.shape, to_right.dtype),
            pltpu.SemaphoreType.DMA((2,)),
            pltpu.SemaphoreType.DMA((2,)),
        ],
        compiler_params=pltpu.CompilerParams(collective_id=0, has_side_effects=True),
    )(to_right, to_left)

def kernel_matrix(left_points, right_points, kernel_scale):
    distance_sq = (left_points[0][..., :, None] - right_points[0][..., None, :]) ** 2
    distance_sq = distance_sq + (left_points[1][..., :, None] - right_points[1][..., None, :]) ** 2
    distance_sq = distance_sq + (left_points[2][..., :, None] - right_points[2][..., None, :]) ** 2
    return 1.0 / (1.0 + kernel_scale * distance_sq)


def interpolation(left_points, right_points, kernel_scale):
    values = kernel_matrix(left_points, right_points, kernel_scale)
    return values / jnp.sum(values, axis=-1, keepdims=True)


def near_kernel(slots, halo, stretch, source_ref, tiles_ref, target_ref, out_ref):
    box = pl.program_id(0)
    boxes = pl.num_programs(0)
    size = target_ref.shape[0]
    rows = out_ref.shape[0]
    target_x = jnp.broadcast_to(target_ref[:, 0:1] * stretch, (size, size))
    target_y = jnp.broadcast_to(target_ref[:, 1:2] * stretch, (size, size))
    target_z = jnp.broadcast_to(target_ref[:, 2:3] * stretch, (size, size))
    here = box + halo
    columns = pl.ds(pl.multiple_of(box * size, size), size)

    def tile_columns(tile):
        return pl.ds(pl.multiple_of(tile * size, size), size)

    def probes_of(tile):
        return tiles_ref[0:rows, tile_columns(tile)]

    def block(tile):
        near = tiles_ref[rows : rows + 3, tile_columns(tile)] * stretch
        distance_sq = (near[0:1, :] - target_x) ** 2
        distance_sq = distance_sq + (near[1:2, :] - target_y) ** 2
        distance_sq = distance_sq + (near[2:3, :] - target_z) ** 2
        return 1.0 / (1.0 + distance_sq)

    def gather_into(tile, kernel_block):
        out_ref[:, columns] += lax.dot_general(
            probes_of(tile), kernel_block, (((1,), (1,)), ((), ())),
            precision=lax.Precision.HIGH, preferred_element_type=jnp.float32,
        )

    @pl.when(box == 0)
    def _():
        out_ref[...] = jnp.zeros_like(out_ref)
        gather_into(here - 1, block(here - 1))

    gather_into(here, block(here))
    pair_block = block(here + 1)
    gather_into(here + 1, pair_block)

    @pl.when(box < boxes - 1)
    def _():
        following = pl.ds(pl.multiple_of((box + 1) * size, size), size)
        out_ref[:, following] += jnp.dot(
            probes_of(here), pair_block, precision=lax.Precision.HIGH,
            preferred_element_type=jnp.float32,
        )

    def lists(row, tile):
        found = source_ref[row * slots] == tile
        for k in range(1, slots):
            found = found | (source_ref[row * slots + k] == tile)
        return found

    even = lax.rem(box, 2) == 0
    shared = []
    for step, allowed in ((2, True), (3, even)):
        partner = jnp.minimum(box + step, boxes - 1)
        shared.append(
            allowed & (box + step < boxes) & lists(box, here + step) & lists(partner, here)
        )
    skipped = []
    for step, allowed in ((2, True), (3, jnp.logical_not(even))):
        partner = jnp.maximum(box - step, 0)
        skipped.append(
            allowed & (box - step >= 0) & lists(box, here - step) & lists(partner, here)
        )
    for step, flag in zip((2, 3), shared):

        @pl.when(flag)
        def _():
            kernel_block = block(here + step)
            gather_into(here + step, kernel_block)
            later = pl.ds(pl.multiple_of((box + step) * size, size), size)
            out_ref[:, later] += jnp.dot(
                probes_of(here), kernel_block, precision=lax.Precision.HIGH,
                preferred_element_type=jnp.float32,
            )

    for slot in range(slots):
        source = source_ref[box * slots + slot]
        done = (source == here - 1) | (source == here) | (source == here + 1)
        done = done | ((source == here + 2) & shared[0]) | ((source == here + 3) & shared[1])
        done = done | ((source == here - 2) & skipped[0]) | ((source == here - 3) & skipped[1])

        @pl.when((source >= 0) & jnp.logical_not(done))
        def _():
            gather_into(source, block(source))


def near_field_call(slot_source, tiles, points, kernel_scale):
    rows = tiles.shape[0] - 3
    size = P_SIZE
    boxes = points.shape[1] // size
    slots = slot_source.shape[0] // boxes
    return pl.pallas_call(
        functools.partial(near_kernel, slots, W, kernel_scale**0.5),
        out_shape=jax.ShapeDtypeStruct((rows, boxes * size), jnp.float32),
        grid_spec=pltpu.PrefetchScalarGridSpec(
            num_scalar_prefetch=1,
            grid=(boxes,),
            in_specs=[
                pl.BlockSpec(tiles.shape, lambda b, s: (0, 0)),
                pl.BlockSpec((size, 3), lambda b, s: (b, 0)),
            ],
            out_specs=pl.BlockSpec((rows, boxes * size), lambda b, s: (0, 0)),
        ),
        compiler_params=pltpu.CompilerParams(dimension_semantics=("arbitrary",)),
        cost_estimate=pl.CostEstimate(
            flops=boxes * slots * size * size * (2 * rows + 12),
            transcendentals=0,
            bytes_accessed=4 * (tiles.size + 2 * rows * boxes * size),
        ),
    )(slot_source, tiles, points.T)


def body(probes, points, near_list, leaf_proxy, inner_proxy, top_proxy, far_list):
    groups = lax.axis_size("boxes")
    device = lax.axis_index("boxes")
    boxes_all = BOXES_DEV * groups
    kernel_scale = SHARPNESS * boxes_all
    rows_here = probes.shape[0]
    local_depth = BOXES_DEV.bit_length() - 1
    tree_depth = groups.bit_length() - 1
    live_slot = near_list >= 0
    slot_weight = live_slot.astype(jnp.float32)
    where_in = jnp.where(live_slot, (near_list - device * BOXES_DEV + W + boxes_all) % boxes_all, 0)
    box_points = points.reshape(3, BOXES_DEV, P_SIZE)
    probe_tiles = probes.reshape(rows_here, BOXES_DEV, P_SIZE)
    leaf_points = leaf_proxy.reshape(3, BOXES_DEV, R)
    leaf_basis = interpolation(box_points, leaf_points, kernel_scale)
    inner_points = inner_proxy.reshape(3, INNER_DEV, R)
    top_points = top_proxy.reshape(3, top_proxy.shape[1] // R, R)

    def node_proxy(height, node_index):
        offset = 2 * groups - 2 * (groups >> height)
        return lax.dynamic_slice_in_dim(top_points, offset + node_index, 1, 1)

    proxies = [leaf_points]
    for height in range(1, local_depth):
        offset = BOXES_DEV - (BOXES_DEV >> height - 1)
        number = BOXES_DEV >> height
        proxies.append(inner_points[:, offset : offset + number, :])
    proxies.append(node_proxy(0, device))
    level_moments = [jnp.einsum("qbp,bpr->qbr", probe_tiles, leaf_basis, precision=PRECISE)]
    transfer_maps = []
    for height in range(local_depth):
        interp_map = interpolation(
            proxies[height], jnp.repeat(proxies[height + 1], 2, axis=1), kernel_scale
        )
        transfer_maps.append(interp_map)
        lifted = jnp.einsum("qnr,nrs->qns", level_moments[-1], interp_map, precision=PRECISE)
        level_moments.append(lifted.reshape(rows_here, -1, 2, R).sum(axis=2))
    pyramid = jnp.concatenate(
        [
            jnp.concatenate(level_moments[:local_depth], axis=1),
            jnp.concatenate([leaf_points, inner_points], axis=1),
        ],
        axis=0,
    )
    pyramid_nodes = pyramid.shape[1]
    stacked = jnp.concatenate([probes, points], axis=0)
    width = W * P_SIZE
    flat_pyramid = pyramid.reshape(rows_here + 3, -1)
    from_left, from_right = exchange_halo(
        jnp.concatenate([stacked[:, -width:], flat_pyramid], axis=1),
        jnp.concatenate([stacked[:, :width], flat_pyramid], axis=1),
    )
    extended = jnp.concatenate([from_left[:, :width], stacked, from_right[:, :width]], axis=1)
    spread = jnp.concatenate(
        [
            from_left[:, width:].reshape(pyramid.shape),
            pyramid,
            from_right[:, width:].reshape(pyramid.shape),
        ],
        axis=1,
    )
    slot_source = jnp.where(live_slot, jnp.clip(where_in, 0, BOXES_DEV + 2 * W - 1), -1)
    near_field = near_field_call(
        slot_source.reshape(-1).astype(jnp.int32),
        extended,
        points,
        kernel_scale,
    )
    index_parts, target_parts, mask_parts = [], [], []
    for height in range(local_depth):
        count = BOXES_DEV >> height
        start = 0 if height == 0 else 2 * BOXES_DEV - (BOXES_DEV >> height - 1)
        if height == 0:
            live_far = far_list >= 0
            view_ids = [
                jnp.where(
                    live_far[:, slot],
                    (far_list[:, slot] - device * BOXES_DEV + BOXES_DEV + boxes_all) % boxes_all,
                    0,
                )
                for slot in range(3)
            ]
            mask_parts += [live_far[:, slot].astype(jnp.float32) for slot in range(3)]
        else:
            node = jnp.arange(count, dtype=jnp.int32)
            third = jnp.where(node % 2 == 0, node + 3, node - 3)
            view_ids = [node - 2 + count, node + 2 + count, third + count]
            mask_parts += [jnp.ones((count,), jnp.float32)] * 3
        for view_id in view_ids:
            index_parts.append(view_id // count * pyramid_nodes + start + view_id % count)
            target_parts.append(proxies[height])
    picked = jnp.take(spread, jnp.concatenate(index_parts), axis=1)
    kernel_block = kernel_matrix(picked[rows_here:], jnp.concatenate(target_parts, axis=1), kernel_scale)
    source_moment = picked[:rows_here] * jnp.concatenate(mask_parts)[None, :, None]
    contributions = jnp.einsum("qnr,nrs->qns", source_moment, kernel_block, precision=PRECISE)
    local_couplings = []
    first = 0
    for height in range(local_depth):
        count = BOXES_DEV >> height
        part = contributions[:, first : first + 3 * count, :]
        local_couplings.append(part.reshape(rows_here, 3, count, R).sum(axis=1))
        first += 3 * count

    top_levels = tree_depth - 1
    level_points = []
    for height in range(top_levels):
        offset = 2 * groups - 2 * (groups >> height)
        level_points.append(top_points[:, offset : offset + (groups >> height), :])
    own_edges = []
    for height in range(top_levels - 1):
        own_edges.append(
            interpolation(
                lax.dynamic_slice_in_dim(level_points[height], device // 2**height, 1, 1),
                lax.dynamic_slice_in_dim(level_points[height + 1], device // 2 ** (height + 1), 1, 1),
                kernel_scale,
            )
        )
    path_moments = [level_moments[local_depth]]
    for height in range(top_levels - 1):
        path_moments.append(
            jnp.einsum("qnr,nrs->qns", path_moments[-1], own_edges[height], precision=PRECISE)
        )
    gathered = lax.all_gather(jnp.concatenate(path_moments, axis=1), "boxes", axis=0)
    top_moments, top_sources, top_targets, top_slots = [], [], [], []
    for height in range(top_levels):
        number = groups >> height
        node = device // 2**height
        level_sums = gathered[:, :, height, :].reshape(number, 2**height, rows_here, R).sum(axis=1)
        third = jnp.where(node % 2 == 0, node + 3, node - 3) % number
        if number > 4:
            source_ids = [(node - 2) % number, (node + 2) % number, third]
        else:
            source_ids = [(node + 2) % number]
        top_slots.append(len(source_ids))
        for source in source_ids:
            top_moments.append(lax.dynamic_index_in_dim(level_sums, source, 0, keepdims=True))
            top_sources.append(lax.dynamic_slice_in_dim(level_points[height], source, 1, 1))
            top_targets.append(lax.dynamic_slice_in_dim(level_points[height], node, 1, 1))
    kernel_block = kernel_matrix(
        jnp.concatenate(top_sources, axis=1), jnp.concatenate(top_targets, axis=1), kernel_scale
    )
    contributions = jnp.einsum(
        "nqr,nrs->qns", jnp.concatenate(top_moments, axis=0), kernel_block, precision=PRECISE
    )
    top_couplings = []
    first = 0
    for slots in top_slots:
        top_couplings.append(contributions[:, first : first + slots, :].sum(axis=1, keepdims=True))
        first += slots
    descent = top_couplings[-1]
    for height in range(top_levels - 2, -1, -1):
        descent = (
            jnp.einsum("qns,nrs->qnr", descent, own_edges[height], precision=PRECISE)
            + top_couplings[height]
        )
    for height in range(local_depth - 1, -1, -1):
        descent = jnp.einsum(
            "qns,nrs->qnr", jnp.repeat(descent, 2, axis=1), transfer_maps[height], precision=PRECISE
        )
        descent = descent + local_couplings[height]
    far_field = jnp.einsum("qbr,bpr->qbp", descent, leaf_basis, precision=PRECISE).reshape(
        rows_here, BOXES_DEV * P_SIZE
    )
    return near_field + far_field + NUGGET * probes


def solution(mesh):
    in_specs = (
        P("probe", "boxes"),
        P(None, "boxes"),
        P("boxes", None),
        P(None, "boxes"),
        P(None, "boxes"),
        P(),
        P("boxes", None),
    )
    out_specs = P("probe", "boxes")
    return jax.shard_map(body, mesh=mesh, in_specs=in_specs, out_specs=out_specs, check_vma=False)
```

```python
import functools

import jax
import jax.numpy as jnp
from jax import lax
from jax.experimental import pallas as pl
from jax.experimental.pallas import tpu as pltpu
from jax.sharding import PartitionSpec as P

BOXES_DEV = 32
P_SIZE = 256
R = 64
W = 3
INNER_DEV = 30


SHARPNESS = 0.05
NUGGET = 1.0
PRECISE = lax.Precision.HIGH
MESH = pl.DeviceIdType.MESH


def halo_kernel(to_right, to_left, from_left, from_right, left_slot, right_slot, send_sems, recv_sems):
    me = lax.axis_index("boxes")
    size = lax.axis_size("boxes")
    probe = lax.axis_index("probe")
    right = lax.rem(me + 1, size)
    left = lax.rem(me + size - 1, size)
    barrier = pltpu.get_barrier_semaphore()
    for neighbour in (left, right):
        pl.semaphore_signal(barrier, inc=1, device_id=(neighbour, probe), device_id_type=MESH)
    pl.semaphore_wait(barrier, 2)
    rightward = pltpu.make_async_remote_copy(
        src_ref=to_right,
        dst_ref=left_slot,
        send_sem=send_sems.at[0],
        recv_sem=recv_sems.at[0],
        device_id=(right, probe),
        device_id_type=MESH,
    )
    leftward = pltpu.make_async_remote_copy(
        src_ref=to_left,
        dst_ref=right_slot,
        send_sem=send_sems.at[1],
        recv_sem=recv_sems.at[1],
        device_id=(left, probe),
        device_id_type=MESH,
    )
    rightward.start()
    leftward.start()
    rightward.wait()
    leftward.wait()
    from_left[...] = left_slot[...]
    from_right[...] = right_slot[...]


def exchange_halo(to_right, to_left):
    shape = jax.ShapeDtypeStruct(to_right.shape, to_right.dtype)
    vmem = pl.BlockSpec(memory_space=pltpu.VMEM)
    return pl.pallas_call(
        halo_kernel,
        out_shape=(shape, shape),
        in_specs=[vmem, vmem],
        out_specs=(vmem, vmem),
        scratch_shapes=[
            pltpu.VMEM(to_right.shape, to_right.dtype),
            pltpu.VMEM(to_right.shape, to_right.dtype),
            pltpu.SemaphoreType.DMA((2,)),
            pltpu.SemaphoreType.DMA((2,)),
        ],
        compiler_params=pltpu.CompilerParams(collective_id=0, has_side_effects=True),
    )(to_right, to_left)

def kernel_matrix(left_points, right_points, kernel_scale):
    distance_sq = (left_points[0][..., :, None] - right_points[0][..., None, :]) ** 2
    distance_sq = distance_sq + (left_points[1][..., :, None] - right_points[1][..., None, :]) ** 2
    distance_sq = distance_sq + (left_points[2][..., :, None] - right_points[2][..., None, :]) ** 2
    return 1.0 / (1.0 + kernel_scale * distance_sq)


def interpolation(left_points, right_points, kernel_scale):
    values = kernel_matrix(left_points, right_points, kernel_scale)
    return values / jnp.sum(values, axis=-1, keepdims=True)


def near_kernel(slots, halo, source_ref, probes_ref, coords_ref, target_ref, out_ref):
    box = pl.program_id(0)
    boxes = pl.num_programs(0)
    size = target_ref.shape[0]
    target_x = jnp.broadcast_to(target_ref[:, 0:1], (size, size))
    target_y = jnp.broadcast_to(target_ref[:, 1:2], (size, size))
    target_z = jnp.broadcast_to(target_ref[:, 2:3], (size, size))
    here = box + halo
    columns = pl.ds(pl.multiple_of(box * size, size), size)

    def block(tile):
        near = coords_ref[tile]
        distance_sq = (near[0:1, :] - target_x) ** 2
        distance_sq = distance_sq + (near[1:2, :] - target_y) ** 2
        distance_sq = distance_sq + (near[2:3, :] - target_z) ** 2
        return pl.reciprocal(1.0 + distance_sq, approx=False)

    def gather_into(tile, kernel_block):
        out_ref[:, columns] += lax.dot_general(
            probes_ref[tile], kernel_block, (((1,), (1,)), ((), ())),
            precision=lax.Precision.HIGH, preferred_element_type=jnp.float32,
        )

    @pl.when(box == 0)
    def _():
        out_ref[...] = jnp.zeros_like(out_ref)
        gather_into(here - 1, block(here - 1))

    gather_into(here, block(here))
    pair_block = block(here + 1)
    gather_into(here + 1, pair_block)

    @pl.when(box < boxes - 1)
    def _():
        following = pl.ds(pl.multiple_of((box + 1) * size, size), size)
        out_ref[:, following] += jnp.dot(
            probes_ref[here], pair_block, precision=lax.Precision.HIGH,
            preferred_element_type=jnp.float32,
        )

    def lists(row, tile):
        found = source_ref[row * slots] == tile
        for k in range(1, slots):
            found = found | (source_ref[row * slots + k] == tile)
        return found

    even = lax.rem(box, 2) == 0
    shared = []
    for step, allowed in ((2, True), (3, even)):
        partner = jnp.minimum(box + step, boxes - 1)
        shared.append(
            allowed & (box + step < boxes) & lists(box, here + step) & lists(partner, here)
        )
    skipped = []
    for step, allowed in ((2, True), (3, jnp.logical_not(even))):
        partner = jnp.maximum(box - step, 0)
        skipped.append(
            allowed & (box - step >= 0) & lists(box, here - step) & lists(partner, here)
        )
    for step, flag in zip((2, 3), shared):

        @pl.when(flag)
        def _():
            kernel_block = block(here + step)
            gather_into(here + step, kernel_block)
            later = pl.ds(pl.multiple_of((box + step) * size, size), size)
            out_ref[:, later] += jnp.dot(
                probes_ref[here], kernel_block, precision=lax.Precision.HIGH,
                preferred_element_type=jnp.float32,
            )

    for slot in range(slots):
        source = source_ref[box * slots + slot]
        done = (source == here - 1) | (source == here) | (source == here + 1)
        done = done | ((source == here + 2) & shared[0]) | ((source == here + 3) & shared[1])
        done = done | ((source == here - 2) & skipped[0]) | ((source == here - 3) & skipped[1])

        @pl.when((source >= 0) & jnp.logical_not(done))
        def _():
            gather_into(source, block(source))


def near_field_call(slot_source, probe_tiles, coord_tiles, points, kernel_scale):
    tiles, rows, size = probe_tiles.shape
    boxes = points.shape[1] // size
    slots = slot_source.shape[0] // boxes
    stretch = kernel_scale**0.5
    return pl.pallas_call(
        functools.partial(near_kernel, slots, W),
        out_shape=jax.ShapeDtypeStruct((rows, boxes * size), jnp.float32),
        grid_spec=pltpu.PrefetchScalarGridSpec(
            num_scalar_prefetch=1,
            grid=(boxes,),
            in_specs=[
                pl.BlockSpec((tiles, rows, size), lambda b, s: (0, 0, 0)),
                pl.BlockSpec((tiles, 3, size), lambda b, s: (0, 0, 0)),
                pl.BlockSpec((size, 3), lambda b, s: (b, 0)),
            ],
            out_specs=pl.BlockSpec((rows, boxes * size), lambda b, s: (0, 0)),
        ),
        compiler_params=pltpu.CompilerParams(dimension_semantics=("arbitrary",)),
        cost_estimate=pl.CostEstimate(
            flops=boxes * slots * size * size * (2 * rows + 12),
            transcendentals=0,
            bytes_accessed=4 * (probe_tiles.size + coord_tiles.size + 2 * rows * boxes * size),
        ),
    )(slot_source, probe_tiles, coord_tiles * stretch, points.T * stretch)


def body(probes, points, near_list, leaf_proxy, inner_proxy, top_proxy, far_list):
    groups = lax.axis_size("boxes")
    device = lax.axis_index("boxes")
    boxes_all = BOXES_DEV * groups
    kernel_scale = SHARPNESS * boxes_all
    rows_here = probes.shape[0]
    local_depth = BOXES_DEV.bit_length() - 1
    tree_depth = groups.bit_length() - 1
    live_slot = near_list >= 0
    slot_weight = live_slot.astype(jnp.float32)
    where_in = jnp.where(live_slot, (near_list - device * BOXES_DEV + W + boxes_all) % boxes_all, 0)
    box_points = points.reshape(3, BOXES_DEV, P_SIZE)
    probe_tiles = probes.reshape(rows_here, BOXES_DEV, P_SIZE)
    leaf_points = leaf_proxy.reshape(3, BOXES_DEV, R)
    leaf_basis = interpolation(box_points, leaf_points, kernel_scale)
    inner_points = inner_proxy.reshape(3, INNER_DEV, R)
    top_points = top_proxy.reshape(3, top_proxy.shape[1] // R, R)

    def node_proxy(height, node_index):
        offset = 2 * groups - 2 * (groups >> height)
        return lax.dynamic_slice_in_dim(top_points, offset + node_index, 1, 1)

    proxies = [leaf_points]
    for height in range(1, local_depth):
        offset = BOXES_DEV - (BOXES_DEV >> height - 1)
        number = BOXES_DEV >> height
        proxies.append(inner_points[:, offset : offset + number, :])
    proxies.append(node_proxy(0, device))
    level_moments = [jnp.einsum("qbp,bpr->qbr", probe_tiles, leaf_basis, precision=PRECISE)]
    transfer_maps = []
    for height in range(local_depth):
        interp_map = interpolation(
            proxies[height], jnp.repeat(proxies[height + 1], 2, axis=1), kernel_scale
        )
        transfer_maps.append(interp_map)
        lifted = jnp.einsum("qnr,nrs->qns", level_moments[-1], interp_map, precision=PRECISE)
        level_moments.append(lifted.reshape(rows_here, -1, 2, R).sum(axis=2))
    pyramid = jnp.concatenate(
        [
            jnp.concatenate(level_moments[:local_depth], axis=1),
            jnp.concatenate([leaf_points, inner_points], axis=1),
        ],
        axis=0,
    )
    pyramid_nodes = pyramid.shape[1]
    stacked = jnp.concatenate([probes, points], axis=0)
    width = W * P_SIZE
    flat_pyramid = pyramid.reshape(rows_here + 3, -1)
    from_left, from_right = exchange_halo(
        jnp.concatenate([stacked[:, -width:], flat_pyramid], axis=1),
        jnp.concatenate([stacked[:, :width], flat_pyramid], axis=1),
    )
    extended = jnp.concatenate([from_left[:, :width], stacked, from_right[:, :width]], axis=1)
    extended = extended.reshape(rows_here + 3, BOXES_DEV + 2 * W, P_SIZE)
    spread = jnp.concatenate(
        [
            from_left[:, width:].reshape(pyramid.shape),
            pyramid,
            from_right[:, width:].reshape(pyramid.shape),
        ],
        axis=1,
    )
    slot_source = jnp.where(live_slot, jnp.clip(where_in, 0, BOXES_DEV + 2 * W - 1), -1)
    near_field = near_field_call(
        slot_source.reshape(-1).astype(jnp.int32),
        jnp.moveaxis(extended[:rows_here], 1, 0),
        jnp.moveaxis(extended[rows_here:], 0, 1),
        points,
        kernel_scale,
    )
    index_parts, target_parts, mask_parts = [], [], []
    for height in range(local_depth):
        count = BOXES_DEV >> height
        start = 0 if height == 0 else 2 * BOXES_DEV - (BOXES_DEV >> height - 1)
        if height == 0:
            live_far = far_list >= 0
            view_ids = [
                jnp.where(
                    live_far[:, slot],
                    (far_list[:, slot] - device * BOXES_DEV + BOXES_DEV + boxes_all) % boxes_all,
                    0,
                )
                for slot in range(3)
            ]
            mask_parts += [live_far[:, slot].astype(jnp.float32) for slot in range(3)]
        else:
            node = jnp.arange(count, dtype=jnp.int32)
            third = jnp.where(node % 2 == 0, node + 3, node - 3)
            view_ids = [node - 2 + count, node + 2 + count, third + count]
            mask_parts += [jnp.ones((count,), jnp.float32)] * 3
        for view_id in view_ids:
            index_parts.append(view_id // count * pyramid_nodes + start + view_id % count)
            target_parts.append(proxies[height])
    picked = jnp.take(spread, jnp.concatenate(index_parts), axis=1)
    kernel_block = kernel_matrix(picked[rows_here:], jnp.concatenate(target_parts, axis=1), kernel_scale)
    source_moment = picked[:rows_here] * jnp.concatenate(mask_parts)[None, :, None]
    contributions = jnp.einsum("qnr,nrs->qns", source_moment, kernel_block, precision=PRECISE)
    local_couplings = []
    first = 0
    for height in range(local_depth):
        count = BOXES_DEV >> height
        part = contributions[:, first : first + 3 * count, :]
        local_couplings.append(part.reshape(rows_here, 3, count, R).sum(axis=1))
        first += 3 * count

    top_levels = tree_depth - 1
    level_points = []
    for height in range(top_levels):
        offset = 2 * groups - 2 * (groups >> height)
        level_points.append(top_points[:, offset : offset + (groups >> height), :])
    own_edges = []
    for height in range(top_levels - 1):
        own_edges.append(
            interpolation(
                lax.dynamic_slice_in_dim(level_points[height], device // 2**height, 1, 1),
                lax.dynamic_slice_in_dim(level_points[height + 1], device // 2 ** (height + 1), 1, 1),
                kernel_scale,
            )
        )
    path_moments = [level_moments[local_depth]]
    for height in range(top_levels - 1):
        path_moments.append(
            jnp.einsum("qnr,nrs->qns", path_moments[-1], own_edges[height], precision=PRECISE)
        )
    gathered = lax.all_gather(jnp.concatenate(path_moments, axis=1), "boxes", axis=0)
    top_moments, top_sources, top_targets, top_slots = [], [], [], []
    for height in range(top_levels):
        number = groups >> height
        node = device // 2**height
        level_sums = gathered[:, :, height, :].reshape(number, 2**height, rows_here, R).sum(axis=1)
        third = jnp.where(node % 2 == 0, node + 3, node - 3) % number
        if number > 4:
            source_ids = [(node - 2) % number, (node + 2) % number, third]
        else:
            source_ids = [(node + 2) % number]
        top_slots.append(len(source_ids))
        for source in source_ids:
            top_moments.append(lax.dynamic_index_in_dim(level_sums, source, 0, keepdims=True))
            top_sources.append(lax.dynamic_slice_in_dim(level_points[height], source, 1, 1))
            top_targets.append(lax.dynamic_slice_in_dim(level_points[height], node, 1, 1))
    kernel_block = kernel_matrix(
        jnp.concatenate(top_sources, axis=1), jnp.concatenate(top_targets, axis=1), kernel_scale
    )
    contributions = jnp.einsum(
        "nqr,nrs->qns", jnp.concatenate(top_moments, axis=0), kernel_block, precision=PRECISE
    )
    top_couplings = []
    first = 0
    for slots in top_slots:
        top_couplings.append(contributions[:, first : first + slots, :].sum(axis=1, keepdims=True))
        first += slots
    descent = top_couplings[-1]
    for height in range(top_levels - 2, -1, -1):
        descent = (
            jnp.einsum("qns,nrs->qnr", descent, own_edges[height], precision=PRECISE)
            + top_couplings[height]
        )
    for height in range(local_depth - 1, -1, -1):
        descent = jnp.einsum(
            "qns,nrs->qnr", jnp.repeat(descent, 2, axis=1), transfer_maps[height], precision=PRECISE
        )
        descent = descent + local_couplings[height]
    far_field = jnp.einsum("qbr,bpr->qbp", descent, leaf_basis, precision=PRECISE).reshape(
        rows_here, BOXES_DEV * P_SIZE
    )
    return near_field + far_field + NUGGET * probes


def solution(mesh):
    in_specs = (
        P("probe", "boxes"),
        P(None, "boxes"),
        P("boxes", None),
        P(None, "boxes"),
        P(None, "boxes"),
        P(),
        P("boxes", None),
    )
    out_specs = P("probe", "boxes")
    return jax.shard_map(body, mesh=mesh, in_specs=in_specs, out_specs=out_specs, check_vma=False)
```

```python
import functools

import jax
import jax.numpy as jnp
from jax import lax
from jax.experimental import pallas as pl
from jax.experimental.pallas import tpu as pltpu
from jax.sharding import PartitionSpec as P

BOXES_DEV = 32
P_SIZE = 256
R = 64
W = 3
INNER_DEV = 30


SHARPNESS = 0.05
NUGGET = 1.0
PRECISE = lax.Precision.HIGHEST
MESH = pl.DeviceIdType.MESH


def halo_kernel(to_right, to_left, from_left, from_right, left_slot, right_slot, send_sems, recv_sems):
    me = lax.axis_index("boxes")
    size = lax.axis_size("boxes")
    probe = lax.axis_index("probe")
    right = lax.rem(me + 1, size)
    left = lax.rem(me + size - 1, size)
    barrier = pltpu.get_barrier_semaphore()
    for neighbour in (left, right):
        pl.semaphore_signal(barrier, inc=1, device_id=(neighbour, probe), device_id_type=MESH)
    pl.semaphore_wait(barrier, 2)
    rightward = pltpu.make_async_remote_copy(
        src_ref=to_right,
        dst_ref=left_slot,
        send_sem=send_sems.at[0],
        recv_sem=recv_sems.at[0],
        device_id=(right, probe),
        device_id_type=MESH,
    )
    leftward = pltpu.make_async_remote_copy(
        src_ref=to_left,
        dst_ref=right_slot,
        send_sem=send_sems.at[1],
        recv_sem=recv_sems.at[1],
        device_id=(left, probe),
        device_id_type=MESH,
    )
    rightward.start()
    leftward.start()
    rightward.wait()
    leftward.wait()
    from_left[...] = left_slot[...]
    from_right[...] = right_slot[...]


def exchange_halo(to_right, to_left):
    shape = jax.ShapeDtypeStruct(to_right.shape, to_right.dtype)
    vmem = pl.BlockSpec(memory_space=pltpu.VMEM)
    return pl.pallas_call(
        halo_kernel,
        out_shape=(shape, shape),
        in_specs=[vmem, vmem],
        out_specs=(vmem, vmem),
        scratch_shapes=[
            pltpu.VMEM(to_right.shape, to_right.dtype),
            pltpu.VMEM(to_right.shape, to_right.dtype),
            pltpu.SemaphoreType.DMA((2,)),
            pltpu.SemaphoreType.DMA((2,)),
        ],
        compiler_params=pltpu.CompilerParams(collective_id=0, has_side_effects=True),
    )(to_right, to_left)

def kernel_matrix(left_points, right_points, kernel_scale):
    distance_sq = (left_points[0][..., :, None] - right_points[0][..., None, :]) ** 2
    distance_sq = distance_sq + (left_points[1][..., :, None] - right_points[1][..., None, :]) ** 2
    distance_sq = distance_sq + (left_points[2][..., :, None] - right_points[2][..., None, :]) ** 2
    return 1.0 / (1.0 + kernel_scale * distance_sq)


def interpolation(left_points, right_points, kernel_scale):
    values = kernel_matrix(left_points, right_points, kernel_scale)
    return values / jnp.sum(values, axis=-1, keepdims=True)


def near_kernel(slots, halo, source_ref, probes_ref, coords_ref, target_ref, out_ref):
    box = pl.program_id(0)
    boxes = pl.num_programs(0)
    size = target_ref.shape[0]
    target_x = jnp.broadcast_to(target_ref[:, 0:1], (size, size))
    target_y = jnp.broadcast_to(target_ref[:, 1:2], (size, size))
    target_z = jnp.broadcast_to(target_ref[:, 2:3], (size, size))
    here = box + halo
    columns = pl.ds(pl.multiple_of(box * size, size), size)

    def block(tile):
        near = coords_ref[tile]
        distance_sq = (near[0:1, :] - target_x) ** 2
        distance_sq = distance_sq + (near[1:2, :] - target_y) ** 2
        distance_sq = distance_sq + (near[2:3, :] - target_z) ** 2
        return 1.0 / (1.0 + distance_sq)

    def gather_into(tile, kernel_block):
        out_ref[:, columns] += lax.dot_general(
            probes_ref[tile], kernel_block, (((1,), (1,)), ((), ())),
            precision=lax.Precision.HIGH, preferred_element_type=jnp.float32,
        )

    @pl.when(box == 0)
    def _():
        out_ref[...] = jnp.zeros_like(out_ref)
        gather_into(here - 1, block(here - 1))

    half = size // 2
    own = coords_ref[here]
    own_probes = probes_ref[here]

    def quarter(rows, cols):
        distance_sq = (own[0:1, cols] - target_x[rows, cols]) ** 2
        distance_sq = distance_sq + (own[1:2, cols] - target_y[rows, cols]) ** 2
        distance_sq = distance_sq + (own[2:3, cols] - target_z[rows, cols]) ** 2
        return 1.0 / (1.0 + distance_sq)

    low, high = slice(0, half), slice(half, size)
    upper_left = quarter(low, low)
    upper_right = quarter(low, high)
    lower_right = quarter(high, high)

    def side(probe_part, kernel_part):
        return lax.dot_general(
            probe_part, kernel_part, (((1,), (1,)), ((), ())),
            precision=lax.Precision.HIGH, preferred_element_type=jnp.float32,
        )

    first = pl.ds(pl.multiple_of(box * size, size), half)
    second = pl.ds(pl.multiple_of(box * size + half, half), half)
    out_ref[:, first] += side(own_probes[:, low], upper_left) + side(own_probes[:, high], upper_right)
    out_ref[:, second] += jnp.dot(
        own_probes[:, low], upper_right, precision=lax.Precision.HIGH,
        preferred_element_type=jnp.float32,
    ) + side(own_probes[:, high], lower_right)
    pair_block = block(here + 1)
    gather_into(here + 1, pair_block)

    @pl.when(box < boxes - 1)
    def _():
        following = pl.ds(pl.multiple_of((box + 1) * size, size), size)
        out_ref[:, following] += jnp.dot(
            probes_ref[here], pair_block, precision=lax.Precision.HIGH,
            preferred_element_type=jnp.float32,
        )

    def lists(row, tile):
        found = source_ref[row * slots] == tile
        for k in range(1, slots):
            found = found | (source_ref[row * slots + k] == tile)
        return found

    even = lax.rem(box, 2) == 0
    shared = []
    for step, allowed in ((2, True), (3, even)):
        partner = jnp.minimum(box + step, boxes - 1)
        shared.append(
            allowed & (box + step < boxes) & lists(box, here + step) & lists(partner, here)
        )
    skipped = []
    for step, allowed in ((2, True), (3, jnp.logical_not(even))):
        partner = jnp.maximum(box - step, 0)
        skipped.append(
            allowed & (box - step >= 0) & lists(box, here - step) & lists(partner, here)
        )
    for step, flag in zip((2, 3), shared):

        @pl.when(flag)
        def _():
            kernel_block = block(here + step)
            gather_into(here + step, kernel_block)
            later = pl.ds(pl.multiple_of((box + step) * size, size), size)
            out_ref[:, later] += jnp.dot(
                probes_ref[here], kernel_block, precision=lax.Precision.HIGH,
                preferred_element_type=jnp.float32,
            )

    for slot in range(slots):
        source = source_ref[box * slots + slot]
        done = (source == here - 1) | (source == here) | (source == here + 1)
        done = done | ((source == here + 2) & shared[0]) | ((source == here + 3) & shared[1])
        done = done | ((source == here - 2) & skipped[0]) | ((source == here - 3) & skipped[1])

        @pl.when((source >= 0) & jnp.logical_not(done))
        def _():
            gather_into(source, block(source))


def near_field_call(slot_source, probe_tiles, coord_tiles, points, kernel_scale):
    tiles, rows, size = probe_tiles.shape
    boxes = points.shape[1] // size
    slots = slot_source.shape[0] // boxes
    stretch = kernel_scale**0.5
    return pl.pallas_call(
        functools.partial(near_kernel, slots, W),
        out_shape=jax.ShapeDtypeStruct((rows, boxes * size), jnp.float32),
        grid_spec=pltpu.PrefetchScalarGridSpec(
            num_scalar_prefetch=1,
            grid=(boxes,),
            in_specs=[
                pl.BlockSpec((tiles, rows, size), lambda b, s: (0, 0, 0)),
                pl.BlockSpec((tiles, 3, size), lambda b, s: (0, 0, 0)),
                pl.BlockSpec((size, 3), lambda b, s: (b, 0)),
            ],
            out_specs=pl.BlockSpec((rows, boxes * size), lambda b, s: (0, 0)),
        ),
        compiler_params=pltpu.CompilerParams(dimension_semantics=("arbitrary",)),
        cost_estimate=pl.CostEstimate(
            flops=boxes * slots * size * size * (2 * rows + 12),
            transcendentals=0,
            bytes_accessed=4 * (probe_tiles.size + coord_tiles.size + 2 * rows * boxes * size),
        ),
    )(slot_source, probe_tiles, coord_tiles * stretch, points.T * stretch)


def body(probes, points, near_list, leaf_proxy, inner_proxy, top_proxy, far_list):
    groups = lax.axis_size("boxes")
    device = lax.axis_index("boxes")
    boxes_all = BOXES_DEV * groups
    kernel_scale = SHARPNESS * boxes_all
    rows_here = probes.shape[0]
    local_depth = BOXES_DEV.bit_length() - 1
    tree_depth = groups.bit_length() - 1
    live_slot = near_list >= 0
    slot_weight = live_slot.astype(jnp.float32)
    where_in = jnp.where(live_slot, (near_list - device * BOXES_DEV + W + boxes_all) % boxes_all, 0)
    box_points = points.reshape(3, BOXES_DEV, P_SIZE)
    probe_tiles = probes.reshape(rows_here, BOXES_DEV, P_SIZE)
    leaf_points = leaf_proxy.reshape(3, BOXES_DEV, R)
    leaf_basis = interpolation(box_points, leaf_points, kernel_scale)
    inner_points = inner_proxy.reshape(3, INNER_DEV, R)
    top_points = top_proxy.reshape(3, top_proxy.shape[1] // R, R)

    def node_proxy(height, node_index):
        offset = 2 * groups - 2 * (groups >> height)
        return lax.dynamic_slice_in_dim(top_points, offset + node_index, 1, 1)

    proxies = [leaf_points]
    for height in range(1, local_depth):
        offset = BOXES_DEV - (BOXES_DEV >> height - 1)
        number = BOXES_DEV >> height
        proxies.append(inner_points[:, offset : offset + number, :])
    proxies.append(node_proxy(0, device))
    level_moments = [jnp.einsum("qbp,bpr->qbr", probe_tiles, leaf_basis, precision=PRECISE)]
    transfer_maps = []
    for height in range(local_depth):
        interp_map = interpolation(
            proxies[height], jnp.repeat(proxies[height + 1], 2, axis=1), kernel_scale
        )
        transfer_maps.append(interp_map)
        lifted = jnp.einsum("qnr,nrs->qns", level_moments[-1], interp_map, precision=PRECISE)
        level_moments.append(lifted.reshape(rows_here, -1, 2, R).sum(axis=2))
    pyramid = jnp.concatenate(
        [
            jnp.concatenate(level_moments[:local_depth], axis=1),
            jnp.concatenate([leaf_points, inner_points], axis=1),
        ],
        axis=0,
    )
    pyramid_nodes = pyramid.shape[1]
    stacked = jnp.concatenate([probes, points], axis=0)
    width = W * P_SIZE
    flat_pyramid = pyramid.reshape(rows_here + 3, -1)
    from_left, from_right = exchange_halo(
        jnp.concatenate([stacked[:, -width:], flat_pyramid], axis=1),
        jnp.concatenate([stacked[:, :width], flat_pyramid], axis=1),
    )
    extended = jnp.concatenate([from_left[:, :width], stacked, from_right[:, :width]], axis=1)
    extended = extended.reshape(rows_here + 3, BOXES_DEV + 2 * W, P_SIZE)
    spread = jnp.concatenate(
        [
            from_left[:, width:].reshape(pyramid.shape),
            pyramid,
            from_right[:, width:].reshape(pyramid.shape),
        ],
        axis=1,
    )
    slot_source = jnp.where(live_slot, jnp.clip(where_in, 0, BOXES_DEV + 2 * W - 1), -1)
    near_field = near_field_call(
        slot_source.reshape(-1).astype(jnp.int32),
        jnp.moveaxis(extended[:rows_here], 1, 0),
        jnp.moveaxis(extended[rows_here:], 0, 1),
        points,
        kernel_scale,
    )
    index_parts, target_parts, mask_parts = [], [], []
    for height in range(local_depth):
        count = BOXES_DEV >> height
        start = 0 if height == 0 else 2 * BOXES_DEV - (BOXES_DEV >> height - 1)
        if height == 0:
            live_far = far_list >= 0
            view_ids = [
                jnp.where(
                    live_far[:, slot],
                    (far_list[:, slot] - device * BOXES_DEV + BOXES_DEV + boxes_all) % boxes_all,
                    0,
                )
                for slot in range(3)
            ]
            mask_parts += [live_far[:, slot].astype(jnp.float32) for slot in range(3)]
        else:
            node = jnp.arange(count, dtype=jnp.int32)
            third = jnp.where(node % 2 == 0, node + 3, node - 3)
            view_ids = [node - 2 + count, node + 2 + count, third + count]
            mask_parts += [jnp.ones((count,), jnp.float32)] * 3
        for view_id in view_ids:
            index_parts.append(view_id // count * pyramid_nodes + start + view_id % count)
            target_parts.append(proxies[height])
    picked = jnp.take(spread, jnp.concatenate(index_parts), axis=1)
    kernel_block = kernel_matrix(picked[rows_here:], jnp.concatenate(target_parts, axis=1), kernel_scale)
    source_moment = picked[:rows_here] * jnp.concatenate(mask_parts)[None, :, None]
    contributions = jnp.einsum("qnr,nrs->qns", source_moment, kernel_block, precision=PRECISE)
    local_couplings = []
    first = 0
    for height in range(local_depth):
        count = BOXES_DEV >> height
        part = contributions[:, first : first + 3 * count, :]
        local_couplings.append(part.reshape(rows_here, 3, count, R).sum(axis=1))
        first += 3 * count

    top_levels = tree_depth - 1
    level_points = []
    for height in range(top_levels):
        offset = 2 * groups - 2 * (groups >> height)
        level_points.append(top_points[:, offset : offset + (groups >> height), :])
    own_edges = []
    for height in range(top_levels - 1):
        own_edges.append(
            interpolation(
                lax.dynamic_slice_in_dim(level_points[height], device // 2**height, 1, 1),
                lax.dynamic_slice_in_dim(level_points[height + 1], device // 2 ** (height + 1), 1, 1),
                kernel_scale,
            )
        )
    path_moments = [level_moments[local_depth]]
    for height in range(top_levels - 1):
        path_moments.append(
            jnp.einsum("qnr,nrs->qns", path_moments[-1], own_edges[height], precision=PRECISE)
        )
    gathered = lax.all_gather(jnp.concatenate(path_moments, axis=1), "boxes", axis=0)
    top_moments, top_sources, top_targets, top_slots = [], [], [], []
    for height in range(top_levels):
        number = groups >> height
        node = device // 2**height
        level_sums = gathered[:, :, height, :].reshape(number, 2**height, rows_here, R).sum(axis=1)
        third = jnp.where(node % 2 == 0, node + 3, node - 3) % number
        if number > 4:
            source_ids = [(node - 2) % number, (node + 2) % number, third]
        else:
            source_ids = [(node + 2) % number]
        top_slots.append(len(source_ids))
        for source in source_ids:
            top_moments.append(lax.dynamic_index_in_dim(level_sums, source, 0, keepdims=True))
            top_sources.append(lax.dynamic_slice_in_dim(level_points[height], source, 1, 1))
            top_targets.append(lax.dynamic_slice_in_dim(level_points[height], node, 1, 1))
    kernel_block = kernel_matrix(
        jnp.concatenate(top_sources, axis=1), jnp.concatenate(top_targets, axis=1), kernel_scale
    )
    contributions = jnp.einsum(
        "nqr,nrs->qns", jnp.concatenate(top_moments, axis=0), kernel_block, precision=PRECISE
    )
    top_couplings = []
    first = 0
    for slots in top_slots:
        top_couplings.append(contributions[:, first : first + slots, :].sum(axis=1, keepdims=True))
        first += slots
    descent = top_couplings[-1]
    for height in range(top_levels - 2, -1, -1):
        descent = (
            jnp.einsum("qns,nrs->qnr", descent, own_edges[height], precision=PRECISE)
            + top_couplings[height]
        )
    for height in range(local_depth - 1, -1, -1):
        descent = jnp.einsum(
            "qns,nrs->qnr", jnp.repeat(descent, 2, axis=1), transfer_maps[height], precision=PRECISE
        )
        descent = descent + local_couplings[height]
    far_field = jnp.einsum("qbr,bpr->qbp", descent, leaf_basis, precision=PRECISE).reshape(
        rows_here, BOXES_DEV * P_SIZE
    )
    return near_field + far_field + NUGGET * probes


def solution(mesh):
    in_specs = (
        P("probe", "boxes"),
        P(None, "boxes"),
        P("boxes", None),
        P(None, "boxes"),
        P(None, "boxes"),
        P(),
        P("boxes", None),
    )
    out_specs = P("probe", "boxes")
    return jax.shard_map(body, mesh=mesh, in_specs=in_specs, out_specs=out_specs, check_vma=False)
```

```python
import functools

import jax
import jax.numpy as jnp
from jax import lax
from jax.experimental import pallas as pl
from jax.experimental.pallas import tpu as pltpu
from jax.sharding import PartitionSpec as P

BOXES_DEV = 32
P_SIZE = 256
R = 64
W = 3
INNER_DEV = 30


SHARPNESS = 0.05
NUGGET = 1.0
PRECISE = lax.Precision.HIGHEST
TAIL_PRECISION = lax.Precision.HIGH
MESH = pl.DeviceIdType.MESH


def halo_kernel(to_right, to_left, from_left, from_right, left_slot, right_slot, send_sems, recv_sems):
    me = lax.axis_index("boxes")
    size = lax.axis_size("boxes")
    probe = lax.axis_index("probe")
    right = lax.rem(me + 1, size)
    left = lax.rem(me + size - 1, size)
    barrier = pltpu.get_barrier_semaphore()
    for neighbour in (left, right):
        pl.semaphore_signal(barrier, inc=1, device_id=(neighbour, probe), device_id_type=MESH)
    pl.semaphore_wait(barrier, 2)
    rightward = pltpu.make_async_remote_copy(
        src_ref=to_right,
        dst_ref=left_slot,
        send_sem=send_sems.at[0],
        recv_sem=recv_sems.at[0],
        device_id=(right, probe),
        device_id_type=MESH,
    )
    leftward = pltpu.make_async_remote_copy(
        src_ref=to_left,
        dst_ref=right_slot,
        send_sem=send_sems.at[1],
        recv_sem=recv_sems.at[1],
        device_id=(left, probe),
        device_id_type=MESH,
    )
    rightward.start()
    leftward.start()
    rightward.wait()
    leftward.wait()
    from_left[...] = left_slot[...]
    from_right[...] = right_slot[...]


def exchange_halo(to_right, to_left):
    shape = jax.ShapeDtypeStruct(to_right.shape, to_right.dtype)
    vmem = pl.BlockSpec(memory_space=pltpu.VMEM)
    return pl.pallas_call(
        halo_kernel,
        out_shape=(shape, shape),
        in_specs=[vmem, vmem],
        out_specs=(vmem, vmem),
        scratch_shapes=[
            pltpu.VMEM(to_right.shape, to_right.dtype),
            pltpu.VMEM(to_right.shape, to_right.dtype),
            pltpu.SemaphoreType.DMA((2,)),
            pltpu.SemaphoreType.DMA((2,)),
        ],
        compiler_params=pltpu.CompilerParams(collective_id=0, has_side_effects=True),
    )(to_right, to_left)

def kernel_matrix(left_points, right_points, kernel_scale):
    distance_sq = (left_points[0][..., :, None] - right_points[0][..., None, :]) ** 2
    distance_sq = distance_sq + (left_points[1][..., :, None] - right_points[1][..., None, :]) ** 2
    distance_sq = distance_sq + (left_points[2][..., :, None] - right_points[2][..., None, :]) ** 2
    return 1.0 / (1.0 + kernel_scale * distance_sq)


def interpolation(left_points, right_points, kernel_scale):
    values = kernel_matrix(left_points, right_points, kernel_scale)
    return values / jnp.sum(values, axis=-1, keepdims=True)


def near_kernel(slots, halo, source_ref, probes_ref, coords_ref, target_ref, out_ref):
    box = pl.program_id(0)
    boxes = pl.num_programs(0)
    size = target_ref.shape[0]
    target_x = jnp.broadcast_to(target_ref[:, 0:1], (size, size))
    target_y = jnp.broadcast_to(target_ref[:, 1:2], (size, size))
    target_z = jnp.broadcast_to(target_ref[:, 2:3], (size, size))
    here = box + halo
    columns = pl.ds(pl.multiple_of(box * size, size), size)

    def block(tile):
        near = coords_ref[tile]
        distance_sq = (near[0:1, :] - target_x) ** 2
        distance_sq = distance_sq + (near[1:2, :] - target_y) ** 2
        distance_sq = distance_sq + (near[2:3, :] - target_z) ** 2
        return 1.0 / (1.0 + distance_sq)

    def gather_into(tile, kernel_block):
        out_ref[:, columns] += lax.dot_general(
            probes_ref[tile], kernel_block, (((1,), (1,)), ((), ())),
            precision=lax.Precision.HIGH, preferred_element_type=jnp.float32,
        )

    @pl.when(box == 0)
    def _():
        out_ref[...] = jnp.zeros_like(out_ref)
        gather_into(here - 1, block(here - 1))

    gather_into(here, block(here))
    pair_block = block(here + 1)
    gather_into(here + 1, pair_block)

    @pl.when(box < boxes - 1)
    def _():
        following = pl.ds(pl.multiple_of((box + 1) * size, size), size)
        out_ref[:, following] += jnp.dot(
            probes_ref[here], pair_block, precision=lax.Precision.HIGH,
            preferred_element_type=jnp.float32,
        )

    def lists(row, tile):
        found = source_ref[row * slots] == tile
        for k in range(1, slots):
            found = found | (source_ref[row * slots + k] == tile)
        return found

    even = lax.rem(box, 2) == 0
    shared = []
    for step, allowed in ((2, True), (3, even)):
        partner = jnp.minimum(box + step, boxes - 1)
        shared.append(
            allowed & (box + step < boxes) & lists(box, here + step) & lists(partner, here)
        )
    skipped = []
    for step, allowed in ((2, True), (3, jnp.logical_not(even))):
        partner = jnp.maximum(box - step, 0)
        skipped.append(
            allowed & (box - step >= 0) & lists(box, here - step) & lists(partner, here)
        )
    for step, flag in zip((2, 3), shared):

        @pl.when(flag)
        def _():
            kernel_block = block(here + step)
            gather_into(here + step, kernel_block)
            later = pl.ds(pl.multiple_of((box + step) * size, size), size)
            out_ref[:, later] += jnp.dot(
                probes_ref[here], kernel_block, precision=lax.Precision.HIGH,
                preferred_element_type=jnp.float32,
            )

    for slot in range(slots):
        source = source_ref[box * slots + slot]
        done = (source == here - 1) | (source == here) | (source == here + 1)
        done = done | ((source == here + 2) & shared[0]) | ((source == here + 3) & shared[1])
        done = done | ((source == here - 2) & skipped[0]) | ((source == here - 3) & skipped[1])

        @pl.when((source >= 0) & jnp.logical_not(done))
        def _():
            gather_into(source, block(source))


def near_field_call(slot_source, probe_tiles, coord_tiles, points, kernel_scale):
    tiles, rows, size = probe_tiles.shape
    boxes = points.shape[1] // size
    slots = slot_source.shape[0] // boxes
    stretch = kernel_scale**0.5
    return pl.pallas_call(
        functools.partial(near_kernel, slots, W),
        out_shape=jax.ShapeDtypeStruct((rows, boxes * size), jnp.float32),
        grid_spec=pltpu.PrefetchScalarGridSpec(
            num_scalar_prefetch=1,
            grid=(boxes,),
            in_specs=[
                pl.BlockSpec((tiles, rows, size), lambda b, s: (0, 0, 0)),
                pl.BlockSpec((tiles, 3, size), lambda b, s: (0, 0, 0)),
                pl.BlockSpec((size, 3), lambda b, s: (b, 0)),
            ],
            out_specs=pl.BlockSpec((rows, boxes * size), lambda b, s: (0, 0)),
        ),
        compiler_params=pltpu.CompilerParams(dimension_semantics=("arbitrary",)),
        cost_estimate=pl.CostEstimate(
            flops=boxes * slots * size * size * (2 * rows + 12),
            transcendentals=0,
            bytes_accessed=4 * (probe_tiles.size + coord_tiles.size + 2 * rows * boxes * size),
        ),
    )(slot_source, probe_tiles, coord_tiles * stretch, points.T * stretch)


def body(probes, points, near_list, leaf_proxy, inner_proxy, top_proxy, far_list):
    groups = lax.axis_size("boxes")
    device = lax.axis_index("boxes")
    boxes_all = BOXES_DEV * groups
    kernel_scale = SHARPNESS * boxes_all
    rows_here = probes.shape[0]
    local_depth = BOXES_DEV.bit_length() - 1
    tree_depth = groups.bit_length() - 1
    live_slot = near_list >= 0
    slot_weight = live_slot.astype(jnp.float32)
    where_in = jnp.where(live_slot, (near_list - device * BOXES_DEV + W + boxes_all) % boxes_all, 0)
    box_points = points.reshape(3, BOXES_DEV, P_SIZE)
    probe_tiles = probes.reshape(rows_here, BOXES_DEV, P_SIZE)
    leaf_points = leaf_proxy.reshape(3, BOXES_DEV, R)
    leaf_basis = interpolation(box_points, leaf_points, kernel_scale)
    inner_points = inner_proxy.reshape(3, INNER_DEV, R)
    top_points = top_proxy.reshape(3, top_proxy.shape[1] // R, R)

    def node_proxy(height, node_index):
        offset = 2 * groups - 2 * (groups >> height)
        return lax.dynamic_slice_in_dim(top_points, offset + node_index, 1, 1)

    proxies = [leaf_points]
    for height in range(1, local_depth):
        offset = BOXES_DEV - (BOXES_DEV >> height - 1)
        number = BOXES_DEV >> height
        proxies.append(inner_points[:, offset : offset + number, :])
    proxies.append(node_proxy(0, device))
    level_moments = [jnp.einsum("qbp,bpr->qbr", probe_tiles, leaf_basis, precision=PRECISE)]
    transfer_maps = []
    for height in range(local_depth):
        interp_map = interpolation(
            proxies[height], jnp.repeat(proxies[height + 1], 2, axis=1), kernel_scale
        )
        transfer_maps.append(interp_map)
        lifted = jnp.einsum("qnr,nrs->qns", level_moments[-1], interp_map, precision=PRECISE)
        level_moments.append(lifted.reshape(rows_here, -1, 2, R).sum(axis=2))
    pyramid = jnp.concatenate(
        [
            jnp.concatenate(level_moments[:local_depth], axis=1),
            jnp.concatenate([leaf_points, inner_points], axis=1),
        ],
        axis=0,
    )
    pyramid_nodes = pyramid.shape[1]
    stacked = jnp.concatenate([probes, points], axis=0)
    width = W * P_SIZE
    flat_pyramid = pyramid.reshape(rows_here + 3, -1)
    from_left, from_right = exchange_halo(
        jnp.concatenate([stacked[:, -width:], flat_pyramid], axis=1),
        jnp.concatenate([stacked[:, :width], flat_pyramid], axis=1),
    )
    extended = jnp.concatenate([from_left[:, :width], stacked, from_right[:, :width]], axis=1)
    extended = extended.reshape(rows_here + 3, BOXES_DEV + 2 * W, P_SIZE)
    spread = jnp.concatenate(
        [
            from_left[:, width:].reshape(pyramid.shape),
            pyramid,
            from_right[:, width:].reshape(pyramid.shape),
        ],
        axis=1,
    )
    slot_source = jnp.where(live_slot, jnp.clip(where_in, 0, BOXES_DEV + 2 * W - 1), -1)
    near_field = near_field_call(
        slot_source.reshape(-1).astype(jnp.int32),
        jnp.moveaxis(extended[:rows_here], 1, 0),
        jnp.moveaxis(extended[rows_here:], 0, 1),
        points,
        kernel_scale,
    )
    index_parts, target_parts, mask_parts = [], [], []
    for height in range(local_depth):
        count = BOXES_DEV >> height
        start = 0 if height == 0 else 2 * BOXES_DEV - (BOXES_DEV >> height - 1)
        if height == 0:
            live_far = far_list >= 0
            view_ids = [
                jnp.where(
                    live_far[:, slot],
                    (far_list[:, slot] - device * BOXES_DEV + BOXES_DEV + boxes_all) % boxes_all,
                    0,
                )
                for slot in range(3)
            ]
            mask_parts += [live_far[:, slot].astype(jnp.float32) for slot in range(3)]
        else:
            node = jnp.arange(count, dtype=jnp.int32)
            third = jnp.where(node % 2 == 0, node + 3, node - 3)
            view_ids = [node - 2 + count, node + 2 + count, third + count]
            mask_parts += [jnp.ones((count,), jnp.float32)] * 3
        for view_id in view_ids:
            index_parts.append(view_id // count * pyramid_nodes + start + view_id % count)
            target_parts.append(proxies[height])
    picked = jnp.take(spread, jnp.concatenate(index_parts), axis=1)
    kernel_block = kernel_matrix(picked[rows_here:], jnp.concatenate(target_parts, axis=1), kernel_scale)
    source_moment = picked[:rows_here] * jnp.concatenate(mask_parts)[None, :, None]
    contributions = jnp.einsum("qnr,nrs->qns", source_moment, kernel_block, precision=PRECISE)
    local_couplings = []
    first = 0
    for height in range(local_depth):
        count = BOXES_DEV >> height
        part = contributions[:, first : first + 3 * count, :]
        local_couplings.append(part.reshape(rows_here, 3, count, R).sum(axis=1))
        first += 3 * count

    top_levels = tree_depth - 1
    level_points = []
    for height in range(top_levels):
        offset = 2 * groups - 2 * (groups >> height)
        level_points.append(top_points[:, offset : offset + (groups >> height), :])
    own_edges = []
    for height in range(top_levels - 1):
        own_edges.append(
            interpolation(
                lax.dynamic_slice_in_dim(level_points[height], device // 2**height, 1, 1),
                lax.dynamic_slice_in_dim(level_points[height + 1], device // 2 ** (height + 1), 1, 1),
                kernel_scale,
            )
        )
    path_moments = [level_moments[local_depth]]
    for height in range(top_levels - 1):
        path_moments.append(
            jnp.einsum("qnr,nrs->qns", path_moments[-1], own_edges[height], precision=PRECISE)
        )
    gathered = lax.all_gather(jnp.concatenate(path_moments, axis=1), "boxes", axis=0)
    top_moments, top_sources, top_targets, top_slots = [], [], [], []
    for height in range(top_levels):
        number = groups >> height
        node = device // 2**height
        level_sums = gathered[:, :, height, :].reshape(number, 2**height, rows_here, R).sum(axis=1)
        third = jnp.where(node % 2 == 0, node + 3, node - 3) % number
        if number > 4:
            source_ids = [(node - 2) % number, (node + 2) % number, third]
        else:
            source_ids = [(node + 2) % number]
        top_slots.append(len(source_ids))
        for source in source_ids:
            top_moments.append(lax.dynamic_index_in_dim(level_sums, source, 0, keepdims=True))
            top_sources.append(lax.dynamic_slice_in_dim(level_points[height], source, 1, 1))
            top_targets.append(lax.dynamic_slice_in_dim(level_points[height], node, 1, 1))
    kernel_block = kernel_matrix(
        jnp.concatenate(top_sources, axis=1), jnp.concatenate(top_targets, axis=1), kernel_scale
    )
    contributions = jnp.einsum(
        "nqr,nrs->qns", jnp.concatenate(top_moments, axis=0), kernel_block, precision=TAIL_PRECISION
    )
    top_couplings = []
    first = 0
    for slots in top_slots:
        top_couplings.append(contributions[:, first : first + slots, :].sum(axis=1, keepdims=True))
        first += slots
    descent = top_couplings[-1]
    for height in range(top_levels - 2, -1, -1):
        descent = (
            jnp.einsum("qns,nrs->qnr", descent, own_edges[height], precision=TAIL_PRECISION)
            + top_couplings[height]
        )
    for height in range(local_depth - 1, -1, -1):
        descent = jnp.einsum(
            "qns,nrs->qnr", jnp.repeat(descent, 2, axis=1), transfer_maps[height], precision=TAIL_PRECISION
        )
        descent = descent + local_couplings[height]
    far_field = jnp.einsum("qbr,bpr->qbp", descent, leaf_basis, precision=TAIL_PRECISION).reshape(
        rows_here, BOXES_DEV * P_SIZE
    )
    return near_field + far_field + NUGGET * probes


def solution(mesh):
    in_specs = (
        P("probe", "boxes"),
        P(None, "boxes"),
        P("boxes", None),
        P(None, "boxes"),
        P(None, "boxes"),
        P(),
        P("boxes", None),
    )
    out_specs = P("probe", "boxes")
    return jax.shard_map(body, mesh=mesh, in_specs=in_specs, out_specs=out_specs, check_vma=False)
```

```python
import functools

import jax
import jax.numpy as jnp
from jax import lax
from jax.experimental import pallas as pl
from jax.experimental.pallas import tpu as pltpu
from jax.sharding import PartitionSpec as P

BOXES_DEV = 32
P_SIZE = 256
R = 64
W = 3
INNER_DEV = 30


SHARPNESS = 0.05
NUGGET = 1.0
PRECISE = lax.Precision.HIGHEST
TAIL_PRECISION = lax.Precision.HIGH
MESH = pl.DeviceIdType.MESH


def halo_kernel(to_right, to_left, from_left, from_right, left_slot, right_slot, send_sems, recv_sems):
    me = lax.axis_index("boxes")
    size = lax.axis_size("boxes")
    probe = lax.axis_index("probe")
    right = lax.rem(me + 1, size)
    left = lax.rem(me + size - 1, size)
    barrier = pltpu.get_barrier_semaphore()
    for neighbour in (left, right):
        pl.semaphore_signal(barrier, inc=1, device_id=(neighbour, probe), device_id_type=MESH)
    pl.semaphore_wait(barrier, 2)
    rightward = pltpu.make_async_remote_copy(
        src_ref=to_right,
        dst_ref=left_slot,
        send_sem=send_sems.at[0],
        recv_sem=recv_sems.at[0],
        device_id=(right, probe),
        device_id_type=MESH,
    )
    leftward = pltpu.make_async_remote_copy(
        src_ref=to_left,
        dst_ref=right_slot,
        send_sem=send_sems.at[1],
        recv_sem=recv_sems.at[1],
        device_id=(left, probe),
        device_id_type=MESH,
    )
    rightward.start()
    leftward.start()
    rightward.wait()
    leftward.wait()
    from_left[...] = left_slot[...]
    from_right[...] = right_slot[...]


def exchange_halo(to_right, to_left):
    shape = jax.ShapeDtypeStruct(to_right.shape, to_right.dtype)
    vmem = pl.BlockSpec(memory_space=pltpu.VMEM)
    return pl.pallas_call(
        halo_kernel,
        out_shape=(shape, shape),
        in_specs=[vmem, vmem],
        out_specs=(vmem, vmem),
        scratch_shapes=[
            pltpu.VMEM(to_right.shape, to_right.dtype),
            pltpu.VMEM(to_right.shape, to_right.dtype),
            pltpu.SemaphoreType.DMA((2,)),
            pltpu.SemaphoreType.DMA((2,)),
        ],
        compiler_params=pltpu.CompilerParams(collective_id=0, has_side_effects=True),
    )(to_right, to_left)

def kernel_matrix(left_points, right_points, kernel_scale):
    distance_sq = (left_points[0][..., :, None] - right_points[0][..., None, :]) ** 2
    distance_sq = distance_sq + (left_points[1][..., :, None] - right_points[1][..., None, :]) ** 2
    distance_sq = distance_sq + (left_points[2][..., :, None] - right_points[2][..., None, :]) ** 2
    return 1.0 / (1.0 + kernel_scale * distance_sq)


def interpolation(left_points, right_points, kernel_scale):
    values = kernel_matrix(left_points, right_points, kernel_scale)
    return values / jnp.sum(values, axis=-1, keepdims=True)


def near_kernel(slots, halo, source_ref, probes_ref, coords_ref, target_ref, out_ref):
    box = pl.program_id(0)
    boxes = pl.num_programs(0)
    size = target_ref.shape[0]
    target_x = jnp.broadcast_to(target_ref[:, 0:1], (size, size))
    target_y = jnp.broadcast_to(target_ref[:, 1:2], (size, size))
    target_z = jnp.broadcast_to(target_ref[:, 2:3], (size, size))
    here = box + halo
    columns = pl.ds(pl.multiple_of(box * size, size), size)

    def block(tile):
        near = coords_ref[tile]
        distance_sq = (near[0:1, :] - target_x) ** 2
        distance_sq = distance_sq + (near[1:2, :] - target_y) ** 2
        distance_sq = distance_sq + (near[2:3, :] - target_z) ** 2
        return 1.0 / (1.0 + distance_sq)

    def gather_into(tile, kernel_block):
        out_ref[:, columns] += lax.dot_general(
            probes_ref[tile], kernel_block, (((1,), (1,)), ((), ())),
            precision=lax.Precision.HIGH, preferred_element_type=jnp.float32,
        )

    @pl.when(box == 0)
    def _():
        out_ref[...] = jnp.zeros_like(out_ref)
        gather_into(here - 1, block(here - 1))

    gather_into(here, block(here))
    pair_block = block(here + 1)
    gather_into(here + 1, pair_block)

    @pl.when(box < boxes - 1)
    def _():
        following = pl.ds(pl.multiple_of((box + 1) * size, size), size)
        out_ref[:, following] += jnp.dot(
            probes_ref[here], pair_block, precision=lax.Precision.HIGH,
            preferred_element_type=jnp.float32,
        )

    def lists(row, tile):
        found = source_ref[row * slots] == tile
        for k in range(1, slots):
            found = found | (source_ref[row * slots + k] == tile)
        return found

    even = lax.rem(box, 2) == 0
    shared = []
    for step, allowed in ((2, True), (3, even)):
        partner = jnp.minimum(box + step, boxes - 1)
        shared.append(
            allowed & (box + step < boxes) & lists(box, here + step) & lists(partner, here)
        )
    skipped = []
    for step, allowed in ((2, True), (3, jnp.logical_not(even))):
        partner = jnp.maximum(box - step, 0)
        skipped.append(
            allowed & (box - step >= 0) & lists(box, here - step) & lists(partner, here)
        )
    for step, flag in zip((2, 3), shared):

        @pl.when(flag)
        def _():
            kernel_block = block(here + step)
            gather_into(here + step, kernel_block)
            later = pl.ds(pl.multiple_of((box + step) * size, size), size)
            out_ref[:, later] += jnp.dot(
                probes_ref[here], kernel_block, precision=lax.Precision.HIGH,
                preferred_element_type=jnp.float32,
            )

    for slot in range(slots):
        source = source_ref[box * slots + slot]
        done = (source == here - 1) | (source == here) | (source == here + 1)
        done = done | ((source == here + 2) & shared[0]) | ((source == here + 3) & shared[1])
        done = done | ((source == here - 2) & skipped[0]) | ((source == here - 3) & skipped[1])

        @pl.when((source >= 0) & jnp.logical_not(done))
        def _():
            gather_into(source, block(source))


def near_field_call(slot_source, probe_tiles, coord_tiles, points, kernel_scale):
    tiles, rows, size = probe_tiles.shape
    boxes = points.shape[1] // size
    slots = slot_source.shape[0] // boxes
    stretch = kernel_scale**0.5
    return pl.pallas_call(
        functools.partial(near_kernel, slots, W),
        out_shape=jax.ShapeDtypeStruct((rows, boxes * size), jnp.float32),
        grid_spec=pltpu.PrefetchScalarGridSpec(
            num_scalar_prefetch=1,
            grid=(boxes,),
            in_specs=[
                pl.BlockSpec((tiles, rows, size), lambda b, s: (0, 0, 0)),
                pl.BlockSpec((tiles, 3, size), lambda b, s: (0, 0, 0)),
                pl.BlockSpec((size, 3), lambda b, s: (b, 0)),
            ],
            out_specs=pl.BlockSpec((rows, boxes * size), lambda b, s: (0, 0)),
        ),
        compiler_params=pltpu.CompilerParams(dimension_semantics=("arbitrary",)),
        cost_estimate=pl.CostEstimate(
            flops=boxes * slots * size * size * (2 * rows + 12),
            transcendentals=0,
            bytes_accessed=4 * (probe_tiles.size + coord_tiles.size + 2 * rows * boxes * size),
        ),
    )(slot_source, probe_tiles, coord_tiles * stretch, points.T * stretch)


def body(probes, points, near_list, leaf_proxy, inner_proxy, top_proxy, far_list):
    groups = lax.axis_size("boxes")
    device = lax.axis_index("boxes")
    boxes_all = BOXES_DEV * groups
    kernel_scale = SHARPNESS * boxes_all
    rows_here = probes.shape[0]
    local_depth = BOXES_DEV.bit_length() - 1
    tree_depth = groups.bit_length() - 1
    live_slot = near_list >= 0
    slot_weight = live_slot.astype(jnp.float32)
    where_in = jnp.where(live_slot, (near_list - device * BOXES_DEV + W + boxes_all) % boxes_all, 0)
    box_points = points.reshape(3, BOXES_DEV, P_SIZE)
    probe_tiles = probes.reshape(rows_here, BOXES_DEV, P_SIZE)
    leaf_points = leaf_proxy.reshape(3, BOXES_DEV, R)
    leaf_basis = interpolation(box_points, leaf_points, kernel_scale)
    inner_points = inner_proxy.reshape(3, INNER_DEV, R)
    top_points = top_proxy.reshape(3, top_proxy.shape[1] // R, R)

    def node_proxy(height, node_index):
        offset = 2 * groups - 2 * (groups >> height)
        return lax.dynamic_slice_in_dim(top_points, offset + node_index, 1, 1)

    proxies = [leaf_points]
    for height in range(1, local_depth):
        offset = BOXES_DEV - (BOXES_DEV >> height - 1)
        number = BOXES_DEV >> height
        proxies.append(inner_points[:, offset : offset + number, :])
    proxies.append(node_proxy(0, device))
    level_moments = [jnp.einsum("qbp,bpr->qbr", probe_tiles, leaf_basis, precision=PRECISE)]
    transfer_maps = []
    for height in range(local_depth):
        interp_map = interpolation(
            proxies[height], jnp.repeat(proxies[height + 1], 2, axis=1), kernel_scale
        )
        transfer_maps.append(interp_map)
        lifted = jnp.einsum("qnr,nrs->qns", level_moments[-1], interp_map, precision=PRECISE)
        level_moments.append(lifted.reshape(rows_here, -1, 2, R).sum(axis=2))
    pyramid = jnp.concatenate(
        [
            jnp.concatenate(level_moments[:local_depth], axis=1),
            jnp.concatenate([leaf_points, inner_points], axis=1),
        ],
        axis=0,
    )
    pyramid_nodes = pyramid.shape[1]
    stacked = jnp.concatenate([probes, points], axis=0)
    width = W * P_SIZE
    flat_pyramid = pyramid.reshape(rows_here + 3, -1)
    from_left, from_right = exchange_halo(
        jnp.concatenate([stacked[:, -width:], flat_pyramid], axis=1),
        jnp.concatenate([stacked[:, :width], flat_pyramid], axis=1),
    )
    extended = jnp.concatenate([from_left[:, :width], stacked, from_right[:, :width]], axis=1)
    extended = extended.reshape(rows_here + 3, BOXES_DEV + 2 * W, P_SIZE)
    spread = jnp.concatenate(
        [
            from_left[:, width:].reshape(pyramid.shape),
            pyramid,
            from_right[:, width:].reshape(pyramid.shape),
        ],
        axis=1,
    )
    slot_source = jnp.where(live_slot, jnp.clip(where_in, 0, BOXES_DEV + 2 * W - 1), -1)
    near_field = near_field_call(
        slot_source.reshape(-1).astype(jnp.int32),
        jnp.moveaxis(extended[:rows_here], 1, 0),
        jnp.moveaxis(extended[rows_here:], 0, 1),
        points,
        kernel_scale,
    )
    index_parts, target_parts, mask_parts = [], [], []
    for height in range(local_depth):
        count = BOXES_DEV >> height
        start = 0 if height == 0 else 2 * BOXES_DEV - (BOXES_DEV >> height - 1)
        if height == 0:
            live_far = far_list >= 0
            view_ids = [
                jnp.where(
                    live_far[:, slot],
                    (far_list[:, slot] - device * BOXES_DEV + BOXES_DEV + boxes_all) % boxes_all,
                    0,
                )
                for slot in range(3)
            ]
            mask_parts += [live_far[:, slot].astype(jnp.float32) for slot in range(3)]
        else:
            node = jnp.arange(count, dtype=jnp.int32)
            third = jnp.where(node % 2 == 0, node + 3, node - 3)
            view_ids = [node - 2 + count, node + 2 + count, third + count]
            mask_parts += [jnp.ones((count,), jnp.float32)] * 3
        for view_id in view_ids:
            index_parts.append(view_id // count * pyramid_nodes + start + view_id % count)
            target_parts.append(proxies[height])
    picked = jnp.take(spread, jnp.concatenate(index_parts), axis=1)
    kernel_block = kernel_matrix(picked[rows_here:], jnp.concatenate(target_parts, axis=1), kernel_scale)
    source_moment = picked[:rows_here] * jnp.concatenate(mask_parts)[None, :, None]
    contributions = jnp.einsum("qnr,nrs->qns", source_moment, kernel_block, precision=TAIL_PRECISION)
    local_couplings = []
    first = 0
    for height in range(local_depth):
        count = BOXES_DEV >> height
        part = contributions[:, first : first + 3 * count, :]
        local_couplings.append(part.reshape(rows_here, 3, count, R).sum(axis=1))
        first += 3 * count

    top_levels = tree_depth - 1
    level_points = []
    for height in range(top_levels):
        offset = 2 * groups - 2 * (groups >> height)
        level_points.append(top_points[:, offset : offset + (groups >> height), :])
    own_edges = []
    for height in range(top_levels - 1):
        own_edges.append(
            interpolation(
                lax.dynamic_slice_in_dim(level_points[height], device // 2**height, 1, 1),
                lax.dynamic_slice_in_dim(level_points[height + 1], device // 2 ** (height + 1), 1, 1),
                kernel_scale,
            )
        )
    path_moments = [level_moments[local_depth]]
    for height in range(top_levels - 1):
        path_moments.append(
            jnp.einsum("qnr,nrs->qns", path_moments[-1], own_edges[height], precision=PRECISE)
        )
    gathered = lax.all_gather(jnp.concatenate(path_moments, axis=1), "boxes", axis=0)
    top_moments, top_sources, top_targets, top_slots = [], [], [], []
    for height in range(top_levels):
        number = groups >> height
        node = device // 2**height
        level_sums = gathered[:, :, height, :].reshape(number, 2**height, rows_here, R).sum(axis=1)
        third = jnp.where(node % 2 == 0, node + 3, node - 3) % number
        if number > 4:
            source_ids = [(node - 2) % number, (node + 2) % number, third]
        else:
            source_ids = [(node + 2) % number]
        top_slots.append(len(source_ids))
        for source in source_ids:
            top_moments.append(lax.dynamic_index_in_dim(level_sums, source, 0, keepdims=True))
            top_sources.append(lax.dynamic_slice_in_dim(level_points[height], source, 1, 1))
            top_targets.append(lax.dynamic_slice_in_dim(level_points[height], node, 1, 1))
    kernel_block = kernel_matrix(
        jnp.concatenate(top_sources, axis=1), jnp.concatenate(top_targets, axis=1), kernel_scale
    )
    contributions = jnp.einsum(
        "nqr,nrs->qns", jnp.concatenate(top_moments, axis=0), kernel_block, precision=TAIL_PRECISION
    )
    top_couplings = []
    first = 0
    for slots in top_slots:
        top_couplings.append(contributions[:, first : first + slots, :].sum(axis=1, keepdims=True))
        first += slots
    descent = top_couplings[-1]
    for height in range(top_levels - 2, -1, -1):
        descent = (
            jnp.einsum("qns,nrs->qnr", descent, own_edges[height], precision=TAIL_PRECISION)
            + top_couplings[height]
        )
    for height in range(local_depth - 1, -1, -1):
        descent = jnp.einsum(
            "qns,nrs->qnr", jnp.repeat(descent, 2, axis=1), transfer_maps[height], precision=TAIL_PRECISION
        )
        descent = descent + local_couplings[height]
    far_field = jnp.einsum("qbr,bpr->qbp", descent, leaf_basis, precision=TAIL_PRECISION).reshape(
        rows_here, BOXES_DEV * P_SIZE
    )
    return near_field + far_field + NUGGET * probes


def solution(mesh):
    in_specs = (
        P("probe", "boxes"),
        P(None, "boxes"),
        P("boxes", None),
        P(None, "boxes"),
        P(None, "boxes"),
        P(),
        P("boxes", None),
    )
    out_specs = P("probe", "boxes")
    return jax.shard_map(body, mesh=mesh, in_specs=in_specs, out_specs=out_specs, check_vma=False)
```
